32 devices in a mesh: rows: 4 (over y, x), cols: 8 (over z, core).
Axes of the slice: x: 2, y: 2, z: 4, core: 2. Of those that a mesh axis runs over, the one named last changes fastest.
Arguments:
- tokens: bfloat16 [1024, 2048], P('rows', 'cols'), may hold values from -6 to 6
- segments: int32 [4, 256], P('rows'), may hold values from 0 to 3, never falling along the last dimension, each value on 1 to 128 neighbouring positions
- w_query: bfloat16 [2048, 2048], P('rows', 'cols'), may hold values from -0.125 to 0.125
- w_key: bfloat16 [2048, 2048], P('rows', 'cols'), may hold values from -0.125 to 0.125
- w_value: bfloat16 [2048, 2048], P('rows', 'cols'), may hold values from -0.125 to 0.125
- w_out: bfloat16 [2048, 2048], P('cols', 'rows'), may hold values from -0.75 to 0.75
- w_gate: bfloat16 [2048, 8192], P('rows', 'cols'), may hold values from -0.125 to 0.125
- w_up: bfloat16 [2048, 8192], P('rows', 'cols'), may hold values from -0.125 to 0.125
- w_down: bfloat16 [8192, 2048], P('cols', 'rows'), may hold values from -0.0625 to 0.0625
- cotangent: bfloat16 [1024, 2048], P('rows', 'cols'), may hold values from -6 to 6
Outputs:
- layer_out: bfloat16 [1024, 2048], P('rows', 'cols')
- grad_input: float32 [1024, 2048], P('rows', 'cols')
- grad_query: float32 [2048, 2048], P('rows', 'cols')
- grad_key: float32 [2048, 2048], P('rows', 'cols')
- grad_value: float32 [2048, 2048], P('rows', 'cols')
- grad_out: float32 [2048, 2048], P('cols', 'rows')
- grad_gate: float32 [2048, 8192], P('rows', 'cols')
- grad_up: float32 [2048, 8192], P('rows', 'cols')
- grad_down: float32 [8192, 2048], P('cols', 'rows')
The draws below stay inside these ranges and needn't reach their ends.
Inputs may be any that keep to these rules, and one draw needn't show every extreme that they name: `segments`: segment numbers never fall along a sequence and start at 0; each document holds 1 to 128 tokens, and in each sequence one holds exactly 128.
All inputs are finite; a program needn't handle non-finite values.
Results may differ from the reference program's by a relative error of at most 0.017.
Values may be sent and summed in bfloat16 or wider, within the bound.
A program may use at most 128 MiB of HBM per device.

```python
import math
import jax
import jax.numpy as jnp
import numpy as np
from jax import lax

D = 2048
HEADS = 16
HD = 128
FF = 8192
LEN = 256
SEQS = 4
TOKENS = 1024


def block_scale(stream_key, shape, cuts, least, largest):
    def one(position, shards_of):
        draws = jax.random.uniform(jax.random.fold_in(jax.random.fold_in(stream_key, 6), position), (shards_of,), jnp.float32, least / len(cuts), largest / len(cuts))
        return jnp.repeat(jnp.exp(draws), shape[position] // shards_of).reshape((-1,) + (1,) * (len(shape) - position - 1))

    level = one(*cuts[0])
    for cut in cuts[1:]:
        level = level * one(*cut)
    return level


def length_profile(amount, total, reach, slope):
    loads = [(1 << 20) // math.isqrt(rank ** slope) + 1 for rank in range(2, amount + 1)]
    rest, holding = total - reach - (amount - 1), [1] * (amount - 1)
    while rest > 0:
        free = [i for i in range(amount - 1) if holding[i] < reach]
        pool, budget = sum([loads[i] for i in free]), rest
        for i in free:
            extra = min(reach - holding[i], max(1, budget * loads[i] // pool), rest)
            holding[i] = holding[i] + extra
            rest = rest - extra
    return np.array([reach] + holding)


def ragged(stream_key, number_of, total, most, lean):
    if number_of == 2:
        one = jax.random.randint(stream_key, (), max(1, total - most), min(most, total - 1) + 1)
        return jnp.stack([one, total - one])
    sizes = jnp.asarray(length_profile(number_of, total, most, lean), jnp.int32)
    pairs = (number_of - 1) // 2
    source_of, taker = sizes[1:1 + 2 * pairs:2], sizes[2:2 + 2 * pairs:2]
    slack = jnp.minimum(source_of - 1, most - taker)
    shifted = jax.random.randint(jax.random.fold_in(stream_key, 1), (pairs,), 0, 1 << 20) % (slack + 1)
    sizes = sizes.at[1:1 + 2 * pairs:2].set(source_of - shifted).at[2:2 + 2 * pairs:2].set(taker + shifted)
    return sizes[jax.random.permutation(jax.random.fold_in(stream_key, 2), number_of)]


def noise(stream_key, shape, spread, most, split=(), kind=jnp.bfloat16):
    values = jax.random.normal(stream_key, shape, jnp.float32) * spread
    if len(split) > 0:
        values = block_scale(stream_key, shape, split, -0.22, 0.18) * values
    return jnp.clip(values, min=-most, max=most).astype(kind)


def setup_inputs(seed: int = 0) -> dict:
    splits = jax.random.split(jax.random.key(seed), 11)
    tokens = noise(splits[0], (TOKENS, D), 1.0, 6.0, ((0, 4), (1, 8)))
    segments = jax.vmap(lambda own: jnp.searchsorted(jnp.cumsum(ragged(own, max(LEN // 64, 4), LEN, LEN // 2, 2)), jnp.arange(LEN), side="right"))(jax.random.split(splits[1], SEQS)).reshape((SEQS, LEN)).astype(jnp.int32)
    w_query = noise(splits[2], (D, D), D ** -0.5, 0.125, ((0, 4), (1, 8)))
    w_key = noise(splits[3], (D, D), D ** -0.5, 0.125, ((0, 4), (1, 8)))
    w_value = noise(splits[4], (D, D), D ** -0.5, 0.125, ((0, 4), (1, 8)))
    w_out = noise(splits[5], (D, D), (D // 32) ** -0.5, 0.75, ((0, 8), (1, 4)))
    w_gate = noise(splits[6], (D, FF), D ** -0.5, 0.125, ((0, 4), (1, 8)))
    w_up = noise(splits[7], (D, FF), D ** -0.5, 0.125, ((0, 4), (1, 8)))
    w_down = noise(splits[8], (FF, D), FF ** -0.5, 0.0625, ((0, 8), (1, 4)))
    cotangent = noise(splits[9], (TOKENS, D), 1.0, 6.0, ((0, 4), (1, 8)))
    return dict(tokens=tokens, segments=segments, w_query=w_query, w_key=w_key, w_value=w_value, w_out=w_out, w_gate=w_gate, w_up=w_up, w_down=w_down, cotangent=cotangent)


EPS = 1e-05
NEG = -1e+30
BASE = 10000.0

@jax.custom_vjp
def low(v):
    return lax.optimization_barrier(v.astype(jnp.bfloat16)).astype(jnp.float32)

@jax.custom_vjp
def low_back(v):
    return v

def low_keep(v):
    return (low(v), None)

def low_pass(kept, grad):
    return (grad,)

def back_keep(v):
    return (v, None)

def back_low(kept, grad):
    return (low(grad),)
low.defvjp(low_keep, low_pass)
low_back.defvjp(back_keep, back_low)

def doc_positions(seg):
    count = seg.shape[0]
    index = jnp.arange(count, dtype=jnp.int32)
    first = jnp.concatenate([jnp.ones((1,), dtype=bool), seg[1:] != seg[:-1]])
    start = lax.cummax(jnp.where(first, index, 0).astype(jnp.int32), axis=0)
    return index - start

def rope_tables(pos):
    half = HD // 2
    freq = BASE ** (-(jnp.arange(half, dtype=jnp.float32) * 2.0) / HD)
    angle = pos.astype(jnp.float32)[:, None] * freq[None, :]
    cosine = jnp.cos(angle)
    sine = jnp.sin(angle)
    return (jnp.concatenate([cosine, cosine], 1)[:, None, :], jnp.concatenate([-sine, sine], 1)[:, None, :])

def swap_halves(v):
    half = HD // 2
    return jnp.concatenate([v[..., half:], v[..., :half]], -1)

def rotate(v, cos_full, sin_full):
    return v * cos_full + swap_halves(v) * sin_full

def norm(v):
    mean = lax.optimization_barrier(jnp.mean(v, -1, keepdims=True))
    var = lax.optimization_barrier(jnp.mean(v * v, -1, keepdims=True)) - mean * mean
    return (v - mean) * lax.rsqrt(var + EPS)

def matmul(a, b):
    return jnp.dot(a, b, precision=lax.Precision.HIGHEST)

def layer(xf, seg, wq, wk, wv, wo, wg, wu, wd):
    length = xf.shape[0]
    pos = doc_positions(seg)
    cos_full, sin_full = rope_tables(pos)
    index = jnp.arange(length, dtype=jnp.int32)
    allowed = (seg[:, None] == seg[None, :]) & (index[:, None] >= index[None, :])
    scale = HD ** (-0.5)
    h1 = low(norm(xf))
    query = low(rotate(low_back(matmul(h1, wq)).reshape(length, HEADS, HD), cos_full, sin_full))
    key = low(rotate(low_back(matmul(h1, wk)).reshape(length, HEADS, HD), cos_full, sin_full))
    value = low(low_back(matmul(h1, wv))).reshape(length, HEADS, HD)

    def one_head(item):
        qh, kh, vh = item
        score = low_back(matmul(qh, kh.T) * scale)
        score = jnp.where(allowed, score, NEG)
        prob = low(jax.nn.softmax(score, axis=-1))
        return matmul(prob, vh)
    mixed = lax.map(jax.checkpoint(one_head), (query.transpose(1, 0, 2), key.transpose(1, 0, 2), value.transpose(1, 0, 2)))
    attn = low(low_back(mixed.transpose(1, 0, 2).reshape(length, D)))
    x1 = xf + low_back(matmul(attn, wo))
    h2 = low(norm(x1))
    gate = low_back(matmul(h2, wg))
    up = low_back(matmul(h2, wu))
    hid = low(jax.nn.silu(gate) * up)
    return x1 + low_back(matmul(hid, wd))

def reference(tokens, segments, w_query, w_key, w_value, w_out, w_gate, w_up, w_down, cotangent):
    weights = (w_query.astype(jnp.float32), w_key.astype(jnp.float32), w_value.astype(jnp.float32), w_out.astype(jnp.float32), w_gate.astype(jnp.float32), w_up.astype(jnp.float32), w_down.astype(jnp.float32))
    inputs = tokens.astype(jnp.float32).reshape(SEQS, LEN, D)
    grads_seq = cotangent.astype(jnp.float32).reshape(SEQS, LEN, D)

    def step(totals, item):
        xs, seg, gs = item

        def forward(xv, wq, wk, wv, wo, wg, wu, wd):
            return layer(xv, seg, wq, wk, wv, wo, wg, wu, wd)
        result, pull = jax.vjp(forward, xs, *weights)
        grads = pull(gs)
        totals = tuple((a + b for a, b in zip(totals, grads[1:])))
        return (totals, (result.astype(jnp.bfloat16), grads[0]))
    zeros = tuple((jnp.zeros_like(w) for w in weights))
    totals, (results, grad_inputs) = lax.scan(step, zeros, (inputs, segments, grads_seq))
    return (results.reshape(TOKENS, D), grad_inputs.reshape(TOKENS, D), totals[0], totals[1], totals[2], totals[3], totals[4], totals[5], totals[6])
```

```python
import functools
import jax
import jax.numpy as jnp
import numpy as np
from jax import lax
from jax.experimental import pallas as pl
from jax.experimental.pallas import tpu as pltpu
from jax.sharding import PartitionSpec as P

HD = 128
EPS = 1e-05
NEG = -1e30
BASE = 10000.0
F32 = jnp.float32
BF = jnp.bfloat16
MESH = pl.DeviceIdType.MESH


def nn(a, b):
    return jnp.dot(a, b, preferred_element_type=F32)


def nt(a, b):
    return lax.dot_general(a, b, (((1,), (1,)), ((), ())), preferred_element_type=F32)


def tn(a, b):
    return lax.dot_general(a, b, (((0,), (0,)), ((), ())), preferred_element_type=F32)


def at(start, size, step=None):
    return pl.ds(pl.multiple_of(start, step or size), size)


class Net:
    def __init__(self, send, recv):
        self.send, self.recv, self.all = send, recv, []

    def __call__(self, src, dst, **peer):
        i = len(self.all)
        c = pltpu.make_async_remote_copy(
            src_ref=src, dst_ref=dst, send_sem=self.send.at[i], recv_sem=self.recv.at[i],
            device_id=peer, device_id_type=MESH)
        c.start()
        self.all.append(c)
        return c

    def drain(self):
        for c in self.all:
            c.wait_send()


class Local:
    def __init__(self, sem):
        self.sem, self.n = sem, 0

    def __call__(self, src, dst):
        c = pltpu.make_async_copy(src, dst, self.sem.at[self.n])
        self.n += 1
        c.start()
        return c


def step_kernel(g, *refs):
    (tok, cot, segr, segc, freq, wq, wk, wv, wo, wg, wu, wd,
     o_out, gi_out, h1w_out, gw_out, h2w_out, dg_out, du_out, hd_out, dqkv_out, go_out,
     xb, h1, xtl, gtl, h1w, gw, h2w, h2t, wqf, wkf, wvf, wof, wgv, wuv, wdv,
     p1, p1a, p1s, p1r, p2, p2a, p2s, p2r, p3, p3a, p3s, p3r, p4, p4a, p4s, p4r,
     x1, n2, dhs, dhr, dho, gus, gur, guo, hda, dga, dua, dh2s, dh2t, dxt, dmt, dmix,
     qb, kb, vb, att, lse, cosb, sinb, mskb, dqkv, gop, gor, fs, ft, lot, git, lob, gib,
     send, recv, loc) = refs
    R, C, L, TL, D, DR, DC, HC, H = (g[k] for k in ("R", "C", "L", "TL", "D", "DR", "DC", "HC", "H"))
    Z = C // 2
    r = lax.axis_index("rows")
    c = lax.axis_index("cols")
    z = c // 2
    core = c % 2
    net = Net(send, recv)
    local = Local(loc)
    scale = HD ** (-0.5)
    my_tl = at(c * TL, TL)

    bar = pltpu.get_barrier_semaphore()
    for k in range(1, R):
        pl.semaphore_signal(bar, inc=1, device_id={"rows": r ^ k}, device_id_type=MESH)
    for k in range(1, C):
        pl.semaphore_signal(bar, inc=1, device_id={"cols": c ^ k}, device_id_type=MESH)

    lx = local(tok, xb.at[:, at(c * DC, DC)])
    lg = local(cot.at[my_tl, :], gtl.at[:, at(c * DC, DC)])
    lws = [local(wq, wqf.at[at(r * DR, DR), :]), local(wk, wkf.at[at(r * DR, DR), :]),
           local(wv, wvf.at[at(r * DR, DR), :]), local(wo, wof.at[:, at(r * DR, DR)])]
    lff = [local(wd, wdv), local(wg, wgv), local(wu, wuv)]

    pl.semaphore_wait(bar, R + C - 2)

    def rows_gather(src, dst):
        return [net(src, dst, rows=r ^ k) for k in range(1, R)]

    def cols_start(blk):
        zs = [net(blk(c), blk(c), cols=c ^ (2 * m)) for m in range(1, Z)]
        return zs, net(blk(c), blk(c), cols=c ^ 1)

    def cols_forward(blk, zs):
        fw = []
        for m in range(1, Z):
            zs[m - 1].wait_recv()
            fw.append(net(blk(c ^ (2 * m)), blk(c ^ (2 * m)), cols=c ^ 1))
        return fw

    def cols_finish(own, fw):
        own.wait_recv()
        for f in fw:
            f.wait_recv()

    def xblk(j):
        return xb.at[:, at(j * DC, DC)]

    xz = [net(tok, xblk(c), cols=c ^ (2 * m)) for m in range(1, Z)]
    xp = net(tok, xblk(c), cols=c ^ 1)
    ga = [net(cot.at[at((c ^ k) * TL, TL), :], gtl.at[:, at(c * DC, DC)], cols=c ^ k) for k in range(1, C)]
    cq = rows_gather(wq, wqf.at[at(r * DR, DR), :])
    ck = rows_gather(wk, wkf.at[at(r * DR, DR), :])

    sr = jnp.broadcast_to(segr[...], (L, L))
    sc = jnp.broadcast_to(segc[...][:, :1], (L, L))
    qi = lax.broadcasted_iota(jnp.int32, (L, L), 0)
    ki = lax.broadcasted_iota(jnp.int32, (L, L), 1)
    ok = (sr == sc) & (qi >= ki)
    okf = jnp.where(ok, 1.0, 0.0)
    mskb[...] = jnp.where(ok, 0.0, NEG)
    pos = jnp.sum(okf, 1, keepdims=True) - 1.0
    angle = pos * freq[...]
    lane = lax.broadcasted_iota(jnp.int32, (L, HD), 1)
    cosb[...] = jnp.cos(angle)
    sn = jnp.sin(angle)
    sinb[...] = jnp.where(lane < HD // 2, -sn, sn)

    lx.wait()
    xf = cols_forward(xblk, xz)
    cols_finish(xp, xf)

    def stats(v):
        mean = jnp.sum(v, 1, keepdims=True) / D
        sq = jnp.sum(v * v, 1, keepdims=True) / D
        return mean, lax.rsqrt(sq - mean * mean + EPS)

    def norm_rows(i, _):
        rows = at(i * 32, 32)
        v = xb[rows, :].astype(F32)
        mean, rstd = stats(v)
        h1[rows, :] = ((v - mean) * rstd).astype(BF)
        return 0

    lax.fori_loop(0, L // 32, norm_rows, 0)

    lg.wait()
    for k in ga:
        k.wait_recv()

    def to_ws(src, dst):
        cps = [net(src.at[:, at((r ^ k) * DR, DR)], dst.at[r, my_tl, :], rows=r ^ k) for k in range(1, R)]
        return cps, local(src.at[:, at(r * DR, DR)], dst.at[r, my_tl, :])

    def landed(cl):
        for k in cl[0]:
            k.wait_recv()
        cl[1].wait()

    a_g = to_ws(gtl, gw)
    a_h = to_ws(h1.at[my_tl, :], h1w)
    cv = rows_gather(wv, wvf.at[at(r * DR, DR), :])
    co = rows_gather(wo, wof.at[:, at(r * DR, DR)])

    def wsblk(buf):
        return lambda j: buf.at[:, at(j * TL, TL), :]

    heads = HC // HD

    def rope(v):
        return jnp.concatenate(
            [v[:, h * HD:(h + 1) * HD] * cosb[...]
             + pltpu.roll(v[:, h * HD:(h + 1) * HD], HD // 2, 1) * sinb[...] for h in range(heads)], 1)

    def unrope(v):
        return v * cosb[...] + pltpu.roll(v * sinb[...], HD // 2, 1)

    lws[0].wait()
    for k in cq:
        k.wait_recv()
    qb[...] = rope(nn(h1[...], wqf[...])).astype(BF)
    landed(a_g)
    g_z, g_p = cols_start(wsblk(gw))
    landed(a_h)
    h_z, h_p = cols_start(wsblk(h1w))
    lws[1].wait()
    for k in ck:
        k.wait_recv()
    kb[...] = rope(nn(h1[...], wkf[...])).astype(BF)
    lws[2].wait()
    for k in cv:
        k.wait_recv()
    vb[...] = nn(h1[...], wvf[...]).astype(BF)

    for h in range(heads):
        hs = slice(h * HD, (h + 1) * HD)
        s = nt(qb[:, hs], kb[:, hs]) * scale
        s = jnp.where(mskb[...] < 0.0, NEG, s)
        top = jnp.max(s, 1, keepdims=True)
        e = jnp.exp(s - top)
        tot = jnp.sum(e, 1, keepdims=True)
        lse[:, hs] = jnp.broadcast_to(top + jnp.log(tot), (L, HD))
        att[:, hs] = nn((e / tot).astype(BF), vb[:, hs]).astype(BF)

    def parts_store(dst, val, i=None):
        for j in range(C):
            v = val[j * TL:(j + 1) * TL, :].astype(BF)
            if i is None:
                dst[j % 2, j // 2, :, :] = v
            else:
                dst[j % 2, j // 2, i, :, :] = v

    lws[3].wait()
    for k in co:
        k.wait_recv()
    W1 = min(512, D)
    for n in range(D // W1):
        ns = slice(n * W1, (n + 1) * W1)
        val = nn(att[...], wof[:, ns])
        for j in range(C):
            p1[j % 2, j // 2, :, ns] = val[j * TL:(j + 1) * TL, :].astype(BF)

    def pre(p, pa):
        return net(p.at[1 - core], pa, cols=c ^ 1)

    def zsend(p, pa, ps, pr):
        out = []
        for m in range(1, Z):
            ps[m] = (p[core, z ^ m].astype(F32) + pa[z ^ m].astype(F32)).astype(BF)
            out.append(net(ps.at[m], pr.at[m], cols=c ^ (2 * m)))
        return out

    def zsum(p, pa, pr, cps):
        tot = p[core, z].astype(F32) + pa[z].astype(F32)
        for m in range(1, Z):
            cps[m - 1].wait_recv()
            tot = tot + pr[m].astype(F32)
        return tot

    k1 = pre(p1, p1a)
    g_f = cols_forward(wsblk(gw), g_z)
    k1.wait_recv()
    z1 = zsend(p1, p1a, p1s, p1r)
    h_f = cols_forward(wsblk(h1w), h_z)
    cols_finish(g_p, g_f)
    cols_finish(h_p, h_f)
    lout = [local(gw, gw_out), local(h1w, h1w_out)]

    lff[0].wait()

    def dhid_block(s, put):
        def one(n, _):
            ns = at(n * 256, 256)
            put(ns, nt(gw[s], wdv[ns, :]))
            return 0
        lax.fori_loop(0, wdv.shape[0] // 256, one, 0)

    order = list(range(1, R))
    dh = {}
    for k in order:
        def put(ns, v, k=k):
            dhs[k, :, ns] = v.astype(BF)
        dhid_block(r ^ k, put)
        if k < R - 1:
            dh[k] = net(dhs.at[k], dhr.at[k], rows=r ^ k)

    def put0(ns, v):
        dho[:, ns] = v
    dhid_block(r, put0)

    xv = xb[my_tl, :].astype(F32)
    xm, xr_ = stats(xv)
    xtl[...] = (xv - xm) * xr_
    v = xv + zsum(p1, p1a, p1r, z1)
    x1[...] = v
    mean2, rstd2 = stats(v)
    n2v = (v - mean2) * rstd2
    n2[...] = n2v
    h2t[...] = n2v.astype(BF)
    a_2 = to_ws(h2t, h2w)
    dh[R - 1] = net(dhs.at[R - 1], dhr.at[R - 1], rows=r ^ (R - 1))
    landed(a_2)
    h2_z, h2_p = cols_start(wsblk(h2w))
    lff[1].wait()
    lff[2].wait()
    h2_f = cols_forward(wsblk(h2w), h2_z)
    cols_finish(h2_p, h2_f)
    lout.append(local(h2w, h2w_out))

    FC = wgv.shape[1]
    QN = g["QN"]
    QW = FC // QN
    gu = {}
    for q in range(QN):
        qs = slice(q * QW, (q + 1) * QW)
        for k in order + [0]:
            ga_ = nn(h2w[r ^ k], wgv[:, qs])
            up_ = nn(h2w[r ^ k], wuv[:, qs])
            if k:
                gus[k, q, 0] = ga_.astype(BF)
                gus[k, q, 1] = up_.astype(BF)
                gu[k, q] = net(gus.at[k, q], gur.at[k, q], rows=r ^ k)
            else:
                guo[q, 0] = ga_
                guo[q, 1] = up_

    for k in order:
        dh[k].wait_recv()
    dgu, hdc = {}, {}
    for q in range(QN):
        for k in order:
            gu[k, q].wait_recv()

        def act(i, _, q=q):
            rows = at(i * 32, 32)
            gate, up = guo[q, 0, rows, :], guo[q, 1, rows, :]
            dhid = dho[rows, q * QW:(q + 1) * QW]
            for k in order:
                gate = gate + gur[k, q, 0, rows, :].astype(F32)
                up = up + gur[k, q, 1, rows, :].astype(F32)
                dhid = dhid + dhr[k, rows, q * QW:(q + 1) * QW].astype(F32)
            sig = 1.0 / (1.0 + jnp.exp(-gate))
            silu = gate * sig
            hda[q, r, rows, :] = (silu * up).astype(BF)
            dga[q, r, rows, :] = (dhid * up * sig * (1.0 + gate * (1.0 - sig))).astype(BF)
            dua[q, r, rows, :] = (dhid * silu).astype(BF)
            return 0
        lax.fori_loop(0, L // 32, act, 0)
        for k in order:
            dgu[k, q, 0] = net(dga.at[q, r], dga.at[q, r], rows=r ^ k)
            dgu[k, q, 1] = net(dua.at[q, r], dua.at[q, r], rows=r ^ k)
    for k in order[:-1]:
        for q in range(QN):
            hdc[k, q] = net(hda.at[q, r], hda.at[q, r], rows=r ^ k)

    k2 = {}

    def dh2_block(k):
        s = r ^ k
        tot = None
        for q in range(QN):
            qs = slice(q * QW, (q + 1) * QW)
            t = nt(dga[q, s], wgv[:, qs]) + nt(dua[q, s], wuv[:, qs])
            tot = t if tot is None else tot + t
        for j in range(C):
            p2[j % 2, k, j // 2] = tot[j * TL:(j + 1) * TL, :].astype(BF)
        k2[k] = net(p2.at[1 - core, k], p2a.at[k], cols=c ^ 1)

    dh2_block(0)
    z2 = {}

    def z2_send(k):
        k2[k].wait_recv()
        for m in range(1, Z):
            p2s[k, m] = (p2[core, k, z ^ m].astype(F32) + p2a[k, z ^ m].astype(F32)).astype(BF)
            z2[k, m] = net(p2s.at[k, m], p2r.at[k, m], cols=c ^ (2 * m))

    for n, k in enumerate(order):
        for q in range(QN):
            dgu[k, q, 0].wait_recv()
            dgu[k, q, 1].wait_recv()
        dh2_block(k)
        z2_send(n)
    z2_send(R - 1)
    lout += [local(dga, dg_out), local(dua, du_out)]

    a_d = []
    for k in range(R):
        tot = p2[core, k, z].astype(F32) + p2a[k, z].astype(F32)
        for m in range(1, Z):
            z2[k, m].wait_recv()
            tot = tot + p2r[k, m].astype(F32)
        dh2s[k] = tot
        if k:
            a_d.append(net(dh2s.at[k], dh2t.at[:, at(r * DR, DR)], rows=r ^ k))
        else:
            l_d = local(dh2s.at[0], dh2t.at[:, at(r * DR, DR)])
    for q in range(QN):
        k = order[-1]
        hdc[k, q] = net(hda.at[q, r], hda.at[q, r], rows=r ^ k)
    l_d.wait()
    for k in a_d:
        k.wait_recv()

    def norm_back(grad, normed, rstd):
        a = jnp.sum(grad, 1, keepdims=True) / D
        b = jnp.sum(grad * normed, 1, keepdims=True) / D
        return rstd * (grad - a - normed * b)

    _, rstd2b = stats(x1[...])
    dxv = gtl[...].astype(F32) + norm_back(dh2t[...], n2[...], rstd2b)
    dxt[...] = dxv
    dmt[...] = dxv.astype(BF)
    l_m = local(dmt, dmix.at[my_tl, :])

    def dblk(j):
        return dmix.at[at(j * TL, TL), :]
    m_z = [net(dmt, dblk(c), cols=c ^ (2 * m)) for m in range(1, Z)]
    m_p = net(dmt, dblk(c), cols=c ^ 1)

    for k in order:
        for q in range(QN):
            if k != order[-1]:
                hdc[k, q].wait_recv()

    def ffn_block(k):
        s = r ^ k
        tot = None
        for q in range(QN):
            t = nn(hda[q, s], wdv[q * QW:(q + 1) * QW, :])
            tot = t if tot is None else tot + t
        for j in range(C):
            p3[j % 2, j // 2, k] = tot[j * TL:(j + 1) * TL, :].astype(BF)

    for k in range(R - 1):
        ffn_block(k)
    m_f = cols_forward(dblk, m_z)
    l_m.wait()
    cols_finish(m_p, m_f)

    da = nt(dmix[...], wof[...]).astype(BF)
    for h in range(heads):
        hs = slice(h * HD, (h + 1) * HD)
        s = nt(qb[:, hs], kb[:, hs]) * scale
        s = jnp.where(mskb[...] < 0.0, NEG, s)
        pr = jnp.exp(s - lse[:, h * HD:h * HD + 1])
        dp = nt(da[:, hs], vb[:, hs])
        inner = jnp.sum(pr * dp, 1, keepdims=True)
        ds = (pr * (dp - inner)).astype(BF)
        dqkv[0, r, :, hs] = unrope(nn(ds, kb[:, hs]) * scale).astype(BF)
        dqkv[1, r, :, hs] = unrope(tn(ds, qb[:, hs]) * scale).astype(BF)
        dqkv[2, r, :, hs] = tn(pr.astype(BF), da[:, hs]).astype(BF)
    cd = [net(dqkv.at[i, r], dqkv.at[i, r], rows=r ^ k) for k in order for i in range(3)]

    for n in range(D // W1):
        ns = slice(n * W1, (n + 1) * W1)
        val = (nt(dqkv[0, r], wqf[ns, :]) + nt(dqkv[1, r], wkf[ns, :]) + nt(dqkv[2, r], wvf[ns, :]))
        for j in range(C):
            p4[j % 2, j // 2, :, ns] = val[j * TL:(j + 1) * TL, :].astype(BF)
    k4 = pre(p4, p4a)
    for s in range(R):
        gop[s] = tn(att[...], dmix[:, s * DR:(s + 1) * DR]).astype(BF)
    cgo = [net(gop.at[r ^ k], gor.at[r], rows=r ^ k) for k in order]
    l_go = local(gop.at[r], gor.at[r])
    k4.wait_recv()
    z4 = zsend(p4, p4a, p4s, p4r)

    for q in range(QN):
        hdc[order[-1], q].wait_recv()
    ffn_block(R - 1)
    lout.append(local(hda, hd_out))
    k3 = pre(p3, p3a)
    k3.wait_recv()
    z3 = zsend(p3, p3a, p3s, p3r)

    _, rstd1 = stats(xb[my_tl, :].astype(F32))
    git[...] = dxt[...] + norm_back(zsum(p4, p4a, p4r, z4), xtl[...], rstd1)

    def to_io(src, dst):
        cps = [net(src.at[:, at((c ^ k) * DC, DC)], dst.at[my_tl, :], cols=c ^ k) for k in range(1, C)]
        return cps, local(src.at[:, at(c * DC, DC)], dst.at[my_tl, :])

    i_g = to_io(git, gib)
    fs[...] = zsum(p3, p3a, p3r, z3)
    a_f = [net(fs.at[k], ft.at[:, at(r * DR, DR)], rows=r ^ k) for k in order]
    l_f = local(fs.at[0], ft.at[:, at(r * DR, DR)])
    l_f.wait()
    for k in a_f:
        k.wait_recv()
    lot[...] = (x1[...] + ft[...]).astype(BF)
    i_o = to_io(lot, lob)
    landed(i_g)
    lout.append(local(gib, gi_out))
    for k in cd:
        k.wait_recv()
    lout.append(local(dqkv, dqkv_out))
    l_go.wait()
    for k in cgo:
        k.wait_recv()
    lout.append(local(gor, go_out))
    landed(i_o)
    lout.append(local(lob, o_out))
    net.drain()
    for k in lout:
        k.wait()


def body(R, C, tokens, segments, w_query, w_key, w_value, w_out, w_gate, w_up, w_down, cotangent):
    L, DC = tokens.shape
    DR, HC = w_query.shape
    D = DR * R
    FC = w_gate.shape[1]
    TL = L // C
    Z = C // 2
    QN = 4 if FC % 1024 == 0 else 2
    QW = FC // QN
    g = dict(R=R, C=C, L=L, TL=TL, D=D, DR=DR, DC=DC, HC=HC, H=FC, QN=QN)
    half = HD // 2
    fr = (BASE ** (-(np.arange(half, dtype=np.float32) * np.float32(2.0)) / np.float32(HD))).astype(np.float32)
    freq = jnp.asarray(np.concatenate([fr, fr])[None, :])
    segc = jnp.broadcast_to(segments.reshape(L, 1), (L, 128))
    S = jax.ShapeDtypeStruct
    V = pltpu.VMEM
    outs = [
        S((L, DC), BF), S((L, DC), F32), S((R, L, DR), BF), S((R, L, DR), BF), S((R, L, DR), BF),
        S((QN, R, L, QW), BF), S((QN, R, L, QW), BF), S((QN, R, L, QW), BF),
        S((3, R, L, HC), BF), S((R, HC, DR), BF),
    ]
    seq = lambda w: [V((2, Z, TL, w), BF), V((Z, TL, w), BF), V((Z, TL, w), BF), V((Z, TL, w), BF)]
    seq4 = lambda: [V((2, Z, R, TL, DR), BF), V((Z, R, TL, DR), BF), V((Z, R, TL, DR), BF), V((Z, R, TL, DR), BF)]
    seq2 = lambda: [V((2, R, Z, TL, DR), BF), V((R, Z, TL, DR), BF), V((R, Z, TL, DR), BF), V((R, Z, TL, DR), BF)]
    scratch = [
        V((L, D), BF), V((L, D), BF), V((TL, D), F32), V((TL, D), BF),
        V((R, L, DR), BF), V((R, L, DR), BF), V((R, L, DR), BF), V((TL, D), BF),
        V((D, HC), BF), V((D, HC), BF), V((D, HC), BF), V((HC, D), BF),
        V((DR, FC), BF), V((DR, FC), BF), V((FC, DR), BF),
        *seq(D), *seq2(), *seq4(), *seq(D),
        V((TL, D), F32), V((TL, D), F32),
        V((R, L, FC), BF), V((R, L, FC), BF), V((L, FC), F32),
        V((R, QN, 2, L, QW), BF), V((R, QN, 2, L, QW), BF), V((QN, 2, L, QW), F32),
        V((QN, R, L, QW), BF), V((QN, R, L, QW), BF), V((QN, R, L, QW), BF),
        V((R, TL, DR), F32), V((TL, D), F32), V((TL, D), F32), V((TL, D), BF), V((L, D), BF),
        V((L, HC), BF), V((L, HC), BF), V((L, HC), BF), V((L, HC), BF), V((L, HC), F32),
        V((L, HD), F32), V((L, HD), F32), V((L, L), F32),
        V((3, R, L, HC), BF), V((R, HC, DR), BF), V((R, HC, DR), BF),
        V((R, TL, DR), F32), V((TL, D), F32), V((TL, D), BF), V((TL, D), F32), V((L, DC), BF), V((L, DC), F32),
        pltpu.SemaphoreType.DMA((g_sems(R, C, QN),)), pltpu.SemaphoreType.DMA((g_sems(R, C, QN),)),
        pltpu.SemaphoreType.DMA((40,)),
    ]
    A = pl.BlockSpec(memory_space=pl.ANY)
    B = pl.BlockSpec(memory_space=pltpu.VMEM)
    res = pl.pallas_call(
        functools.partial(step_kernel, g),
        out_shape=outs,
        in_specs=[A, A, B, B, B] + [A] * 7,
        out_specs=[A] * len(outs),
        scratch_shapes=scratch,
        compiler_params=pltpu.CompilerParams(
            collective_id=0, has_side_effects=True, vmem_limit_bytes=67043328),
        name="layer_step",
    )(tokens, cotangent, segments, segc, freq, w_query, w_key, w_value, w_out, w_gate, w_up, w_down)
    layer_out, grad_in, h1w, gw, h2w, dg, du, hd, dqkv, go = res
    T = R * L
    h1w, gw, h2w = (t.reshape(T, DR) for t in (h1w, gw, h2w))
    gq, gk, gv = (tn(h1w, dqkv[i].reshape(T, HC)) for i in range(3))
    ggate = jnp.einsum("td,qth->dqh", h2w, dg.reshape(QN, T, QW), preferred_element_type=F32).reshape(DR, FC)
    gup = jnp.einsum("td,qth->dqh", h2w, du.reshape(QN, T, QW), preferred_element_type=F32).reshape(DR, FC)
    gdown = jnp.einsum("qth,td->qhd", hd.reshape(QN, T, QW), gw, preferred_element_type=F32).reshape(FC, DR)
    gout = jnp.sum(go.astype(F32), 0)
    return layer_out, grad_in, gq, gk, gv, gout, ggate, gup, gdown


def g_sems(R, C, QN):
    return 12 * (R - 1) + 8 * C + 8 * C + (R - 1) * (12 + 4 * QN) + R * C + 8 * C


def solution(mesh):
    R, C = mesh.shape["rows"], mesh.shape["cols"]
    rc, cr = P("rows", "cols"), P("cols", "rows")
    in_specs = (rc, P("rows", None), rc, rc, rc, cr, rc, rc, cr, rc)
    out_specs = (rc, rc, rc, rc, rc, cr, rc, rc, cr)
    return jax.shard_map(functools.partial(body, R, C), mesh=mesh, in_specs=in_specs,
                         out_specs=out_specs, check_vma=False)
```

```python
import functools
import jax
import jax.numpy as jnp
import numpy as np
from jax import lax
from jax.experimental import pallas as pl
from jax.experimental.pallas import tpu as pltpu
from jax.sharding import PartitionSpec as P

HD = 128
EPS = 1e-05
NEG = -1e30
BASE = 10000.0
F32 = jnp.float32
BF = jnp.bfloat16
MESH = pl.DeviceIdType.MESH


def nn(a, b):
    return jnp.dot(a, b, preferred_element_type=F32)


def nt(a, b):
    return lax.dot_general(a, b, (((1,), (1,)), ((), ())), preferred_element_type=F32)


def tn(a, b):
    return lax.dot_general(a, b, (((0,), (0,)), ((), ())), preferred_element_type=F32)


def at(start, size, step=None):
    return pl.ds(pl.multiple_of(start, step or size), size)


class Net:
    def __init__(self, send, recv):
        self.send, self.recv, self.all = send, recv, []

    def __call__(self, src, dst, **peer):
        i = len(self.all)
        c = pltpu.make_async_remote_copy(
            src_ref=src, dst_ref=dst, send_sem=self.send.at[i], recv_sem=self.recv.at[i],
            device_id=peer, device_id_type=MESH)
        c.start()
        self.all.append(Copy(c))
        return self.all[-1]

    def drain(self):
        for c in self.all:
            c.c.wait_send()


class Copy:
    def __init__(self, c):
        self.c, self.open = c, True

    def wait_recv(self):
        if self.open:
            self.c.wait_recv()
        self.open = False


class LCopy:
    def __init__(self, c):
        self.c, self.open = c, True

    def wait(self):
        if self.open:
            self.c.wait()
        self.open = False


class Local:
    def __init__(self, sem):
        self.sem, self.n, self.all = sem, 0, []

    def __call__(self, src, dst):
        c = pltpu.make_async_copy(src, dst, self.sem.at[self.n])
        self.n += 1
        c.start()
        self.all.append(LCopy(c))
        return self.all[-1]


def step_kernel(g, *refs):
    (tok, cot, segr, freq, wq, wk, wv, wo, wg, wu, wd,
     o_out, gi_out, h1w_out, gw_out, h2w_out, dg_out, du_out, hd_out, dqkv_out, go_out,
     xb, h1, xtl, gtl, h1w, gw, h2w, h2t, wqf, wkf, wvf, wof, wgv, wuv, wdv,
     p1, p1a, p1s, p1r, p2, p2a, p2s, p2r, p3, p3a, p3s, p3r, p4, p4a, p4s, p4r,
     x1, n2, dhs, dhr, dho, gus, gur, guo, hda, dga, dua, dh2s, dh2t, dxt, dmt, dmix,
     qb, kb, vb, att, lse, cosb, sinb, mskb, dqkv, gop, gor, gof, fs, ft, lot, git, lob, gib,
     send, recv, loc) = refs
    R, C, L, TL, D, DR, DC, HC, H = (g[k] for k in ("R", "C", "L", "TL", "D", "DR", "DC", "HC", "H"))
    Z = C // 2
    r = lax.axis_index("rows")
    c = lax.axis_index("cols")
    z = c // 2
    core = c % 2
    net = Net(send, recv)
    local = Local(loc)
    scale = HD ** (-0.5)
    my_tl = at(c * TL, TL)

    bar = pltpu.get_barrier_semaphore()
    for k in range(1, R):
        pl.semaphore_signal(bar, inc=1, device_id={"rows": r ^ k}, device_id_type=MESH)
    for k in range(1, C):
        pl.semaphore_signal(bar, inc=1, device_id={"cols": c ^ k}, device_id_type=MESH)

    lx = local(tok, xb.at[:, at(c * DC, DC)])
    lg = local(cot.at[my_tl, :], gtl.at[:, at(c * DC, DC)])
    lws = [local(wq, wqf.at[at(r * DR, DR), :]), local(wk, wkf.at[at(r * DR, DR), :]),
           local(wv, wvf.at[at(r * DR, DR), :]), local(wo, wof.at[:, at(r * DR, DR)])]
    lff = [local(wd, wdv), local(wg, wgv), local(wu, wuv)]

    pl.semaphore_wait(bar, R + C - 2)

    def rows_gather(src, dst):
        return [net(src, dst, rows=r ^ k) for k in range(1, R)]

    def cols_start(blk):
        zs = [net(blk(c), blk(c), cols=c ^ (2 * m)) for m in range(1, Z)]
        return zs, net(blk(c), blk(c), cols=c ^ 1)

    def cols_forward(blk, zs):
        fw = []
        for m in range(1, Z):
            zs[m - 1].wait_recv()
            fw.append(net(blk(c ^ (2 * m)), blk(c ^ (2 * m)), cols=c ^ 1))
        return fw

    def cols_finish(own, fw):
        own.wait_recv()
        for f in fw:
            f.wait_recv()

    def xblk(j):
        return xb.at[:, at(j * DC, DC)]

    xz = [net(tok, xblk(c), cols=c ^ (2 * m)) for m in range(1, Z)]
    xp = net(tok, xblk(c), cols=c ^ 1)
    ga = [net(cot.at[at((c ^ k) * TL, TL), :], gtl.at[:, at(c * DC, DC)], cols=c ^ k) for k in range(1, C)]
    cq = rows_gather(wq, wqf.at[at(r * DR, DR), :])
    ck = rows_gather(wk, wkf.at[at(r * DR, DR), :])

    sr = jnp.broadcast_to(segr[...].astype(F32), (L, L))
    sc = sr.T
    qi = lax.broadcasted_iota(jnp.int32, (L, L), 0)
    ki = lax.broadcasted_iota(jnp.int32, (L, L), 1)
    ok = (sr == sc) & (qi >= ki)
    okf = jnp.where(ok, 1.0, 0.0)
    mskb[...] = jnp.where(ok, 0.0, NEG)
    pos = jnp.sum(okf, 1, keepdims=True) - 1.0
    angle = pos * freq[...]
    lane = lax.broadcasted_iota(jnp.int32, (L, HD), 1)
    cosb[...] = jnp.cos(angle)
    sn = jnp.sin(angle)
    sinb[...] = jnp.where(lane < HD // 2, -sn, sn)

    lx.wait()
    xf = cols_forward(xblk, xz)
    cols_finish(xp, xf)

    def stats(v):
        mean = jnp.sum(v, 1, keepdims=True) / D
        sq = jnp.sum(v * v, 1, keepdims=True) / D
        return mean, lax.rsqrt(sq - mean * mean + EPS)

    def norm_rows(i, _):
        rows = at(i * 32, 32)
        v = xb[rows, :].astype(F32)
        mean, rstd = stats(v)
        h1[rows, :] = ((v - mean) * rstd).astype(BF)
        return 0

    lax.fori_loop(0, L // 32, norm_rows, 0)

    lg.wait()
    for k in ga:
        k.wait_recv()

    def to_ws(src, dst):
        cps = [net(src.at[:, at((r ^ k) * DR, DR)], dst.at[r, my_tl, :], rows=r ^ k) for k in range(1, R)]
        return cps, local(src.at[:, at(r * DR, DR)], dst.at[r, my_tl, :])

    def landed(cl):
        for k in cl[0]:
            k.wait_recv()
        cl[1].wait()

    a_g = to_ws(gtl, gw)
    a_h = to_ws(h1.at[my_tl, :], h1w)
    cv = rows_gather(wv, wvf.at[at(r * DR, DR), :])
    co = rows_gather(wo, wof.at[:, at(r * DR, DR)])

    def wsblk(buf):
        return lambda j: buf.at[:, at(j * TL, TL), :]

    heads = HC // HD

    def rope(v):
        return jnp.concatenate(
            [v[:, h * HD:(h + 1) * HD] * cosb[...]
             + pltpu.roll(v[:, h * HD:(h + 1) * HD], HD // 2, 1) * sinb[...] for h in range(heads)], 1)

    def unrope(v):
        return v * cosb[...] + pltpu.roll(v * sinb[...], HD // 2, 1)

    lws[0].wait()
    for k in cq:
        k.wait_recv()
    qb[...] = rope(nn(h1[...], wqf[...])).astype(BF)
    landed(a_g)
    g_z, g_p = cols_start(wsblk(gw))
    landed(a_h)
    h_z, h_p = cols_start(wsblk(h1w))
    lws[1].wait()
    for k in ck:
        k.wait_recv()
    kb[...] = rope(nn(h1[...], wkf[...])).astype(BF)
    lws[2].wait()
    for k in cv:
        k.wait_recv()
    vb[...] = nn(h1[...], wvf[...]).astype(BF)

    for h in range(heads):
        hs = slice(h * HD, (h + 1) * HD)
        s = nt(qb[:, hs], kb[:, hs]) * scale
        s = jnp.where(mskb[...] < 0.0, NEG, s)
        top = jnp.max(s, 1, keepdims=True)
        e = jnp.exp(s - top)
        tot = jnp.sum(e, 1, keepdims=True)
        lse[:, hs] = jnp.broadcast_to(top + jnp.log(tot), (L, HD))
        att[:, hs] = nn((e / tot).astype(BF), vb[:, hs]).astype(BF)

    def parts_store(dst, val, i=None):
        for j in range(C):
            v = val[j * TL:(j + 1) * TL, :].astype(BF)
            if i is None:
                dst[j % 2, j // 2, :, :] = v
            else:
                dst[j % 2, j // 2, i, :, :] = v

    lws[3].wait()
    for k in co:
        k.wait_recv()
    W1 = min(512, D)
    for n in range(D // W1):
        ns = slice(n * W1, (n + 1) * W1)
        val = nn(att[...], wof[:, ns])
        for j in range(C):
            p1[j % 2, j // 2, :, ns] = val[j * TL:(j + 1) * TL, :].astype(BF)

    def pre(p, pa):
        return net(p.at[1 - core], pa, cols=c ^ 1)

    def zsend(p, pa, ps, pr):
        out = []
        for m in range(1, Z):
            ps[m] = (p[core, z ^ m].astype(F32) + pa[z ^ m].astype(F32)).astype(BF)
            out.append(net(ps.at[m], pr.at[m], cols=c ^ (2 * m)))
        return out

    def zsum(p, pa, pr, cps):
        tot = p[core, z].astype(F32) + pa[z].astype(F32)
        for m in range(1, Z):
            cps[m - 1].wait_recv()
            tot = tot + pr[m].astype(F32)
        return tot

    k1 = pre(p1, p1a)
    g_f = cols_forward(wsblk(gw), g_z)
    k1.wait_recv()
    z1 = zsend(p1, p1a, p1s, p1r)
    h_f = cols_forward(wsblk(h1w), h_z)
    cols_finish(g_p, g_f)
    cols_finish(h_p, h_f)
    lout = [local(gw, gw_out), local(h1w, h1w_out)]

    lff[0].wait()

    def dhid_block(s, put):
        def one(n, _):
            ns = at(n * 256, 256)
            put(ns, nt(gw[s], wdv[ns, :]))
            return 0
        lax.fori_loop(0, wdv.shape[0] // 256, one, 0)

    order = list(range(1, R))
    dh = {}
    for k in order:
        def put(ns, v, k=k):
            dhs[k, :, ns] = v.astype(BF)
        dhid_block(r ^ k, put)
        if k < R - 1:
            dh[k] = net(dhs.at[k], dhr.at[k], rows=r ^ k)

    def put0(ns, v):
        dho[:, ns] = v
    dhid_block(r, put0)

    xv = xb[my_tl, :].astype(F32)
    xm, xr_ = stats(xv)
    xtl[...] = (xv - xm) * xr_
    v = xv + zsum(p1, p1a, p1r, z1)
    x1[...] = v
    mean2, rstd2 = stats(v)
    n2v = (v - mean2) * rstd2
    n2[...] = n2v
    h2t[...] = n2v.astype(BF)
    a_2 = to_ws(h2t, h2w)
    dh[R - 1] = net(dhs.at[R - 1], dhr.at[R - 1], rows=r ^ (R - 1))
    landed(a_2)
    h2_z, h2_p = cols_start(wsblk(h2w))
    lff[1].wait()
    lff[2].wait()
    h2_f = cols_forward(wsblk(h2w), h2_z)
    cols_finish(h2_p, h2_f)
    lout.append(local(h2w, h2w_out))

    FC = wgv.shape[1]
    QN = g["QN"]
    QW = FC // QN
    gu = {}
    for q in range(QN):
        qs = slice(q * QW, (q + 1) * QW)
        for k in order + [0]:
            ga_ = nn(h2w[r ^ k], wgv[:, qs])
            up_ = nn(h2w[r ^ k], wuv[:, qs])
            if k:
                gus[k, q, 0] = ga_.astype(BF)
                gus[k, q, 1] = up_.astype(BF)
                gu[k, q] = net(gus.at[k, q], gur.at[k, q], rows=r ^ k)
            else:
                guo[q, 0] = ga_
                guo[q, 1] = up_

    for k in order:
        dh[k].wait_recv()
    dgu, hdc = {}, {}
    for q in range(QN):
        for k in order:
            gu[k, q].wait_recv()

        qs = slice(q * QW, (q + 1) * QW)

        def act(i, _, q=q, qs=qs):
            rows = at(i * 32, 32)
            gate, up = guo[q, 0, rows, :], guo[q, 1, rows, :]
            dhid = dho[rows, q * QW:(q + 1) * QW]
            for k in order:
                gate = gate + gur[k, q, 0, rows, :].astype(F32)
                up = up + gur[k, q, 1, rows, :].astype(F32)
                dhid = dhid + dhr[k, rows, q * QW:(q + 1) * QW].astype(F32)
            sig = 1.0 / (1.0 + jnp.exp(-gate))
            silu = gate * sig
            hda[r, rows, qs] = (silu * up).astype(BF)
            dga[r, rows, qs] = (dhid * up * sig * (1.0 + gate * (1.0 - sig))).astype(BF)
            dua[r, rows, qs] = (dhid * silu).astype(BF)
            return 0
        lax.fori_loop(0, L // 32, act, 0)
        for k in order:
            dgu[k, q, 0] = net(dga.at[r, :, qs], dga.at[r, :, qs], rows=r ^ k)
            dgu[k, q, 1] = net(dua.at[r, :, qs], dua.at[r, :, qs], rows=r ^ k)
    for k in order[:-1]:
        hdc[k] = net(hda.at[r], hda.at[r], rows=r ^ k)

    k2 = {}

    def dh2_block(k):
        s = r ^ k
        tot = nt(dga[s], wgv[...]) + nt(dua[s], wuv[...])
        for j in range(C):
            p2[j % 2, k, j // 2] = tot[j * TL:(j + 1) * TL, :].astype(BF)
        k2[k] = net(p2.at[1 - core, k], p2a.at[k], cols=c ^ 1)

    dh2_block(0)
    z2 = {}

    def z2_send(k):
        k2[k].wait_recv()
        for m in range(1, Z):
            p2s[k, m] = (p2[core, k, z ^ m].astype(F32) + p2a[k, z ^ m].astype(F32)).astype(BF)
            z2[k, m] = net(p2s.at[k, m], p2r.at[k, m], cols=c ^ (2 * m))

    for n, k in enumerate(order):
        for q in range(QN):
            dgu[k, q, 0].wait_recv()
            dgu[k, q, 1].wait_recv()
        dh2_block(k)
        z2_send(n)
    z2_send(R - 1)
    lout += [local(dga, dg_out), local(dua, du_out)]

    a_d = []
    for k in range(R):
        tot = p2[core, k, z].astype(F32) + p2a[k, z].astype(F32)
        for m in range(1, Z):
            z2[k, m].wait_recv()
            tot = tot + p2r[k, m].astype(F32)
        dh2s[k] = tot
        if k:
            a_d.append(net(dh2s.at[k], dh2t.at[:, at(r * DR, DR)], rows=r ^ k))
        else:
            l_d = local(dh2s.at[0], dh2t.at[:, at(r * DR, DR)])
    k = order[-1]
    hdc[k] = net(hda.at[r], hda.at[r], rows=r ^ k)
    l_d.wait()
    for k in a_d:
        k.wait_recv()

    def norm_back(grad, normed, rstd):
        a = jnp.sum(grad, 1, keepdims=True) / D
        b = jnp.sum(grad * normed, 1, keepdims=True) / D
        return rstd * (grad - a - normed * b)

    _, rstd2b = stats(x1[...])
    dxv = gtl[...].astype(F32) + norm_back(dh2t[...], n2[...], rstd2b)
    dxt[...] = dxv
    dmt[...] = dxv.astype(BF)
    l_m = local(dmt, dmix.at[my_tl, :])

    def dblk(j):
        return dmix.at[at(j * TL, TL), :]
    m_z = [net(dmt, dblk(c), cols=c ^ (2 * m)) for m in range(1, Z)]
    m_p = net(dmt, dblk(c), cols=c ^ 1)

    for k in order[:-1]:
        hdc[k].wait_recv()

    def ffn_block(k):
        s = r ^ k
        tot = nn(hda[s], wdv[...])
        for j in range(C):
            p3[j % 2, j // 2, k] = tot[j * TL:(j + 1) * TL, :].astype(BF)

    for k in range(R - 1):
        ffn_block(k)
    m_f = cols_forward(dblk, m_z)
    l_m.wait()
    cols_finish(m_p, m_f)

    da = nt(dmix[...], wof[...]).astype(BF)
    for h in range(heads):
        hs = slice(h * HD, (h + 1) * HD)
        s = nt(qb[:, hs], kb[:, hs]) * scale
        s = jnp.where(mskb[...] < 0.0, NEG, s)
        pr = jnp.exp(s - lse[:, h * HD:h * HD + 1])
        dp = nt(da[:, hs], vb[:, hs])
        inner = jnp.sum(pr * dp, 1, keepdims=True)
        ds = (pr * (dp - inner)).astype(BF)
        dqkv[0, r, :, hs] = unrope(nn(ds, kb[:, hs]) * scale).astype(BF)
        dqkv[1, r, :, hs] = unrope(tn(ds, qb[:, hs]) * scale).astype(BF)
        dqkv[2, r, :, hs] = tn(pr.astype(BF), da[:, hs]).astype(BF)
    cd = [net(dqkv.at[i, r], dqkv.at[i, r], rows=r ^ k) for k in order for i in range(3)]

    for n in range(D // W1):
        ns = slice(n * W1, (n + 1) * W1)
        val = (nt(dqkv[0, r], wqf[ns, :]) + nt(dqkv[1, r], wkf[ns, :]) + nt(dqkv[2, r], wvf[ns, :]))
        for j in range(C):
            p4[j % 2, j // 2, :, ns] = val[j * TL:(j + 1) * TL, :].astype(BF)
    k4 = pre(p4, p4a)
    for s in range(R):
        gop[s] = tn(att[...], dmix[:, s * DR:(s + 1) * DR]).astype(BF)
    cgo = [net(gop.at[r ^ k], gor.at[k], rows=r ^ k) for k in order]
    k4.wait_recv()
    z4 = zsend(p4, p4a, p4s, p4r)

    hdc[order[-1]].wait_recv()
    ffn_block(R - 1)
    lout.append(local(hda, hd_out))
    k3 = pre(p3, p3a)
    k3.wait_recv()
    z3 = zsend(p3, p3a, p3s, p3r)

    _, rstd1 = stats(xb[my_tl, :].astype(F32))
    git[...] = dxt[...] + norm_back(zsum(p4, p4a, p4r, z4), xtl[...], rstd1)

    def to_io(src, dst):
        cps = [net(src.at[:, at((c ^ k) * DC, DC)], dst.at[my_tl, :], cols=c ^ k) for k in range(1, C)]
        return cps, local(src.at[:, at(c * DC, DC)], dst.at[my_tl, :])

    i_g = to_io(git, gib)
    fs[...] = zsum(p3, p3a, p3r, z3)
    a_f = [net(fs.at[k], ft.at[:, at(r * DR, DR)], rows=r ^ k) for k in order]
    l_f = local(fs.at[0], ft.at[:, at(r * DR, DR)])
    l_f.wait()
    for k in a_f:
        k.wait_recv()
    lot[...] = (x1[...] + ft[...]).astype(BF)
    i_o = to_io(lot, lob)
    landed(i_g)
    lout.append(local(gib, gi_out))
    for k in cd:
        k.wait_recv()
    lout.append(local(dqkv, dqkv_out))
    for k in cgo:
        k.wait_recv()
    gsum = gop[r].astype(F32)
    for k in order:
        gsum = gsum + gor[k].astype(F32)
    gof[...] = gsum
    lout.append(local(gof, go_out))
    landed(i_o)
    lout.append(local(lob, o_out))
    net.drain()
    for k in lout:
        k.wait()


def body(R, C, tokens, segments, w_query, w_key, w_value, w_out, w_gate, w_up, w_down, cotangent):
    L, DC = tokens.shape
    DR, HC = w_query.shape
    D = DR * R
    FC = w_gate.shape[1]
    TL = L // C
    Z = C // 2
    QN = 4 if FC % 1024 == 0 else 2
    QW = FC // QN
    g = dict(R=R, C=C, L=L, TL=TL, D=D, DR=DR, DC=DC, HC=HC, H=FC, QN=QN)
    half = HD // 2
    fr = (BASE ** (-(np.arange(half, dtype=np.float32) * np.float32(2.0)) / np.float32(HD))).astype(np.float32)
    freq = jnp.asarray(np.concatenate([fr, fr])[None, :])
    S = jax.ShapeDtypeStruct
    V = pltpu.VMEM
    outs = [
        S((L, DC), BF), S((L, DC), F32), S((R, L, DR), BF), S((R, L, DR), BF), S((R, L, DR), BF),
        S((R, L, FC), BF), S((R, L, FC), BF), S((R, L, FC), BF),
        S((3, R, L, HC), BF), S((HC, DR), F32),
    ]
    seq = lambda w: [V((2, Z, TL, w), BF), V((Z, TL, w), BF), V((Z, TL, w), BF), V((Z, TL, w), BF)]
    seq4 = lambda: [V((2, Z, R, TL, DR), BF), V((Z, R, TL, DR), BF), V((Z, R, TL, DR), BF), V((Z, R, TL, DR), BF)]
    seq2 = lambda: [V((2, R, Z, TL, DR), BF), V((R, Z, TL, DR), BF), V((R, Z, TL, DR), BF), V((R, Z, TL, DR), BF)]
    scratch = [
        V((L, D), BF), V((L, D), BF), V((TL, D), F32), V((TL, D), BF),
        V((R, L, DR), BF), V((R, L, DR), BF), V((R, L, DR), BF), V((TL, D), BF),
        V((D, HC), BF), V((D, HC), BF), V((D, HC), BF), V((HC, D), BF),
        V((DR, FC), BF), V((DR, FC), BF), V((FC, DR), BF),
        *seq(D), *seq2(), *seq4(), *seq(D),
        V((TL, D), F32), V((TL, D), F32),
        V((R, L, FC), BF), V((R, L, FC), BF), V((L, FC), F32),
        V((R, QN, 2, L, QW), BF), V((R, QN, 2, L, QW), BF), V((QN, 2, L, QW), F32),
        V((R, L, FC), BF), V((R, L, FC), BF), V((R, L, FC), BF),
        V((R, TL, DR), F32), V((TL, D), F32), V((TL, D), F32), V((TL, D), BF), V((L, D), BF),
        V((L, HC), BF), V((L, HC), BF), V((L, HC), BF), V((L, HC), BF), V((L, HC), F32),
        V((L, HD), F32), V((L, HD), F32), V((L, L), F32),
        V((3, R, L, HC), BF), V((R, HC, DR), BF), V((R, HC, DR), BF), V((HC, DR), F32),
        V((R, TL, DR), F32), V((TL, D), F32), V((TL, D), BF), V((TL, D), F32), V((L, DC), BF), V((L, DC), F32),
        pltpu.SemaphoreType.DMA((g_sems(R, C, QN),)), pltpu.SemaphoreType.DMA((g_sems(R, C, QN),)),
        pltpu.SemaphoreType.DMA((40,)),
    ]
    A = pl.BlockSpec(memory_space=pl.ANY)
    B = pl.BlockSpec(memory_space=pltpu.VMEM)
    res = pl.pallas_call(
        functools.partial(step_kernel, g),
        out_shape=outs,
        in_specs=[A, A, B, B] + [A] * 7,
        out_specs=[A] * len(outs),
        scratch_shapes=scratch,
        compiler_params=pltpu.CompilerParams(
            collective_id=0, has_side_effects=True, vmem_limit_bytes=67043328),
        name="layer_step",
    )(tokens, cotangent, segments, freq, w_query, w_key, w_value, w_out, w_gate, w_up, w_down)
    layer_out, grad_in, h1w, gw, h2w, dg, du, hd, dqkv, go = res
    T = R * L
    h1w, gw, h2w = (t.reshape(T, DR) for t in (h1w, gw, h2w))
    gq, gk, gv = (tn(h1w, dqkv[i].reshape(T, HC)) for i in range(3))
    ggate, gup, gdown = tn(h2w, dg.reshape(T, FC)), tn(h2w, du.reshape(T, FC)), tn(hd.reshape(T, FC), gw)
    return layer_out, grad_in, gq, gk, gv, go, ggate, gup, gdown


def g_sems(R, C, QN):
    return 12 * (R - 1) + 8 * C + 8 * C + (R - 1) * (12 + 4 * QN) + R * C + 8 * C


def solution(mesh):
    R, C = mesh.shape["rows"], mesh.shape["cols"]
    rc, cr = P("rows", "cols"), P("cols", "rows")
    in_specs = (rc, P("rows", None), rc, rc, rc, cr, rc, rc, cr, rc)
    out_specs = (rc, rc, rc, rc, rc, cr, rc, rc, cr)
    return jax.shard_map(functools.partial(body, R, C), mesh=mesh, in_specs=in_specs,
                         out_specs=out_specs, check_vma=False)
```

```python
import functools
import jax
import jax.numpy as jnp
import numpy as np
from jax import lax
from jax.experimental import pallas as pl
from jax.experimental.pallas import tpu as pltpu
from jax.sharding import PartitionSpec as P

HD = 128
EPS = 1e-05
NEG = -1e30
BASE = 10000.0
F32 = jnp.float32
BF = jnp.bfloat16
MESH = pl.DeviceIdType.MESH


def nn(a, b):
    return jnp.dot(a, b, preferred_element_type=F32)


def nt(a, b):
    return lax.dot_general(a, b, (((1,), (1,)), ((), ())), preferred_element_type=F32)


def tn(a, b):
    return lax.dot_general(a, b, (((0,), (0,)), ((), ())), preferred_element_type=F32)


def at(start, size, step=None):
    return pl.ds(pl.multiple_of(start, step or size), size)


class Net:
    def __init__(self, send, recv):
        self.send, self.recv, self.all = send, recv, []

    def __call__(self, src, dst, **peer):
        i = len(self.all)
        assert i < self.send.shape[0]
        c = pltpu.make_async_remote_copy(
            src_ref=src, dst_ref=dst, send_sem=self.send.at[i], recv_sem=self.recv.at[i],
            device_id=peer, device_id_type=MESH)
        c.start()
        self.all.append(Copy(c))
        return self.all[-1]

    def drain(self):
        for c in self.all:
            c.c.wait_send()


class Copy:
    def __init__(self, c):
        self.c, self.open = c, True

    def wait_recv(self):
        if self.open:
            self.c.wait_recv()
        self.open = False


class Gather:
    def __init__(self, net, R, r, own, blk):
        self.net, self.r, self.two, self.blk, self.c = net, r, R == 4, blk, {}
        todo = [(1, 0), (2, 1), (1, 1), (2, 0)] if self.two else [(k, h) for k in range(1, R) for h in range(2)]
        for k, h in todo:
            self.c[k, h] = net(own(h), blk(r, h), rows=r ^ k)

    def forward(self):
        if self.two:
            for k, h in ((1, 0), (2, 1)):
                self.c[k, h].wait_recv()
                b = self.blk(self.r ^ k, h)
                self.c[3, h] = self.net(b, b, rows=self.r ^ (3 - k))

    def wait(self, k):
        for h in range(2):
            self.c[k, h].wait_recv()


class Reduce:
    def __init__(self, net, R, r, snd, rcv):
        self.net, self.r, self.two, self.snd, self.rcv, self.c = net, r, R == 4, snd, rcv, {}
        self.ks = (1, 2) if self.two else tuple(range(1, R))
        if self.two:
            for k, h in ((1, 0), (2, 1)):
                self.c[3, h] = net(snd(3, h), rcv(3, h), rows=r ^ k)
            for k, h in ((1, 0), (2, 1)):
                self.c[k, h] = net(snd(k, h), rcv(k, h), rows=r ^ k)
        else:
            for k in self.ks:
                for h in range(2):
                    self.c[k, h] = net(snd(k, h), rcv(k, h), rows=r ^ k)

    def relay(self):
        if self.two:
            for k, h in ((2, 0), (1, 1)):
                self.c[3, h].wait_recv()
                a = self.snd(k, h)
                a[...] = (a[...].astype(F32) + self.rcv(3, h)[...].astype(F32)).astype(BF)
                self.c[k, h] = self.net(a, self.rcv(k, h), rows=self.r ^ k)

    def wait(self):
        for k in self.ks:
            for h in range(2):
                self.c[k, h].wait_recv()


class LCopy:
    def __init__(self, c):
        self.c, self.open = c, True

    def wait(self):
        if self.open:
            self.c.wait()
        self.open = False


class Local:
    def __init__(self, sem):
        self.sem, self.n, self.all = sem, 0, []

    def __call__(self, src, dst):
        c = pltpu.make_async_copy(src, dst, self.sem.at[self.n])
        self.n += 1
        c.start()
        self.all.append(LCopy(c))
        return self.all[-1]


def step_kernel(g, *refs):
    (tok, cot, segr, freq, wq, wk, wv, wo, wg, wu, wd,
     o_out, gi_out, h1w_out, gw_out, h2w_out, dg_out, du_out, hd_out, dqkv_out, go_out,
     xb, h1, xtl, gtl, h1w, gw, h2w, h2t, wqf, wkf, wvf, wof, wgv, wuv, wdv,
     p1, p1a, p1s, p1r, p2, p2a, p2s, p2r, p3, p3a, p3s, p3r, p4, p4a, p4s, p4r,
     x1, n2, dhs, dhr, dho, gus, gur, guo, hda, dgu, dh2s, dh2t, dxt, dmt, dmix,
     qb, kb, vb, att, lse, cosb, sinb, mskb, dqkv, gop, gor, gof, fs, ft, lot, git, lob, gib,
     send, recv, loc) = refs
    R, C, L, TL, D, DR, DC, HC, H = (g[k] for k in ("R", "C", "L", "TL", "D", "DR", "DC", "HC", "H"))
    Z = C // 2
    r = lax.axis_index("rows")
    c = lax.axis_index("cols")
    z = c // 2
    core = c % 2
    net = Net(send, recv)
    local = Local(loc)
    scale = HD ** (-0.5)
    my_tl = at(c * TL, TL)

    bar = pltpu.get_barrier_semaphore()
    for k in range(1, R):
        pl.semaphore_signal(bar, inc=1, device_id={"rows": r ^ k}, device_id_type=MESH)
    for k in range(1, C):
        pl.semaphore_signal(bar, inc=1, device_id={"cols": c ^ k}, device_id_type=MESH)

    lx = local(tok, xb.at[:, at(c * DC, DC)])
    lg = local(cot.at[my_tl, :], gtl.at[:, at(c * DC, DC)])
    lws = [local(wq, wqf.at[at(r * DR, DR), :]), local(wk, wkf.at[at(r * DR, DR), :]),
           local(wv, wvf.at[at(r * DR, DR), :]), local(wo, wof.at[:, at(r * DR, DR)])]
    lff = [local(wd, wdv), local(wg, wgv), local(wu, wuv)]

    pl.semaphore_wait(bar, R + C - 2)

    def half(n, h):
        return slice(h * (n // 2), (h + 1) * (n // 2))

    def w_in(w, full):
        n = DR // 2
        return Gather(net, R, r, lambda h: w.at[half(DR, h), :], lambda j, h: full.at[at(j * DR + h * n, n), :])

    def cols_start(blk):
        zs = [net(blk(c), blk(c), cols=c ^ (2 * m)) for m in range(1, Z)]
        return zs, net(blk(c), blk(c), cols=c ^ 1)

    def cols_forward(blk, zs):
        fw = []
        for m in range(1, Z):
            zs[m - 1].wait_recv()
            fw.append(net(blk(c ^ (2 * m)), blk(c ^ (2 * m)), cols=c ^ 1))
        return fw

    def cols_finish(own, fw):
        own.wait_recv()
        for f in fw:
            f.wait_recv()

    def xblk(j):
        return xb.at[:, at(j * DC, DC)]

    cq = w_in(wq, wqf)
    xz = [net(tok, xblk(c), cols=c ^ (2 * m)) for m in range(1, Z)]
    xp = net(tok, xblk(c), cols=c ^ 1)
    ga = [net(cot.at[at((c ^ k) * TL, TL), :], gtl.at[:, at(c * DC, DC)], cols=c ^ k) for k in range(1, C)]
    ck = w_in(wk, wkf)

    sr = jnp.broadcast_to(segr[...].astype(F32), (L, L))
    sc = sr.T
    qi = lax.broadcasted_iota(jnp.int32, (L, L), 0)
    ki = lax.broadcasted_iota(jnp.int32, (L, L), 1)
    ok = (sr == sc) & (qi >= ki)
    okf = jnp.where(ok, 1.0, 0.0)
    mskb[...] = jnp.where(ok, 0.0, NEG)
    pos = jnp.sum(okf, 1, keepdims=True) - 1.0
    angle = pos * freq[...]
    lane = lax.broadcasted_iota(jnp.int32, (L, HD), 1)
    cosb[...] = jnp.cos(angle)
    sn = jnp.sin(angle)
    sinb[...] = jnp.where(lane < HD // 2, -sn, sn)

    def to_ws(src, dst):
        cps = [net(src.at[:, at((r ^ k) * DR, DR)], dst.at[r, my_tl, :], rows=r ^ k) for k in range(1, R)]
        return cps, local(src.at[:, at(r * DR, DR)], dst.at[r, my_tl, :])

    def landed(cl):
        for k in cl[0]:
            k.wait_recv()
        cl[1].wait()

    cq.forward()
    cv = w_in(wv, wvf)
    lx.wait()
    xf = cols_forward(xblk, xz)
    lg.wait()
    for k in ga:
        k.wait_recv()
    a_g = to_ws(gtl, gw)
    ck.forward()
    cols_finish(xp, xf)

    def stats(v):
        mean = jnp.sum(v, 1, keepdims=True) / D
        sq = jnp.sum(v * v, 1, keepdims=True) / D
        return mean, lax.rsqrt(sq - mean * mean + EPS)

    def norm_rows(i, _):
        rows = at(i * 32, 32)
        v = xb[rows, :].astype(F32)
        mean, rstd = stats(v)
        h1[rows, :] = ((v - mean) * rstd).astype(BF)
        return 0

    lax.fori_loop(0, L // 32, norm_rows, 0)

    cv.forward()
    co = Gather(net, R, r, lambda h: wo.at[half(HC, h), :], lambda j, h: wof.at[half(HC, h), at(j * DR, DR)])

    def wsblk(buf):
        return lambda j: buf.at[:, at(j * TL, TL), :]

    heads = HC // HD

    def rope(v):
        return jnp.concatenate(
            [v[:, h * HD:(h + 1) * HD] * cosb[...]
             + pltpu.roll(v[:, h * HD:(h + 1) * HD], HD // 2, 1) * sinb[...] for h in range(heads)], 1)

    def unrope(v):
        return v * cosb[...] + pltpu.roll(v * sinb[...], HD // 2, 1)

    def arrived(g):
        for k in range(1, R):
            g.wait(k)

    landed(a_g)
    g_z, g_p = cols_start(wsblk(gw))
    lws[0].wait()
    arrived(cq)
    qb[...] = rope(nn(h1[...], wqf[...])).astype(BF)
    lws[1].wait()
    arrived(ck)
    kb[...] = rope(nn(h1[...], wkf[...])).astype(BF)
    lws[2].wait()
    arrived(cv)
    vb[...] = nn(h1[...], wvf[...]).astype(BF)

    for h in range(heads):
        hs = slice(h * HD, (h + 1) * HD)
        s = nt(qb[:, hs], kb[:, hs]) * scale
        s = jnp.where(mskb[...] < 0.0, NEG, s)
        top = jnp.max(s, 1, keepdims=True)
        e = jnp.exp(s - top)
        tot = jnp.sum(e, 1, keepdims=True)
        lse[:, hs] = jnp.broadcast_to(top + jnp.log(tot), (L, HD))
        att[:, hs] = nn((e / tot).astype(BF), vb[:, hs]).astype(BF)

    def parts_store(dst, val, i=None):
        for j in range(C):
            v = val[j * TL:(j + 1) * TL, :].astype(BF)
            if i is None:
                dst[j % 2, j // 2, :, :] = v
            else:
                dst[j % 2, j // 2, i, :, :] = v

    co.forward()
    lws[3].wait()
    arrived(co)
    W1 = min(512, D)
    for n in range(D // W1):
        ns = slice(n * W1, (n + 1) * W1)
        val = nn(att[...], wof[:, ns])
        for j in range(C):
            p1[j % 2, j // 2, :, ns] = val[j * TL:(j + 1) * TL, :].astype(BF)

    def pre(p, pa):
        return net(p.at[1 - core], pa, cols=c ^ 1)

    def zsend(p, pa, ps, pr):
        out = []
        for m in range(1, Z):
            ps[m] = (p[core, z ^ m].astype(F32) + pa[z ^ m].astype(F32)).astype(BF)
            out.append(net(ps.at[m], pr.at[m], cols=c ^ (2 * m)))
        return out

    def zsum(p, pa, pr, cps):
        tot = p[core, z].astype(F32) + pa[z].astype(F32)
        for m in range(1, Z):
            cps[m - 1].wait_recv()
            tot = tot + pr[m].astype(F32)
        return tot

    k1 = pre(p1, p1a)
    g_f = cols_forward(wsblk(gw), g_z)
    k1.wait_recv()
    z1 = zsend(p1, p1a, p1s, p1r)
    cols_finish(g_p, g_f)
    lout = [local(gw, gw_out)]

    lff[0].wait()
    order = list(range(1, R))
    FC = wgv.shape[1]
    DN = 2
    DW = FC // DN

    def dhid_chunk(n):
        for k in order:
            dhs[k, :, n * DW:(n + 1) * DW] = nt(gw[r ^ k], wdv[n * DW:(n + 1) * DW, :]).astype(BF)

    def dhid_send(n):
        ns = slice(n * DW, (n + 1) * DW)
        return Reduce(net, R, r, lambda k, h: dhs.at[k, half(L, h), ns], lambda k, h: dhr.at[k, half(L, h), ns])

    dhid_chunk(0)
    dh = [dhid_send(0)]
    for n in range(1, DN):
        dhid_chunk(n)

    xv = xb[my_tl, :].astype(F32)
    xm, xr_ = stats(xv)
    xtl[...] = (xv - xm) * xr_
    v = xv + zsum(p1, p1a, p1r, z1)
    x1[...] = v
    mean2, rstd2 = stats(v)
    n2v = (v - mean2) * rstd2
    n2[...] = n2v
    h2t[...] = n2v.astype(BF)
    a_2 = to_ws(h2t, h2w)
    for n in range(1, DN):
        dh.append(dhid_send(n))
    for n in range(DN):
        dho[:, n * DW:(n + 1) * DW] = nt(gw[r], wdv[n * DW:(n + 1) * DW, :])
    landed(a_2)
    h2_z, h2_p = cols_start(wsblk(h2w))
    for d in dh:
        d.relay()
    a_h = to_ws(h1.at[my_tl, :], h1w)
    lff[1].wait()
    lff[2].wait()
    h2_f = cols_forward(wsblk(h2w), h2_z)
    cols_finish(h2_p, h2_f)
    lout.append(local(h2w, h2w_out))

    QN = g["QN"]
    QW = FC // QN
    gu = []

    def gu_chunk(q):
        qs = slice(q * QW, (q + 1) * QW)
        for k in order[::-1] + [0]:
            ga_ = nn(h2w[r ^ k], wgv[:, qs])
            up_ = nn(h2w[r ^ k], wuv[:, qs])
            if k:
                gus[k, q, 0] = ga_.astype(BF)
                gus[k, q, 1] = up_.astype(BF)
            else:
                guo[q, 0] = ga_
                guo[q, 1] = up_
        gu.append(Reduce(net, R, r, lambda k, h: gus.at[k, q, :, half(L, h), :],
                         lambda k, h: gur.at[k, q, :, half(L, h), :]))

    for q in range(QN):
        gu_chunk(q)
        if q:
            gu[q - 1].relay()
    gu[QN - 1].relay()
    landed(a_h)
    h_z, h_p = cols_start(wsblk(h1w))

    for d in dh:
        d.wait()
    dgt = []
    for q in range(QN):
        gu[q].wait()
        qs = slice(q * QW, (q + 1) * QW)

        def act(i, _, q=q, qs=qs):
            rows = at(i * 32, 32)
            gate, up = guo[q, 0, rows, :], guo[q, 1, rows, :]
            dhid = dho[rows, q * QW:(q + 1) * QW]
            for k in gu[q].ks:
                gate = gate + gur[k, q, 0, rows, :].astype(F32)
                up = up + gur[k, q, 1, rows, :].astype(F32)
                dhid = dhid + dhr[k, rows, q * QW:(q + 1) * QW].astype(F32)
            sig = 1.0 / (1.0 + jnp.exp(-gate))
            silu = gate * sig
            hda[r, rows, qs] = (silu * up).astype(BF)
            dgu[0, r, rows, qs] = (dhid * up * sig * (1.0 + gate * (1.0 - sig))).astype(BF)
            dgu[1, r, rows, qs] = (dhid * silu).astype(BF)
            return 0
        lax.fori_loop(0, L // 32, act, 0)
        dgt.append(Gather(net, R, r, lambda h, qs=qs: dgu.at[:, r, half(L, h), qs],
                          lambda j, h, qs=qs: dgu.at[:, j, half(L, h), qs]))

    k2 = {}

    def dh2_block(k):
        s = r ^ k
        tot = nt(dgu[0, s], wgv[...]) + nt(dgu[1, s], wuv[...])
        for j in range(C):
            p2[j % 2, k, j // 2] = tot[j * TL:(j + 1) * TL, :].astype(BF)
        k2[k] = net(p2.at[1 - core, k], p2a.at[k], cols=c ^ 1)

    dh2_block(0)
    z2 = {}
    for q in range(QN):
        dgt[q].forward()
    hdc = Gather(net, R, r, lambda h: hda.at[r, half(L, h), :], lambda j, h: hda.at[j, half(L, h), :])

    def z2_send(k):
        k2[k].wait_recv()
        for m in range(1, Z):
            p2s[k, m] = (p2[core, k, z ^ m].astype(F32) + p2a[k, z ^ m].astype(F32)).astype(BF)
            z2[k, m] = net(p2s.at[k, m], p2r.at[k, m], cols=c ^ (2 * m))

    for n, k in enumerate(order):
        for q in range(QN):
            dgt[q].wait(k)
        dh2_block(k)
        z2_send(n)
    z2_send(R - 1)
    lout += [local(dgu.at[0], dg_out), local(dgu.at[1], du_out)]
    h_f = cols_forward(wsblk(h1w), h_z)
    hdc.forward()

    a_d = []
    for k in range(R):
        tot = p2[core, k, z].astype(F32) + p2a[k, z].astype(F32)
        for m in range(1, Z):
            z2[k, m].wait_recv()
            tot = tot + p2r[k, m].astype(F32)
        dh2s[k] = tot
        if k:
            a_d.append(net(dh2s.at[k], dh2t.at[:, at(r * DR, DR)], rows=r ^ k))
        else:
            l_d = local(dh2s.at[0], dh2t.at[:, at(r * DR, DR)])
    l_d.wait()
    for k in a_d:
        k.wait_recv()

    def norm_back(grad, normed, rstd):
        a = jnp.sum(grad, 1, keepdims=True) / D
        b = jnp.sum(grad * normed, 1, keepdims=True) / D
        return rstd * (grad - a - normed * b)

    _, rstd2b = stats(x1[...])
    dxv = gtl[...].astype(F32) + norm_back(dh2t[...], n2[...], rstd2b)
    dxt[...] = dxv
    dmt[...] = dxv.astype(BF)
    l_m = local(dmt, dmix.at[my_tl, :])

    def dblk(j):
        return dmix.at[at(j * TL, TL), :]
    m_z = [net(dmt, dblk(c), cols=c ^ (2 * m)) for m in range(1, Z)]
    m_p = net(dmt, dblk(c), cols=c ^ 1)

    def ffn_block(k):
        s = r ^ k
        tot = nn(hda[s], wdv[...])
        for j in range(C):
            p3[j % 2, j // 2, k] = tot[j * TL:(j + 1) * TL, :].astype(BF)

    ffn_block(0)
    for k in order:
        hdc.wait(k)
        ffn_block(k)
    k3 = pre(p3, p3a)
    cols_finish(h_p, h_f)
    lout += [local(hda, hd_out), local(h1w, h1w_out)]
    k3.wait_recv()
    z3 = zsend(p3, p3a, p3s, p3r)
    m_f = cols_forward(dblk, m_z)
    l_m.wait()
    cols_finish(m_p, m_f)

    for k in order:
        gop[k] = tn(att[...], dmix[:, at((r ^ k) * DR, DR)]).astype(BF)
    cgo = Reduce(net, R, r, lambda k, h: gop.at[k, half(HC, h), :], lambda k, h: gor.at[k, half(HC, h), :])
    da = nt(dmix[...], wof[...]).astype(BF)
    for h in range(heads):
        hs = slice(h * HD, (h + 1) * HD)
        s = nt(qb[:, hs], kb[:, hs]) * scale
        s = jnp.where(mskb[...] < 0.0, NEG, s)
        pr = jnp.exp(s - lse[:, h * HD:h * HD + 1])
        dp = nt(da[:, hs], vb[:, hs])
        inner = jnp.sum(pr * dp, 1, keepdims=True)
        ds = (pr * (dp - inner)).astype(BF)
        dqkv[0, r, :, hs] = unrope(nn(ds, kb[:, hs]) * scale).astype(BF)
        dqkv[1, r, :, hs] = unrope(tn(ds, qb[:, hs]) * scale).astype(BF)
        dqkv[2, r, :, hs] = tn(pr.astype(BF), da[:, hs]).astype(BF)
    cd = Gather(net, R, r, lambda h: dqkv.at[:, r, half(L, h), :], lambda j, h: dqkv.at[:, j, half(L, h), :])

    for n in range(D // W1):
        ns = slice(n * W1, (n + 1) * W1)
        val = (nt(dqkv[0, r], wqf[ns, :]) + nt(dqkv[1, r], wkf[ns, :]) + nt(dqkv[2, r], wvf[ns, :]))
        for j in range(C):
            p4[j % 2, j // 2, :, ns] = val[j * TL:(j + 1) * TL, :].astype(BF)
    k4 = pre(p4, p4a)
    cgo.relay()
    gof[...] = tn(att[...], dmix[:, at(r * DR, DR)])
    k4.wait_recv()
    z4 = zsend(p4, p4a, p4s, p4r)
    cd.forward()

    fs[...] = zsum(p3, p3a, p3r, z3)
    a_f = [net(fs.at[k], ft.at[:, at(r * DR, DR)], rows=r ^ k) for k in order]
    l_f = local(fs.at[0], ft.at[:, at(r * DR, DR)])
    _, rstd1 = stats(xb[my_tl, :].astype(F32))
    git[...] = dxt[...] + norm_back(zsum(p4, p4a, p4r, z4), xtl[...], rstd1)

    def to_io(src, dst):
        cps = [net(src.at[:, at((c ^ k) * DC, DC)], dst.at[my_tl, :], cols=c ^ k) for k in range(1, C)]
        return cps, local(src.at[:, at(c * DC, DC)], dst.at[my_tl, :])

    i_g = to_io(git, gib)
    l_f.wait()
    for k in a_f:
        k.wait_recv()
    lot[...] = (x1[...] + ft[...]).astype(BF)
    i_o = to_io(lot, lob)
    landed(i_g)
    lout.append(local(gib, gi_out))
    arrived(cd)
    lout.append(local(dqkv, dqkv_out))
    cgo.wait()
    gsum = gof[...]
    for k in cgo.ks:
        gsum = gsum + gor[k].astype(F32)
    gof[...] = gsum
    lout.append(local(gof, go_out))
    landed(i_o)
    lout.append(local(lob, o_out))
    net.drain()
    for k in lout:
        k.wait()


def body(R, C, tokens, segments, w_query, w_key, w_value, w_out, w_gate, w_up, w_down, cotangent):
    L, DC = tokens.shape
    DR, HC = w_query.shape
    D = DR * R
    FC = w_gate.shape[1]
    TL = L // C
    Z = C // 2
    QN = 4 if FC % 1024 == 0 else 2
    QW = FC // QN
    g = dict(R=R, C=C, L=L, TL=TL, D=D, DR=DR, DC=DC, HC=HC, H=FC, QN=QN)
    half = HD // 2
    fr = (BASE ** (-(np.arange(half, dtype=np.float32) * np.float32(2.0)) / np.float32(HD))).astype(np.float32)
    freq = jnp.asarray(np.concatenate([fr, fr])[None, :])
    S = jax.ShapeDtypeStruct
    V = pltpu.VMEM
    outs = [
        S((L, DC), BF), S((L, DC), F32), S((R, L, DR), BF), S((R, L, DR), BF), S((R, L, DR), BF),
        S((R, L, FC), BF), S((R, L, FC), BF), S((R, L, FC), BF),
        S((3, R, L, HC), BF), S((HC, DR), F32),
    ]
    seq = lambda w: [V((2, Z, TL, w), BF), V((Z, TL, w), BF), V((Z, TL, w), BF), V((Z, TL, w), BF)]
    seq4 = lambda: [V((2, Z, R, TL, DR), BF), V((Z, R, TL, DR), BF), V((Z, R, TL, DR), BF), V((Z, R, TL, DR), BF)]
    seq2 = lambda: [V((2, R, Z, TL, DR), BF), V((R, Z, TL, DR), BF), V((R, Z, TL, DR), BF), V((R, Z, TL, DR), BF)]
    scratch = [
        V((L, D), BF), V((L, D), BF), V((TL, D), F32), V((TL, D), BF),
        V((R, L, DR), BF), V((R, L, DR), BF), V((R, L, DR), BF), V((TL, D), BF),
        V((D, HC), BF), V((D, HC), BF), V((D, HC), BF), V((HC, D), BF),
        V((DR, FC), BF), V((DR, FC), BF), V((FC, DR), BF),
        *seq(D), *seq2(), *seq4(), *seq(D),
        V((TL, D), F32), V((TL, D), F32),
        V((R, L, FC), BF), V((R, L, FC), BF), V((L, FC), F32),
        V((R, QN, 2, L, QW), BF), V((R, QN, 2, L, QW), BF), V((QN, 2, L, QW), F32),
        V((R, L, FC), BF), V((2, R, L, FC), BF),
        V((R, TL, DR), F32), V((TL, D), F32), V((TL, D), F32), V((TL, D), BF), V((L, D), BF),
        V((L, HC), BF), V((L, HC), BF), V((L, HC), BF), V((L, HC), BF), V((L, HC), F32),
        V((L, HD), F32), V((L, HD), F32), V((L, L), F32),
        V((3, R, L, HC), BF), V((R, HC, DR), BF), V((R, HC, DR), BF), V((HC, DR), F32),
        V((R, TL, DR), F32), V((TL, D), F32), V((TL, D), BF), V((TL, D), F32), V((L, DC), BF), V((L, DC), F32),
        pltpu.SemaphoreType.DMA((g_sems(R, C, QN),)), pltpu.SemaphoreType.DMA((g_sems(R, C, QN),)),
        pltpu.SemaphoreType.DMA((40,)),
    ]
    A = pl.BlockSpec(memory_space=pl.ANY)
    B = pl.BlockSpec(memory_space=pltpu.VMEM)
    res = pl.pallas_call(
        functools.partial(step_kernel, g),
        out_shape=outs,
        in_specs=[A, A, B, B] + [A] * 7,
        out_specs=[A] * len(outs),
        scratch_shapes=scratch,
        compiler_params=pltpu.CompilerParams(
            collective_id=0, has_side_effects=True, vmem_limit_bytes=67043328),
        name="layer_step",
    )(tokens, cotangent, segments, freq, w_query, w_key, w_value, w_out, w_gate, w_up, w_down)
    layer_out, grad_in, h1w, gw, h2w, dg, du, hd, dqkv, go = res
    T = R * L
    h1w, gw, h2w = (t.reshape(T, DR) for t in (h1w, gw, h2w))
    gq, gk, gv = (tn(h1w, dqkv[i].reshape(T, HC)) for i in range(3))
    ggate, gup, gdown = tn(h2w, dg.reshape(T, FC)), tn(h2w, du.reshape(T, FC)), tn(hd.reshape(T, FC), gw)
    return layer_out, grad_in, gq, gk, gv, go, ggate, gup, gdown


def g_sems(R, C, QN):
    return 2 * (R - 1) * (6 + QN) + 2 * R * (3 + QN) + 5 * (R - 1) + 7 * C + (R + 3) * C // 2 + 2 * C


def solution(mesh):
    R, C = mesh.shape["rows"], mesh.shape["cols"]
    rc, cr = P("rows", "cols"), P("cols", "rows")
    in_specs = (rc, P("rows", None), rc, rc, rc, cr, rc, rc, cr, rc)
    out_specs = (rc, rc, rc, rc, rc, cr, rc, rc, cr)
    return jax.shard_map(functools.partial(body, R, C), mesh=mesh, in_specs=in_specs,
                         out_specs=out_specs, check_vma=False)
```

```python
import functools
import jax
import jax.numpy as jnp
import numpy as np
from jax import lax
from jax.experimental import pallas as pl
from jax.experimental.pallas import tpu as pltpu
from jax.sharding import PartitionSpec as P

HD = 128
EPS = 1e-05
NEG = -1e30
BASE = 10000.0
F32 = jnp.float32
BF = jnp.bfloat16
MESH = pl.DeviceIdType.MESH


def nn(a, b):
    return jnp.dot(a, b, preferred_element_type=F32)


def nt(a, b):
    return lax.dot_general(a, b, (((1,), (1,)), ((), ())), preferred_element_type=F32)


def tn(a, b):
    return lax.dot_general(a, b, (((0,), (0,)), ((), ())), preferred_element_type=F32)


def at(start, size, step=None):
    return pl.ds(pl.multiple_of(start, step or size), size)


class Net:
    def __init__(self, send, recv):
        self.send, self.recv, self.all = send, recv, []

    def __call__(self, src, dst, **peer):
        i = len(self.all)
        assert i < self.send.shape[0]
        c = pltpu.make_async_remote_copy(
            src_ref=src, dst_ref=dst, send_sem=self.send.at[i], recv_sem=self.recv.at[i],
            device_id=peer, device_id_type=MESH)
        c.start()
        self.all.append(Copy(c))
        return self.all[-1]

    def drain(self):
        for c in self.all:
            c.c.wait_send()


class Copy:
    def __init__(self, c):
        self.c, self.open = c, True

    def wait_recv(self):
        if self.open:
            self.c.wait_recv()
        self.open = False


class Gather:
    def __init__(self, net, R, r, own, blk):
        self.net, self.r, self.two, self.blk, self.c = net, r, R == 4, blk, {}
        todo = [(1, 0), (2, 1), (1, 1), (2, 0)] if self.two else [(k, h) for k in range(1, R) for h in range(2)]
        for k, h in todo:
            self.c[k, h] = net(own(h), blk(r, h), rows=r ^ k)

    def forward(self):
        if self.two:
            for k, h in ((1, 0), (2, 1)):
                self.c[k, h].wait_recv()
                b = self.blk(self.r ^ k, h)
                self.c[3, h] = self.net(b, b, rows=self.r ^ (3 - k))

    def wait(self, k):
        for h in range(2):
            self.c[k, h].wait_recv()


class Reduce:
    def __init__(self, net, R, r, snd, rcv):
        self.net, self.r, self.two, self.snd, self.rcv, self.c = net, r, R == 4, snd, rcv, {}
        self.ks = (1, 2) if self.two else tuple(range(1, R))
        if self.two:
            for k, h in ((1, 0), (2, 1)):
                self.c[3, h] = net(snd(3, h), rcv(3, h), rows=r ^ k)
            for k, h in ((1, 0), (2, 1)):
                self.c[k, h] = net(snd(k, h), rcv(k, h), rows=r ^ k)
        else:
            for k in self.ks:
                for h in range(2):
                    self.c[k, h] = net(snd(k, h), rcv(k, h), rows=r ^ k)

    def relay(self):
        if self.two:
            for k, h in ((2, 0), (1, 1)):
                self.c[3, h].wait_recv()
                a = self.snd(k, h)
                a[...] = (a[...].astype(F32) + self.rcv(3, h)[...].astype(F32)).astype(BF)
                self.c[k, h] = self.net(a, self.rcv(k, h), rows=self.r ^ k)

    def wait(self):
        for k in self.ks:
            for h in range(2):
                self.c[k, h].wait_recv()


class LCopy:
    def __init__(self, c):
        self.c, self.open = c, True

    def wait(self):
        if self.open:
            self.c.wait()
        self.open = False


class Local:
    def __init__(self, sem):
        self.sem, self.n, self.all = sem, 0, []

    def __call__(self, src, dst):
        c = pltpu.make_async_copy(src, dst, self.sem.at[self.n])
        self.n += 1
        c.start()
        self.all.append(LCopy(c))
        return self.all[-1]


def step_kernel(g, *refs):
    (tok, cot, seg_in, freq_in, wq, wk, wv, wo, wg, wu, wd,
     o_out, gi_out, h1w_out, gw_out, h2w_out, dg_out, du_out, hd_out, dq_out, dk_out, dv_out, go_out,
     xb, h1, xtl, gtl, h1w, gw, h2w, h2t, wqf, wkf, wvf, wof, wgv, wuv, wdv,
     p1, p1a, p1s, p1r, p2, p2a, p2s, p2r, p3, p3a, p3s, p3r, p4, p4a, p4s, p4r,
     x1, n2, dhs, dhr, dho, gus, gur, guo, hda, dgu, dh2s, dh2t, dxt, dmt, dmix,
     qb, kb, vb, att, lse, cosb, sinb, mskb, dqkv, gop, gor, gof, fs, ft, lot, git, lob, gib, gif, segr, freq,
     send, recv, loc) = refs
    R, C, L, TL, D, DR, DC, HC, H = (g[k] for k in ("R", "C", "L", "TL", "D", "DR", "DC", "HC", "H"))
    Z = C // 2
    r = lax.axis_index("rows")
    c = lax.axis_index("cols")
    z = c // 2
    core = c % 2
    net = Net(send, recv)
    local = Local(loc)
    scale = HD ** (-0.5)
    my_tl = at(c * TL, TL)

    bar = pltpu.get_barrier_semaphore()
    for k in range(1, R):
        pl.semaphore_signal(bar, inc=1, device_id={"rows": r ^ k}, device_id_type=MESH)
    for k in range(1, C):
        pl.semaphore_signal(bar, inc=1, device_id={"cols": c ^ k}, device_id_type=MESH)

    lsm = [local(seg_in, segr), local(freq_in, freq)]
    lx = local(tok, xb.at[:, at(c * DC, DC)])
    lg = local(cot.at[my_tl, :], gtl.at[:, at(c * DC, DC)])
    lws = [local(wq, wqf.at[at(r * DR, DR), :]), local(wk, wkf.at[at(r * DR, DR), :]),
           local(wv, wvf.at[at(r * DR, DR), :]), local(wo, wof.at[:, at(r * DR, DR)])]
    lff = [local(wd, wdv), local(wg, wgv), local(wu, wuv)]

    pl.semaphore_wait(bar, R + C - 2)

    def half(n, h):
        return slice(h * (n // 2), (h + 1) * (n // 2))

    def w_in(w, full):
        n = DR // 2
        return Gather(net, R, r, lambda h: w.at[half(DR, h), :], lambda j, h: full.at[at(j * DR + h * n, n), :])

    def cols_start(blk):
        zs = [net(blk(c), blk(c), cols=c ^ (2 * m)) for m in range(1, Z)]
        return zs, net(blk(c), blk(c), cols=c ^ 1)

    def cols_forward(blk, zs):
        fw = []
        for m in range(1, Z):
            zs[m - 1].wait_recv()
            fw.append(net(blk(c ^ (2 * m)), blk(c ^ (2 * m)), cols=c ^ 1))
        return fw

    def cols_finish(own, fw):
        own.wait_recv()
        for f in fw:
            f.wait_recv()

    def xblk(j):
        return xb.at[:, at(j * DC, DC)]

    cq = w_in(wq, wqf)
    xz = [net(tok, xblk(c), cols=c ^ (2 * m)) for m in range(1, Z)]
    xp = net(tok, xblk(c), cols=c ^ 1)
    ga = [net(cot.at[at((c ^ k) * TL, TL), :], gtl.at[:, at(c * DC, DC)], cols=c ^ k) for k in range(1, C)]
    ck = w_in(wk, wkf)

    for k in lsm:
        k.wait()
    sr = jnp.broadcast_to(segr[...].astype(F32), (L, L))
    sc = sr.T
    qi = lax.broadcasted_iota(jnp.int32, (L, L), 0)
    ki = lax.broadcasted_iota(jnp.int32, (L, L), 1)
    ok = (sr == sc) & (qi >= ki)
    okf = jnp.where(ok, 1.0, 0.0)
    mskb[...] = jnp.where(ok, 0.0, NEG)
    pos = jnp.sum(okf, 1, keepdims=True) - 1.0
    angle = pos * freq[...]
    lane = lax.broadcasted_iota(jnp.int32, (L, HD), 1)
    cosb[...] = jnp.cos(angle)
    sn = jnp.sin(angle)
    sinb[...] = jnp.where(lane < HD // 2, -sn, sn)

    def to_ws(src, dst):
        cps = [net(src.at[:, at((r ^ k) * DR, DR)], dst.at[r, my_tl, :], rows=r ^ k) for k in range(1, R)]
        return cps, local(src.at[:, at(r * DR, DR)], dst.at[r, my_tl, :])

    def landed(cl):
        for k in cl[0]:
            k.wait_recv()
        cl[1].wait()

    cq.forward()
    cv = w_in(wv, wvf)
    lx.wait()
    xf = cols_forward(xblk, xz)
    lg.wait()
    for k in ga:
        k.wait_recv()
    a_g = to_ws(gtl, gw)
    ck.forward()
    cols_finish(xp, xf)

    def stats(v):
        mean = jnp.sum(v, 1, keepdims=True) / D
        sq = jnp.sum(v * v, 1, keepdims=True) / D
        return mean, lax.rsqrt(sq - mean * mean + EPS)

    def norm_rows(i, _):
        rows = at(i * 32, 32)
        v = xb[rows, :].astype(F32)
        mean, rstd = stats(v)
        h1[rows, :] = ((v - mean) * rstd).astype(BF)
        return 0

    lax.fori_loop(0, L // 32, norm_rows, 0)

    cv.forward()
    co = Gather(net, R, r, lambda h: wo.at[half(HC, h), :], lambda j, h: wof.at[half(HC, h), at(j * DR, DR)])

    def wsblk(buf):
        return lambda j: buf.at[:, at(j * TL, TL), :]

    heads = HC // HD

    def rope(v):
        return jnp.concatenate(
            [v[:, h * HD:(h + 1) * HD] * cosb[...]
             + pltpu.roll(v[:, h * HD:(h + 1) * HD], HD // 2, 1) * sinb[...] for h in range(heads)], 1)

    def unrope(v):
        return v * cosb[...] + pltpu.roll(v * sinb[...], HD // 2, 1)

    def arrived(g):
        for k in range(1, R):
            g.wait(k)

    landed(a_g)
    g_z, g_p = cols_start(wsblk(gw))
    lws[0].wait()
    arrived(cq)
    qb[...] = rope(nn(h1[...], wqf[...])).astype(BF)
    lws[1].wait()
    arrived(ck)
    kb[...] = rope(nn(h1[...], wkf[...])).astype(BF)
    lws[2].wait()
    arrived(cv)
    vb[...] = nn(h1[...], wvf[...]).astype(BF)

    for h in range(heads):
        hs = slice(h * HD, (h + 1) * HD)
        s = nt(qb[:, hs], kb[:, hs]) * scale
        s = jnp.where(mskb[...] < 0.0, NEG, s)
        top = jnp.max(s, 1, keepdims=True)
        e = jnp.exp(s - top)
        tot = jnp.sum(e, 1, keepdims=True)
        lse[:, hs] = jnp.broadcast_to(top + jnp.log(tot), (L, HD))
        att[:, hs] = nn((e / tot).astype(BF), vb[:, hs]).astype(BF)

    def parts_store(dst, val, i=None):
        for j in range(C):
            v = val[j * TL:(j + 1) * TL, :].astype(BF)
            if i is None:
                dst[j % 2, j // 2, :, :] = v
            else:
                dst[j % 2, j // 2, i, :, :] = v

    co.forward()
    lws[3].wait()
    arrived(co)
    W1 = min(512, D)
    for n in range(D // W1):
        ns = slice(n * W1, (n + 1) * W1)
        val = nn(att[...], wof[:, ns])
        for j in range(C):
            p1[j % 2, j // 2, :, ns] = val[j * TL:(j + 1) * TL, :].astype(BF)

    def pre(p, pa):
        return net(p.at[1 - core], pa, cols=c ^ 1)

    def zsend(p, pa, ps, pr):
        out = []
        for m in range(1, Z):
            ps[m] = (p[core, z ^ m].astype(F32) + pa[z ^ m].astype(F32)).astype(BF)
            out.append(net(ps.at[m], pr.at[m], cols=c ^ (2 * m)))
        return out

    def zsum(p, pa, pr, cps):
        tot = p[core, z].astype(F32) + pa[z].astype(F32)
        for m in range(1, Z):
            cps[m - 1].wait_recv()
            tot = tot + pr[m].astype(F32)
        return tot

    k1 = pre(p1, p1a)
    g_f = cols_forward(wsblk(gw), g_z)
    k1.wait_recv()
    z1 = zsend(p1, p1a, p1s, p1r)
    cols_finish(g_p, g_f)
    lout = [local(gw, gw_out)]

    lff[0].wait()
    order = list(range(1, R))
    FC = wgv.shape[1]
    DN = 2
    DW = FC // DN

    def dhid_chunk(n):
        for k in order:
            dhs[k, :, n * DW:(n + 1) * DW] = nt(gw[r ^ k], wdv[n * DW:(n + 1) * DW, :]).astype(BF)

    def dhid_send(n):
        ns = slice(n * DW, (n + 1) * DW)
        return Reduce(net, R, r, lambda k, h: dhs.at[k, half(L, h), ns], lambda k, h: dhr.at[k, half(L, h), ns])

    dhid_chunk(0)
    dh = [dhid_send(0)]
    for n in range(1, DN):
        dhid_chunk(n)

    xv = xb[my_tl, :].astype(F32)
    xm, xr_ = stats(xv)
    xtl[...] = (xv - xm) * xr_
    v = xv + zsum(p1, p1a, p1r, z1)
    x1[...] = v
    mean2, rstd2 = stats(v)
    n2v = (v - mean2) * rstd2
    n2[...] = n2v
    h2t[...] = n2v.astype(BF)
    a_2 = to_ws(h2t, h2w)
    for n in range(1, DN):
        dh.append(dhid_send(n))
    for n in range(DN):
        dho[:, n * DW:(n + 1) * DW] = nt(gw[r], wdv[n * DW:(n + 1) * DW, :])
    landed(a_2)
    h2_z, h2_p = cols_start(wsblk(h2w))
    for d in dh:
        d.relay()
    a_h = to_ws(h1.at[my_tl, :], h1w)
    lff[1].wait()
    lff[2].wait()
    h2_f = cols_forward(wsblk(h2w), h2_z)
    cols_finish(h2_p, h2_f)
    lout.append(local(h2w, h2w_out))

    QN = g["QN"]
    QW = FC // QN
    gu = []

    def gu_chunk(q):
        qs = slice(q * QW, (q + 1) * QW)
        for k in order[::-1] + [0]:
            ga_ = nn(h2w[r ^ k], wgv[:, qs])
            up_ = nn(h2w[r ^ k], wuv[:, qs])
            if k:
                gus[k, q, 0] = ga_.astype(BF)
                gus[k, q, 1] = up_.astype(BF)
            else:
                guo[q, 0] = ga_
                guo[q, 1] = up_
        gu.append(Reduce(net, R, r, lambda k, h: gus.at[k, q, :, half(L, h), :],
                         lambda k, h: gur.at[k, q, :, half(L, h), :]))

    for q in range(QN):
        gu_chunk(q)
        if q:
            gu[q - 1].relay()
    gu[QN - 1].relay()
    landed(a_h)
    h_z, h_p = cols_start(wsblk(h1w))

    for d in dh:
        d.wait()
    dgt = []
    for q in range(QN):
        gu[q].wait()
        qs = slice(q * QW, (q + 1) * QW)

        def act(i, _, q=q, qs=qs):
            rows = at(i * 32, 32)
            gate, up = guo[q, 0, rows, :], guo[q, 1, rows, :]
            dhid = dho[rows, q * QW:(q + 1) * QW]
            for k in gu[q].ks:
                gate = gate + gur[k, q, 0, rows, :].astype(F32)
                up = up + gur[k, q, 1, rows, :].astype(F32)
                dhid = dhid + dhr[k, rows, q * QW:(q + 1) * QW].astype(F32)
            sig = 1.0 / (1.0 + jnp.exp(-gate))
            silu = gate * sig
            hda[r, rows, qs] = (silu * up).astype(BF)
            dgu[0, r, rows, qs] = (dhid * up * sig * (1.0 + gate * (1.0 - sig))).astype(BF)
            dgu[1, r, rows, qs] = (dhid * silu).astype(BF)
            return 0
        lax.fori_loop(0, L // 32, act, 0)
        dgt.append(Gather(net, R, r, lambda h, qs=qs: dgu.at[:, r, half(L, h), qs],
                          lambda j, h, qs=qs: dgu.at[:, j, half(L, h), qs]))

    k2 = {}

    def dh2_block(k):
        s = r ^ k
        tot = nt(dgu[0, s], wgv[...]) + nt(dgu[1, s], wuv[...])
        for j in range(C):
            p2[j % 2, k, j // 2] = tot[j * TL:(j + 1) * TL, :].astype(BF)
        k2[k] = net(p2.at[1 - core, k], p2a.at[k], cols=c ^ 1)

    dh2_block(0)
    z2 = {}
    for q in range(QN):
        dgt[q].forward()

    def hid_send(n):
        ns = slice(n * DW, (n + 1) * DW)
        return Gather(net, R, r, lambda h: hda.at[r, half(L, h), ns], lambda j, h: hda.at[j, half(L, h), ns])

    hdc = [hid_send(0)]

    def z2_send(k):
        k2[k].wait_recv()
        for m in range(1, Z):
            p2s[k, m] = (p2[core, k, z ^ m].astype(F32) + p2a[k, z ^ m].astype(F32)).astype(BF)
            z2[k, m] = net(p2s.at[k, m], p2r.at[k, m], cols=c ^ (2 * m))

    for n, k in enumerate(order):
        for q in range(QN):
            dgt[q].wait(k)
        dh2_block(k)
        z2_send(n)
    z2_send(R - 1)
    lout += [local(dgu.at[0], dg_out), local(dgu.at[1], du_out)]
    hdc[0].forward()

    a_d = []
    for k in range(R):
        tot = p2[core, k, z].astype(F32) + p2a[k, z].astype(F32)
        for m in range(1, Z):
            z2[k, m].wait_recv()
            tot = tot + p2r[k, m].astype(F32)
        dh2s[k] = tot.astype(BF)
        if k:
            a_d.append(net(dh2s.at[k], dh2t.at[:, at(r * DR, DR)], rows=r ^ k))
        else:
            l_d = local(dh2s.at[0], dh2t.at[:, at(r * DR, DR)])
    hdc += [hid_send(n) for n in range(1, DN)]
    l_d.wait()
    for k in a_d:
        k.wait_recv()

    def norm_back(grad, normed, rstd):
        a = jnp.sum(grad, 1, keepdims=True) / D
        b = jnp.sum(grad * normed, 1, keepdims=True) / D
        return rstd * (grad - a - normed * b)

    _, rstd2b = stats(x1[...])
    dxv = gtl[...].astype(F32) + norm_back(dh2t[...].astype(F32), n2[...], rstd2b)
    dxt[...] = dxv
    dmt[...] = dxv.astype(BF)
    l_m = local(dmt, dmix.at[my_tl, :])

    def dblk(j):
        return dmix.at[at(j * TL, TL), :]
    m_z = [net(dmt, dblk(c), cols=c ^ (2 * m)) for m in range(1, Z)]
    m_p = net(dmt, dblk(c), cols=c ^ 1)

    def ffn_block(k):
        s = r ^ k
        tot = nn(hda[s], wdv[...])
        for j in range(C):
            p3[j % 2, j // 2, k] = tot[j * TL:(j + 1) * TL, :].astype(BF)

    ffn_block(0)
    h_f = cols_forward(wsblk(h1w), h_z)
    for d in hdc[1:]:
        d.forward()
    for k in order:
        for d in hdc:
            d.wait(k)
        ffn_block(k)
    k3 = pre(p3, p3a)
    cols_finish(h_p, h_f)
    lout += [local(hda, hd_out), local(h1w, h1w_out)]
    k3.wait_recv()
    m_f = cols_forward(dblk, m_z)
    z3 = zsend(p3, p3a, p3s, p3r)
    l_m.wait()
    cols_finish(m_p, m_f)

    for k in order:
        gop[k] = tn(att[...], dmix[:, at((r ^ k) * DR, DR)]).astype(BF)
    cgo = Reduce(net, R, r, lambda k, h: gop.at[k, half(HC, h), :], lambda k, h: gor.at[k, half(HC, h), :])
    da = nt(dmix[...], wof[...]).astype(BF)
    for h in range(heads):
        hs = slice(h * HD, (h + 1) * HD)
        s = nt(qb[:, hs], kb[:, hs]) * scale
        s = jnp.where(mskb[...] < 0.0, NEG, s)
        pr = jnp.exp(s - lse[:, h * HD:h * HD + 1])
        dp = nt(da[:, hs], vb[:, hs])
        inner = jnp.sum(pr * dp, 1, keepdims=True)
        ds = (pr * (dp - inner)).astype(BF)
        dqkv[0, r, :, hs] = unrope(nn(ds, kb[:, hs]) * scale).astype(BF)
        dqkv[1, r, :, hs] = unrope(tn(ds, qb[:, hs]) * scale).astype(BF)
        dqkv[2, r, :, hs] = tn(pr.astype(BF), da[:, hs]).astype(BF)
    cd = Gather(net, R, r, lambda h: dqkv.at[:, r, half(L, h), :], lambda j, h: dqkv.at[:, j, half(L, h), :])

    for n in range(D // W1):
        ns = slice(n * W1, (n + 1) * W1)
        val = (nt(dqkv[0, r], wqf[ns, :]) + nt(dqkv[1, r], wkf[ns, :]) + nt(dqkv[2, r], wvf[ns, :]))
        for j in range(C):
            p4[j % 2, j // 2, :, ns] = val[j * TL:(j + 1) * TL, :].astype(BF)
    k4 = pre(p4, p4a)
    cgo.relay()
    gof[...] = tn(att[...], dmix[:, at(r * DR, DR)])
    k4.wait_recv()
    z4 = zsend(p4, p4a, p4s, p4r)
    cd.forward()

    fs[...] = zsum(p3, p3a, p3r, z3).astype(BF)
    a_f = [net(fs.at[k], ft.at[:, at(r * DR, DR)], rows=r ^ k) for k in order]
    l_f = local(fs.at[0], ft.at[:, at(r * DR, DR)])
    _, rstd1 = stats(xb[my_tl, :].astype(F32))
    git[...] = (dxt[...] + norm_back(zsum(p4, p4a, p4r, z4), xtl[...], rstd1)).astype(BF)

    def to_io(src, dst):
        cps = [net(src.at[:, at((c ^ k) * DC, DC)], dst.at[my_tl, :], cols=c ^ k) for k in range(1, C)]
        return cps, local(src.at[:, at(c * DC, DC)], dst.at[my_tl, :])

    i_g = to_io(git, gib)
    l_f.wait()
    for k in a_f:
        k.wait_recv()
    lot[...] = (x1[...] + ft[...].astype(F32)).astype(BF)
    i_o = to_io(lot, lob)
    landed(i_g)
    gif[...] = gib[...].astype(F32)
    lout.append(local(gif, gi_out))
    arrived(cd)
    lout += [local(dqkv.at[0], dq_out), local(dqkv.at[1], dk_out), local(dqkv.at[2], dv_out)]
    cgo.wait()
    gsum = gof[...]
    for k in cgo.ks:
        gsum = gsum + gor[k].astype(F32)
    gof[...] = gsum
    lout.append(local(gof, go_out))
    landed(i_o)
    lout.append(local(lob, o_out))
    net.drain()
    for k in lout:
        k.wait()


def body(R, C, tokens, segments, w_query, w_key, w_value, w_out, w_gate, w_up, w_down, cotangent):
    L, DC = tokens.shape
    DR, HC = w_query.shape
    D = DR * R
    FC = w_gate.shape[1]
    TL = L // C
    Z = C // 2
    QN = 4 if FC % 1024 == 0 else 2
    QW = FC // QN
    g = dict(R=R, C=C, L=L, TL=TL, D=D, DR=DR, DC=DC, HC=HC, H=FC, QN=QN)
    half = HD // 2
    fr = (BASE ** (-(np.arange(half, dtype=np.float32) * np.float32(2.0)) / np.float32(HD))).astype(np.float32)
    freq = jnp.asarray(np.concatenate([fr, fr])[None, :])
    S = jax.ShapeDtypeStruct
    V = pltpu.VMEM
    outs = [
        S((L, DC), BF), S((L, DC), F32), S((R, L, DR), BF), S((R, L, DR), BF), S((R, L, DR), BF),
        S((R, L, FC), BF), S((R, L, FC), BF), S((R, L, FC), BF),
        S((R, L, HC), BF), S((R, L, HC), BF), S((R, L, HC), BF), S((HC, DR), F32),
    ]
    seq = lambda w: [V((2, Z, TL, w), BF), V((Z, TL, w), BF), V((Z, TL, w), BF), V((Z, TL, w), BF)]
    seq4 = lambda: [V((2, Z, R, TL, DR), BF), V((Z, R, TL, DR), BF), V((Z, R, TL, DR), BF), V((Z, R, TL, DR), BF)]
    seq2 = lambda: [V((2, R, Z, TL, DR), BF), V((R, Z, TL, DR), BF), V((R, Z, TL, DR), BF), V((R, Z, TL, DR), BF)]
    scratch = [
        V((L, D), BF), V((L, D), BF), V((TL, D), F32), V((TL, D), BF),
        V((R, L, DR), BF), V((R, L, DR), BF), V((R, L, DR), BF), V((TL, D), BF),
        V((D, HC), BF), V((D, HC), BF), V((D, HC), BF), V((HC, D), BF),
        V((DR, FC), BF), V((DR, FC), BF), V((FC, DR), BF),
        *seq(D), *seq2(), *seq4(), *seq(D),
        V((TL, D), F32), V((TL, D), F32),
        V((R, L, FC), BF), V((R, L, FC), BF), V((L, FC), F32),
        V((R, QN, 2, L, QW), BF), V((R, QN, 2, L, QW), BF), V((QN, 2, L, QW), F32),
        V((R, L, FC), BF), V((2, R, L, FC), BF),
        V((R, TL, DR), BF), V((TL, D), BF), V((TL, D), F32), V((TL, D), BF), V((L, D), BF),
        V((L, HC), BF), V((L, HC), BF), V((L, HC), BF), V((L, HC), BF), V((L, HC), F32),
        V((L, HD), F32), V((L, HD), F32), V((L, L), F32),
        V((3, R, L, HC), BF), V((R, HC, DR), BF), V((R, HC, DR), BF), V((HC, DR), F32),
        V((R, TL, DR), BF), V((TL, D), BF), V((TL, D), BF), V((TL, D), BF), V((L, DC), BF), V((L, DC), BF), V((L, DC), F32),
        V((1, L), jnp.int32), V((1, HD), F32),
        pltpu.SemaphoreType.DMA((g_sems(R, C, QN),)), pltpu.SemaphoreType.DMA((g_sems(R, C, QN),)),
        pltpu.SemaphoreType.DMA((40,)),
    ]
    A = pl.BlockSpec(memory_space=pl.ANY)
    res = pl.pallas_call(
        functools.partial(step_kernel, g),
        out_shape=outs,
        in_specs=[A] * 11,
        out_specs=[A] * len(outs),
        scratch_shapes=scratch,
        compiler_params=pltpu.CompilerParams(
            collective_id=0, has_side_effects=True, vmem_limit_bytes=67043328),
        name="layer_step",
    )(tokens, cotangent, segments, freq, w_query, w_key, w_value, w_out, w_gate, w_up, w_down)
    layer_out, grad_in, h1w, gw, h2w, dg, du, hd, dq, dk, dv, go = res
    T = R * L
    h1w, gw, h2w = (t.reshape(T, DR) for t in (h1w, gw, h2w))
    gq, gk, gv = (tn(h1w, t.reshape(T, HC)) for t in (dq, dk, dv))
    ggate, gup, gdown = tn(h2w, dg.reshape(T, FC)), tn(h2w, du.reshape(T, FC)), tn(hd.reshape(T, FC), gw)
    return layer_out, grad_in, gq, gk, gv, go, ggate, gup, gdown


def g_sems(R, C, QN):
    return 2 * (R - 1) * (7 + QN) + 2 * R * (3 + QN) + 5 * (R - 1) + 7 * C + (R + 3) * C // 2 + 2 * C


def solution(mesh):
    R, C = mesh.shape["rows"], mesh.shape["cols"]
    rc, cr = P("rows", "cols"), P("cols", "rows")
    in_specs = (rc, P("rows", None), rc, rc, rc, cr, rc, rc, cr, rc)
    out_specs = (rc, rc, rc, rc, rc, cr, rc, rc, cr)
    return jax.shard_map(functools.partial(body, R, C), mesh=mesh, in_specs=in_specs,
                         out_specs=out_specs, check_vma=False)
```

```python
import functools
import jax
import jax.numpy as jnp
import numpy as np
from jax import lax
from jax.experimental import pallas as pl
from jax.experimental.pallas import tpu as pltpu
from jax.sharding import PartitionSpec as P

HD = 128
EPS = 1e-05
NEG = -1e30
BASE = 10000.0
F32 = jnp.float32
BF = jnp.bfloat16
MESH = pl.DeviceIdType.MESH


def nn(a, b):
    return jnp.dot(a, b, preferred_element_type=F32)


def nt(a, b):
    return lax.dot_general(a, b, (((1,), (1,)), ((), ())), preferred_element_type=F32)


def tn(a, b):
    return lax.dot_general(a, b, (((0,), (0,)), ((), ())), preferred_element_type=F32)


def at(start, size, step=None):
    return pl.ds(pl.multiple_of(start, step or size), size)


class Net:
    def __init__(self, send, recv):
        self.send, self.recv, self.all = send, recv, []

    def __call__(self, src, dst, **peer):
        i = len(self.all)
        assert i < self.send.shape[0]
        c = pltpu.make_async_remote_copy(
            src_ref=src, dst_ref=dst, send_sem=self.send.at[i], recv_sem=self.recv.at[i],
            device_id=peer, device_id_type=MESH)
        c.start()
        self.all.append(Copy(c))
        return self.all[-1]

    def drain(self):
        for c in self.all:
            c.c.wait_send()


class Copy:
    def __init__(self, c):
        self.c, self.open = c, True

    def wait_recv(self):
        if self.open:
            self.c.wait_recv()
        self.open = False


class Gather:
    def __init__(self, net, R, r, own, blk):
        self.net, self.r, self.two, self.blk, self.c = net, r, R == 4, blk, {}
        todo = [(1, 0), (2, 1), (1, 1), (2, 0)] if self.two else [(k, h) for k in range(1, R) for h in range(2)]
        for k, h in todo:
            self.c[k, h] = net(own(h), blk(r, h), rows=r ^ k)

    def forward(self):
        if self.two:
            for k, h in ((1, 0), (2, 1)):
                self.c[k, h].wait_recv()
                b = self.blk(self.r ^ k, h)
                self.c[3, h] = self.net(b, b, rows=self.r ^ (3 - k))

    def wait(self, k):
        for h in range(2):
            self.c[k, h].wait_recv()


class Reduce:
    def __init__(self, net, R, r, snd, rcv):
        self.net, self.r, self.two, self.snd, self.rcv, self.c = net, r, R == 4, snd, rcv, {}
        self.ks = (1, 2) if self.two else tuple(range(1, R))
        if self.two:
            for k, h in ((1, 0), (2, 1)):
                self.c[3, h] = net(snd(3, h), rcv(3, h), rows=r ^ k)
            for k, h in ((1, 0), (2, 1)):
                self.c[k, h] = net(snd(k, h), rcv(k, h), rows=r ^ k)
        else:
            for k in self.ks:
                for h in range(2):
                    self.c[k, h] = net(snd(k, h), rcv(k, h), rows=r ^ k)

    def relay(self):
        if self.two:
            for k, h in ((2, 0), (1, 1)):
                self.c[3, h].wait_recv()
                a = self.snd(k, h)
                a[...] = (a[...].astype(F32) + self.rcv(3, h)[...].astype(F32)).astype(BF)
                self.c[k, h] = self.net(a, self.rcv(k, h), rows=self.r ^ k)

    def wait(self):
        for k in self.ks:
            for h in range(2):
                self.c[k, h].wait_recv()


class LCopy:
    def __init__(self, c):
        self.c, self.open = c, True

    def wait(self):
        if self.open:
            self.c.wait()
        self.open = False


class Local:
    def __init__(self, sem):
        self.sem, self.n, self.all = sem, 0, []

    def __call__(self, src, dst):
        c = pltpu.make_async_copy(src, dst, self.sem.at[self.n])
        self.n += 1
        c.start()
        self.all.append(LCopy(c))
        return self.all[-1]


def step_kernel(g, *refs):
    (tok, cot, seg_in, freq_in, wq, wk, wv, wo, wg, wu, wd,
     o_out, gi_out, h1w_out, gw_out, h2w_out, dg_out, du_out, hd_out, dq_out, dk_out, dv_out, go_out,
     xb, h1, xtl, gtl, h1w, gw, h2w, h2t, wqf, wkf, wvf, wof, wgv, wuv, wdv,
     p1, p1a, p1s, p1r, p2, p2a, p2s, p2r, p3, p3a, p3s, p3r, p4, p4a, p4s, p4r,
     x1, n2, dhs, dhr, dho, gus, gur, guo, hda, dgu, dh2s, dh2t, dxt, dmt, dmix,
     qb, kb, vb, att, lse, cosb, sinb, mskb, dqkv, gop, gor, gof, fs, ft, lot, git, lob, gib, gif, segr, freq,
     send, recv, loc) = refs
    R, C, L, TL, D, DR, DC, HC, NT = (g[k] for k in ("R", "C", "L", "TL", "D", "DR", "DC", "HC", "NT"))
    LH, TH = L // NT, TL // NT
    Z = C // 2
    r = lax.axis_index("rows")
    c = lax.axis_index("cols")
    z = c // 2
    core = c % 2
    net = Net(send, recv)
    local = Local(loc)
    scale = HD ** (-0.5)
    my_th = at(c * TH, TH)

    def piece(val, j, t):
        return val[t * LH + j * TH:t * LH + (j + 1) * TH, :]

    bar = pltpu.get_barrier_semaphore()
    for k in range(1, R):
        pl.semaphore_signal(bar, inc=1, device_id={"rows": r ^ k}, device_id_type=MESH)
    for k in range(1, C):
        pl.semaphore_signal(bar, inc=1, device_id={"cols": c ^ k}, device_id_type=MESH)

    lsm = [local(seg_in, segr), local(freq_in, freq)]
    lx = local(tok, xb.at[:, :, at(c * DC, DC)])
    lg = local(cot.at[:, my_th, :], gtl.at[:, :, at(c * DC, DC)])
    lws = [local(wq, wqf.at[at(r * DR, DR), :]), local(wk, wkf.at[at(r * DR, DR), :]),
           local(wv, wvf.at[at(r * DR, DR), :]), local(wo, wof.at[:, at(r * DR, DR)])]
    lff = [local(wd, wdv), local(wg, wgv), local(wu, wuv)]

    pl.semaphore_wait(bar, R + C - 2)

    def half(n, h):
        return slice(h * (n // 2), (h + 1) * (n // 2))

    def w_in(w, full):
        n = DR // 2
        return Gather(net, R, r, lambda h: w.at[half(DR, h), :], lambda j, h: full.at[at(j * DR + h * n, n), :])

    def cols_start(blk):
        zs = [net(blk(c), blk(c), cols=c ^ (2 * m)) for m in range(1, Z)]
        return zs, net(blk(c), blk(c), cols=c ^ 1)

    def cols_forward(blk, zs):
        fw = []
        for m in range(1, Z):
            zs[m - 1].wait_recv()
            fw.append(net(blk(c ^ (2 * m)), blk(c ^ (2 * m)), cols=c ^ 1))
        return fw

    def cols_finish(own, fw):
        own.wait_recv()
        for f in fw:
            f.wait_recv()

    def xblk(j):
        return xb.at[:, :, at(j * DC, DC)]

    cq = w_in(wq, wqf)
    xz = [net(tok, xblk(c), cols=c ^ (2 * m)) for m in range(1, Z)]
    xp = net(tok, xblk(c), cols=c ^ 1)
    ga = [net(cot.at[:, at((c ^ k) * TH, TH), :], gtl.at[:, :, at(c * DC, DC)], cols=c ^ k) for k in range(1, C)]
    ck = w_in(wk, wkf)

    for k in lsm:
        k.wait()
    sr = jnp.broadcast_to(segr[...].astype(F32), (L, L))
    sc = sr.T
    qi = lax.broadcasted_iota(jnp.int32, (L, L), 0)
    ki = lax.broadcasted_iota(jnp.int32, (L, L), 1)
    ok = (sr == sc) & (qi >= ki)
    okf = jnp.where(ok, 1.0, 0.0)
    mskb[...] = jnp.where(ok, 0.0, NEG)
    pos = jnp.sum(okf, 1, keepdims=True) - 1.0
    angle = pos * freq[...]
    lane = lax.broadcasted_iota(jnp.int32, (L, HD), 1)
    cosb[...] = jnp.cos(angle)
    sn = jnp.sin(angle)
    sinb[...] = jnp.where(lane < HD // 2, -sn, sn)

    def to_ws(src, dst, t=slice(None)):
        cps = [net(src.at[t, :, at((r ^ k) * DR, DR)], dst.at[r, t, my_th, :], rows=r ^ k) for k in range(1, R)]
        return cps, local(src.at[t, :, at(r * DR, DR)], dst.at[r, t, my_th, :])

    def landed(cl):
        for k in cl[0]:
            k.wait_recv()
        cl[1].wait()

    cq.forward()
    cv = w_in(wv, wvf)
    lx.wait()
    xf = cols_forward(xblk, xz)
    lg.wait()
    for k in ga:
        k.wait_recv()
    a_g = to_ws(gtl, gw)
    ck.forward()
    cols_finish(xp, xf)

    def stats(v):
        mean = jnp.sum(v, 1, keepdims=True) / D
        sq = jnp.sum(v * v, 1, keepdims=True) / D
        return mean, lax.rsqrt(sq - mean * mean + EPS)

    for t in range(NT):
        def norm_rows(i, _, t=t):
            rows = at(i * 32, 32)
            v = xb[t, rows, :].astype(F32)
            mean, rstd = stats(v)
            h1[t, rows, :] = ((v - mean) * rstd).astype(BF)
            return 0

        lax.fori_loop(0, LH // 32, norm_rows, 0)

    cv.forward()
    co = Gather(net, R, r, lambda h: wo.at[half(HC, h), :], lambda j, h: wof.at[half(HC, h), at(j * DR, DR)])

    def wsblk(buf, t=slice(None)):
        return lambda j: buf.at[:, t, at(j * TH, TH), :]

    heads = HC // HD

    def rope(v):
        return jnp.concatenate(
            [v[:, h * HD:(h + 1) * HD] * cosb[...]
             + pltpu.roll(v[:, h * HD:(h + 1) * HD], HD // 2, 1) * sinb[...] for h in range(heads)], 1)

    def unrope(v):
        return v * cosb[...] + pltpu.roll(v * sinb[...], HD // 2, 1)

    def arrived(g):
        for k in range(1, R):
            g.wait(k)

    landed(a_g)
    g_z, g_p = cols_start(wsblk(gw))
    lws[0].wait()
    arrived(cq)
    qb[...] = rope(nn(h1[...].reshape(L, D), wqf[...])).astype(BF)
    lws[1].wait()
    arrived(ck)
    kb[...] = rope(nn(h1[...].reshape(L, D), wkf[...])).astype(BF)
    lws[2].wait()
    arrived(cv)
    vb[...] = nn(h1[...].reshape(L, D), wvf[...]).astype(BF)

    for h in range(heads):
        hs = slice(h * HD, (h + 1) * HD)
        s = nt(qb[:, hs], kb[:, hs]) * scale
        s = jnp.where(mskb[...] < 0.0, NEG, s)
        top = jnp.max(s, 1, keepdims=True)
        e = jnp.exp(s - top)
        tot = jnp.sum(e, 1, keepdims=True)
        lse[:, hs] = jnp.broadcast_to(top + jnp.log(tot), (L, HD))
        att[:, hs] = nn((e / tot).astype(BF), vb[:, hs]).astype(BF)

    co.forward()
    lws[3].wait()
    arrived(co)
    W1 = min(512, D)
    for n in range(D // W1):
        ns = slice(n * W1, (n + 1) * W1)
        val = nn(att[...], wof[:, ns])
        for j in range(C):
            for t in range(NT):
                p1[t, j % 2, j // 2, :, ns] = piece(val, j, t).astype(BF)

    def pre(p, pa):
        return net(p.at[1 - core], pa, cols=c ^ 1)

    def zsend(p, pa, ps, pr):
        out = []
        for m in range(1, Z):
            ps[m] = (p[core, z ^ m].astype(F32) + pa[z ^ m].astype(F32)).astype(BF)
            out.append(net(ps.at[m], pr.at[m], cols=c ^ (2 * m)))
        return out

    def zsum(p, pa, pr, cps):
        tot = p[core, z].astype(F32) + pa[z].astype(F32)
        for m in range(1, Z):
            cps[m - 1].wait_recv()
            tot = tot + pr[m].astype(F32)
        return tot

    k1 = [pre(p1.at[t], p1a.at[t]) for t in range(NT)]
    g_f = cols_forward(wsblk(gw), g_z)
    z1 = []
    for t in range(NT):
        k1[t].wait_recv()
        z1.append(zsend(p1.at[t], p1a.at[t], p1s.at[t], p1r.at[t]))
    cols_finish(g_p, g_f)
    lout = [local(gw, gw_out)]

    lff[0].wait()
    order = list(range(1, R))
    FC = wgv.shape[1]
    DN = 2
    DW = FC // DN

    def dhid_chunk(n):
        for k in order:
            dhs[k, :, n * DW:(n + 1) * DW] = nt(gw[r ^ k].reshape(L, DR), wdv[n * DW:(n + 1) * DW, :]).astype(BF)

    def dhid_send(n):
        ns = slice(n * DW, (n + 1) * DW)
        return Reduce(net, R, r, lambda k, h: dhs.at[k, half(L, h), ns], lambda k, h: dhr.at[k, half(L, h), ns])

    dhid_chunk(0)
    dh = [dhid_send(0)]
    for n in range(1, DN):
        dhid_chunk(n)

    xv = xb[:, my_th, :].reshape(TL, D).astype(F32)
    xm, xr_ = stats(xv)
    xtl[...] = (xv - xm) * xr_

    def second_norm(t):
        rows = slice(t * TH, (t + 1) * TH)
        v = xb[t, my_th, :].astype(F32) + zsum(p1.at[t], p1a.at[t], p1r.at[t], z1[t])
        x1[rows, :] = v
        mean2, rstd2 = stats(v)
        n2v = (v - mean2) * rstd2
        n2[rows, :] = n2v
        h2t[t] = n2v.astype(BF)
        return to_ws(h2t, h2w, t)

    h2_c = []
    for t in range(NT):
        a_2 = second_norm(t)
        if t == 0:
            for n in range(1, DN):
                dh.append(dhid_send(n))
            for n in range(DN):
                dho[:, n * DW:(n + 1) * DW] = nt(gw[r].reshape(L, DR), wdv[n * DW:(n + 1) * DW, :])
        else:
            dh[0].relay()
        landed(a_2)
        h2_c.append(cols_start(wsblk(h2w, t)))
    for d in dh[min(NT, 2) - 1:]:
        d.relay()
    a_h = to_ws(h1.at[:, my_th, :], h1w)
    lff[1].wait()
    lff[2].wait()

    QN = g["QN"]
    QW = FC // QN
    gu = []
    parts = [(t, q) for t in range(NT) for q in range(QN)]

    def gu_chunk(t, q):
        qs = slice(q * QW, (q + 1) * QW)
        for k in order[::-1] + [0]:
            ga_ = nn(h2w[r ^ k, t], wgv[:, qs])
            up_ = nn(h2w[r ^ k, t], wuv[:, qs])
            if k:
                gus[k, t, q, 0] = ga_.astype(BF)
                gus[k, t, q, 1] = up_.astype(BF)
            else:
                guo[t, q, 0] = ga_
                guo[t, q, 1] = up_
        gu.append(Reduce(net, R, r, lambda k, h: gus.at[k, t, q, :, half(LH, h), :],
                         lambda k, h: gur.at[k, t, q, :, half(LH, h), :]))

    for t, q in parts:
        if q == 0:
            cols_finish(h2_c[t][1], cols_forward(wsblk(h2w, t), h2_c[t][0]))
        gu_chunk(t, q)
        if len(gu) > 1:
            gu[-2].relay()
    gu[-1].relay()
    lout.append(local(h2w, h2w_out))
    landed(a_h)
    h_z, h_p = cols_start(wsblk(h1w))

    for d in dh:
        d.wait()
    dgt = []
    AR = 16
    for n, (t, q) in enumerate(parts):
        gu[n].wait()
        qs = slice(q * QW, (q + 1) * QW)

        def act(i, _, n=n, t=t, q=q, qs=qs):
            part = at(i * AR, AR)
            rows = at(t * LH + i * AR, AR)
            gate, up = guo[t, q, 0, part, :], guo[t, q, 1, part, :]
            dhid = dho[rows, qs]
            for k in gu[n].ks:
                gate = gate + gur[k, t, q, 0, part, :].astype(F32)
                up = up + gur[k, t, q, 1, part, :].astype(F32)
                dhid = dhid + dhr[k, rows, qs].astype(F32)
            sig = 1.0 / (1.0 + jnp.exp(-gate))
            silu = gate * sig
            hda[r, rows, qs] = (silu * up).astype(BF)
            dgu[0, r, rows, qs] = (dhid * up * sig * (1.0 + gate * (1.0 - sig))).astype(BF)
            dgu[1, r, rows, qs] = (dhid * silu).astype(BF)
            return 0
        lax.fori_loop(0, LH // AR, act, 0)

        def tok_half(h, t=t):
            return slice(t * LH + h * (LH // 2), t * LH + (h + 1) * (LH // 2))
        dgt.append(Gather(net, R, r, lambda h, qs=qs, f=tok_half: dgu.at[:, r, f(h), qs],
                          lambda j, h, qs=qs, f=tok_half: dgu.at[:, j, f(h), qs]))

    k2 = {}

    def dh2_block(k):
        s = r ^ k
        tot = nt(dgu[0, s], wgv[...]) + nt(dgu[1, s], wuv[...])
        for j in range(C):
            for t in range(NT):
                p2[j % 2, k, j // 2, t * TH:(t + 1) * TH] = piece(tot, j, t).astype(BF)
        k2[k] = net(p2.at[1 - core, k], p2a.at[k], cols=c ^ 1)

    dh2_block(0)
    z2 = {}
    for d in dgt:
        d.forward()

    def hid_send(n):
        ns = slice(n * DW, (n + 1) * DW)
        return Gather(net, R, r, lambda h: hda.at[r, half(L, h), ns], lambda j, h: hda.at[j, half(L, h), ns])

    hdc = [hid_send(0)]

    def z2_send(k):
        k2[k].wait_recv()
        for m in range(1, Z):
            p2s[k, m] = (p2[core, k, z ^ m].astype(F32) + p2a[k, z ^ m].astype(F32)).astype(BF)
            z2[k, m] = net(p2s.at[k, m], p2r.at[k, m], cols=c ^ (2 * m))

    for n, k in enumerate(order):
        for d in dgt:
            d.wait(k)
        dh2_block(k)
        z2_send(n)
    z2_send(R - 1)
    lout += [local(dgu.at[0], dg_out), local(dgu.at[1], du_out)]
    hdc[0].forward()

    a_d = []
    for k in range(R):
        tot = p2[core, k, z].astype(F32) + p2a[k, z].astype(F32)
        for m in range(1, Z):
            z2[k, m].wait_recv()
            tot = tot + p2r[k, m].astype(F32)
        dh2s[k] = tot.astype(BF)
        if k:
            a_d.append(net(dh2s.at[k], dh2t.at[:, at(r * DR, DR)], rows=r ^ k))
        else:
            l_d = local(dh2s.at[0], dh2t.at[:, at(r * DR, DR)])
    hdc += [hid_send(n) for n in range(1, DN)]
    l_d.wait()
    for k in a_d:
        k.wait_recv()

    def norm_back(grad, normed, rstd):
        a = jnp.sum(grad, 1, keepdims=True) / D
        b = jnp.sum(grad * normed, 1, keepdims=True) / D
        return rstd * (grad - a - normed * b)

    _, rstd2b = stats(x1[...])
    dxv = gtl[...].reshape(TL, D).astype(F32) + norm_back(dh2t[...].astype(F32), n2[...], rstd2b)
    dxt[...] = dxv
    dmt[...] = dxv.astype(BF).reshape(NT, TH, D)
    l_m = local(dmt, dmix.at[:, my_th, :])

    def dblk(j):
        return dmix.at[:, at(j * TH, TH), :]
    m_z = [net(dmt, dblk(c), cols=c ^ (2 * m)) for m in range(1, Z)]
    m_p = net(dmt, dblk(c), cols=c ^ 1)

    def ffn_block(k):
        s = r ^ k
        tot = nn(hda[s], wdv[...])
        for j in range(C):
            for t in range(NT):
                p3[j % 2, j // 2, k, t * TH:(t + 1) * TH] = piece(tot, j, t).astype(BF)

    ffn_block(0)
    h_f = cols_forward(wsblk(h1w), h_z)
    for d in hdc[1:]:
        d.forward()
    for k in order:
        for d in hdc:
            d.wait(k)
        ffn_block(k)
    k3 = pre(p3, p3a)
    cols_finish(h_p, h_f)
    lout += [local(hda, hd_out), local(h1w, h1w_out)]
    k3.wait_recv()
    m_f = cols_forward(dblk, m_z)
    z3 = zsend(p3, p3a, p3s, p3r)
    l_m.wait()
    cols_finish(m_p, m_f)

    for k in order:
        gop[k] = tn(att[...], dmix[:, :, at((r ^ k) * DR, DR)].reshape(L, DR)).astype(BF)
    cgo = Reduce(net, R, r, lambda k, h: gop.at[k, half(HC, h), :], lambda k, h: gor.at[k, half(HC, h), :])
    da = nt(dmix[...].reshape(L, D), wof[...]).astype(BF)
    for h in range(heads):
        hs = slice(h * HD, (h + 1) * HD)
        s = nt(qb[:, hs], kb[:, hs]) * scale
        s = jnp.where(mskb[...] < 0.0, NEG, s)
        pr = jnp.exp(s - lse[:, h * HD:h * HD + 1])
        dp = nt(da[:, hs], vb[:, hs])
        inner = jnp.sum(pr * dp, 1, keepdims=True)
        ds = (pr * (dp - inner)).astype(BF)
        dqkv[0, r, :, hs] = unrope(nn(ds, kb[:, hs]) * scale).astype(BF)
        dqkv[1, r, :, hs] = unrope(tn(ds, qb[:, hs]) * scale).astype(BF)
        dqkv[2, r, :, hs] = tn(pr.astype(BF), da[:, hs]).astype(BF)
    cd = Gather(net, R, r, lambda h: dqkv.at[:, r, half(L, h), :], lambda j, h: dqkv.at[:, j, half(L, h), :])

    for n in range(D // W1):
        ns = slice(n * W1, (n + 1) * W1)
        val = (nt(dqkv[0, r], wqf[ns, :]) + nt(dqkv[1, r], wkf[ns, :]) + nt(dqkv[2, r], wvf[ns, :]))
        for j in range(C):
            for t in range(NT):
                p4[t, j % 2, j // 2, :, ns] = piece(val, j, t).astype(BF)
    k4 = [pre(p4.at[t], p4a.at[t]) for t in range(NT)]
    z4 = []
    for t in range(NT):
        k4[t].wait_recv()
        z4.append(zsend(p4.at[t], p4a.at[t], p4s.at[t], p4r.at[t]))
    gof[...] = tn(att[...], dmix[:, :, at(r * DR, DR)].reshape(L, DR))
    cgo.relay()

    fs[...] = zsum(p3, p3a, p3r, z3).astype(BF)
    a_f = [net(fs.at[k], ft.at[:, at(r * DR, DR)], rows=r ^ k) for k in order]
    l_f = local(fs.at[0], ft.at[:, at(r * DR, DR)])
    cd.forward()

    def to_io(src, dst, t=slice(None)):
        cps = [net(src.at[t, :, at((c ^ k) * DC, DC)], dst.at[t, my_th, :], cols=c ^ k) for k in range(1, C)]
        return cps, local(src.at[t, :, at(c * DC, DC)], dst.at[t, my_th, :])

    l_f.wait()
    for k in a_f:
        k.wait_recv()
    lot[...] = (x1[...] + ft[...].astype(F32)).astype(BF).reshape(NT, TH, D)
    i_o = to_io(lot, lob)
    i_g = []
    for t in range(NT):
        rows = slice(t * TH, (t + 1) * TH)
        _, rstd1 = stats(xb[t, my_th, :].astype(F32))
        dh1 = zsum(p4.at[t], p4a.at[t], p4r.at[t], z4[t])
        git[t] = (dxt[rows, :] + norm_back(dh1, xtl[rows, :], rstd1)).astype(BF)
        i_g.append(to_io(git, gib, t))
    landed(i_o)
    lout.append(local(lob, o_out))
    for k in i_g:
        landed(k)
    gif[...] = gib[...].astype(F32)
    lout.append(local(gif, gi_out))
    arrived(cd)
    lout += [local(dqkv.at[0], dq_out), local(dqkv.at[1], dk_out), local(dqkv.at[2], dv_out)]
    cgo.wait()
    gsum = gof[...]
    for k in cgo.ks:
        gsum = gsum + gor[k].astype(F32)
    gof[...] = gsum
    lout.append(local(gof, go_out))
    net.drain()
    for k in lout:
        k.wait()


def body(R, C, tokens, segments, w_query, w_key, w_value, w_out, w_gate, w_up, w_down, cotangent):
    L, DC = tokens.shape
    DR, HC = w_query.shape
    D = DR * R
    FC = w_gate.shape[1]
    TL = L // C
    Z = C // 2
    NT = 2 if TL % 32 == 0 else 1
    LH, TH = L // NT, TL // NT
    QN = 4 // NT if FC % 1024 == 0 else 2
    QW = FC // QN
    g = dict(R=R, C=C, L=L, TL=TL, D=D, DR=DR, DC=DC, HC=HC, NT=NT, QN=QN)
    half = HD // 2
    fr = (BASE ** (-(np.arange(half, dtype=np.float32) * np.float32(2.0)) / np.float32(HD))).astype(np.float32)
    freq = jnp.asarray(np.concatenate([fr, fr])[None, :])
    S = jax.ShapeDtypeStruct
    V = pltpu.VMEM
    outs = [
        S((NT, LH, DC), BF), S((NT, LH, DC), F32), *[S((R, NT, LH, DR), BF)] * 3,
        S((R, L, FC), BF), S((R, L, FC), BF), S((R, L, FC), BF),
        S((R, L, HC), BF), S((R, L, HC), BF), S((R, L, HC), BF), S((HC, DR), F32),
    ]
    seq = lambda w: [V((NT, 2, Z, TH, w), BF)] + [V((NT, Z, TH, w), BF)] * 3
    seq4 = lambda: [V((2, Z, R, TL, DR), BF), V((Z, R, TL, DR), BF), V((Z, R, TL, DR), BF), V((Z, R, TL, DR), BF)]
    seq2 = lambda: [V((2, R, Z, TL, DR), BF), V((R, Z, TL, DR), BF), V((R, Z, TL, DR), BF), V((R, Z, TL, DR), BF)]
    scratch = [
        V((NT, LH, D), BF), V((NT, LH, D), BF), V((TL, D), F32), V((NT, TH, D), BF),
        *[V((R, NT, LH, DR), BF)] * 3, V((NT, TH, D), BF),
        V((D, HC), BF), V((D, HC), BF), V((D, HC), BF), V((HC, D), BF),
        V((DR, FC), BF), V((DR, FC), BF), V((FC, DR), BF),
        *seq(D), *seq2(), *seq4(), *seq(D),
        V((TL, D), F32), V((TL, D), F32),
        V((R, L, FC), BF), V((R, L, FC), BF), V((L, FC), F32),
        V((R, NT, QN, 2, LH, QW), BF), V((R, NT, QN, 2, LH, QW), BF), V((NT, QN, 2, LH, QW), F32),
        V((R, L, FC), BF), V((2, R, L, FC), BF),
        V((R, TL, DR), BF), V((TL, D), BF), V((TL, D), F32), V((NT, TH, D), BF), V((NT, LH, D), BF),
        V((L, HC), BF), V((L, HC), BF), V((L, HC), BF), V((L, HC), BF), V((L, HC), F32),
        V((L, HD), F32), V((L, HD), F32), V((L, L), F32),
        V((3, R, L, HC), BF), V((R, HC, DR), BF), V((R, HC, DR), BF), V((HC, DR), F32),
        V((R, TL, DR), BF), V((TL, D), BF), V((NT, TH, D), BF), V((NT, TH, D), BF),
        V((NT, LH, DC), BF), V((NT, LH, DC), BF), V((NT, LH, DC), F32),
        V((1, L), jnp.int32), V((1, HD), F32),
        pltpu.SemaphoreType.DMA((g_sems(R, C, NT * QN),)), pltpu.SemaphoreType.DMA((g_sems(R, C, NT * QN),)),
        pltpu.SemaphoreType.DMA((48,)),
    ]
    A = pl.BlockSpec(memory_space=pl.ANY)
    res = pl.pallas_call(
        functools.partial(step_kernel, g),
        out_shape=outs,
        in_specs=[A] * 11,
        out_specs=[A] * len(outs),
        scratch_shapes=scratch,
        compiler_params=pltpu.CompilerParams(
            collective_id=0, has_side_effects=True, vmem_limit_bytes=67043328),
        name="layer_step",
    )(tokens.reshape(NT, LH, DC), cotangent.reshape(NT, LH, DC), segments, freq, w_query, w_key, w_value, w_out, w_gate, w_up, w_down)
    layer_out, grad_in, h1w, gw, h2w, dg, du, hd, dq, dk, dv, go = res
    T = R * L
    h1w, gw, h2w = (t.reshape(T, DR) for t in (h1w, gw, h2w))
    gq, gk, gv = (tn(h1w, t.reshape(T, HC)) for t in (dq, dk, dv))
    ggate, gup, gdown = tn(h2w, dg.reshape(T, FC)), tn(h2w, du.reshape(T, FC)), tn(hd.reshape(T, FC), gw)
    return layer_out.reshape(L, DC), grad_in.reshape(L, DC), gq, gk, gv, go, ggate, gup, gdown


def g_sems(R, C, n):
    return 2 * (R - 1) * (8 + n) + 2 * R * (3 + n) + 8 * (R - 1) + 16 * C + (R + 4) * C // 2


def solution(mesh):
    R, C = mesh.shape["rows"], mesh.shape["cols"]
    rc, cr = P("rows", "cols"), P("cols", "rows")
    in_specs = (rc, P("rows", None), rc, rc, rc, cr, rc, rc, cr, rc)
    out_specs = (rc, rc, rc, rc, rc, cr, rc, rc, cr)
    return jax.shard_map(functools.partial(body, R, C), mesh=mesh, in_specs=in_specs,
                         out_specs=out_specs, check_vma=False)
```

```python
import functools
import jax
import jax.numpy as jnp
import numpy as np
from jax import lax
from jax.experimental import pallas as pl
from jax.experimental.pallas import tpu as pltpu
from jax.sharding import PartitionSpec as P

HD = 128
EPS = 1e-05
NEG = -1e30
BASE = 10000.0
F32 = jnp.float32
BF = jnp.bfloat16
MESH = pl.DeviceIdType.MESH


def nn(a, b):
    return jnp.dot(a, b, preferred_element_type=F32)


def nt(a, b):
    return lax.dot_general(a, b, (((1,), (1,)), ((), ())), preferred_element_type=F32)


def tn(a, b):
    return lax.dot_general(a, b, (((0,), (0,)), ((), ())), preferred_element_type=F32)


def at(start, size, step=None):
    return pl.ds(pl.multiple_of(start, step or size), size)


class Net:
    def __init__(self, send, recv):
        self.send, self.recv, self.all = send, recv, []

    def make(self, src, dst, i, j, peer):
        return pltpu.make_async_remote_copy(
            src_ref=src, dst_ref=dst, send_sem=self.send.at[i], recv_sem=self.recv.at[j],
            device_id=peer, device_id_type=MESH)

    def slot(self):
        assert len(self.all) < self.send.shape[0]
        self.all.append(None)
        return len(self.all) - 1

    def __call__(self, src, dst, **peer):
        i = self.slot()
        c = self.make(src, dst, i, i, peer)
        c.start()
        self.all[i] = Copy(c)
        return self.all[i]

    def only(self, pred, src, dst, land=None, **peer):
        i = self.slot()
        c = self.make(src, dst, i, i if land is None else land.i, peer)

        @pl.when(pred)
        def _():
            c.start()

        self.all[i] = Copy(c, pred, i)
        return self.all[i]

    def drain(self):
        for c in self.all:
            if c is None:
                continue
            if c.pred is None:
                c.c.wait_send()
            else:
                pl.when(c.pred)(c.c.wait_send)


class Copy:
    def __init__(self, c, pred=None, i=None):
        self.c, self.open, self.pred, self.i = c, True, pred, i

    def wait_recv(self):
        if self.open:
            self.c.wait_recv()
        self.open = False


class Gather:
    def __init__(self, net, R, r, own, blk):
        self.net, self.r, self.two, self.blk, self.c = net, r, R == 4, blk, {}
        todo = [(1, 0), (2, 1), (1, 1), (2, 0)] if self.two else [(k, h) for k in range(1, R) for h in range(2)]
        for k, h in todo:
            self.c[k, h] = net(own(h), blk(r, h), rows=r ^ k)

    def forward(self):
        if self.two:
            for k, h in ((1, 0), (2, 1)):
                self.c[k, h].wait_recv()
                b = self.blk(self.r ^ k, h)
                self.c[3, h] = self.net(b, b, rows=self.r ^ (3 - k))

    def wait(self, k):
        for h in range(2):
            self.c[k, h].wait_recv()


class Reduce:
    def __init__(self, net, R, r, snd, rcv):
        self.net, self.r, self.two, self.snd, self.rcv, self.c = net, r, R == 4, snd, rcv, {}
        self.ks = (1, 2) if self.two else tuple(range(1, R))
        if self.two:
            for k, h in ((1, 0), (2, 1)):
                self.c[3, h] = net(snd(3, h), rcv(3, h), rows=r ^ k)
            for k, h in ((1, 0), (2, 1)):
                self.c[k, h] = net(snd(k, h), rcv(k, h), rows=r ^ k)
        else:
            for k in self.ks:
                for h in range(2):
                    self.c[k, h] = net(snd(k, h), rcv(k, h), rows=r ^ k)

    def relay(self):
        if self.two:
            for k, h in ((2, 0), (1, 1)):
                self.c[3, h].wait_recv()
                a = self.snd(k, h)
                a[...] = (a[...].astype(F32) + self.rcv(3, h)[...].astype(F32)).astype(BF)
                self.c[k, h] = self.net(a, self.rcv(k, h), rows=self.r ^ k)

    def wait(self):
        for k in self.ks:
            for h in range(2):
                self.c[k, h].wait_recv()


class LCopy:
    def __init__(self, c):
        self.c, self.open = c, True

    def wait(self):
        if self.open:
            self.c.wait()
        self.open = False


class Local:
    def __init__(self, sem):
        self.sem, self.n, self.all = sem, 0, []

    def __call__(self, src, dst):
        c = pltpu.make_async_copy(src, dst, self.sem.at[self.n])
        self.n += 1
        c.start()
        self.all.append(LCopy(c))
        return self.all[-1]


def step_kernel(g, *refs):
    (tok, cot, seg_in, freq_in, wq, wk, wv, wo, wg, wu, wd,
     o_out, gi_out, h1w_out, gw_out, h2w_out, dg_out, du_out, hd_out, dq_out, dk_out, dv_out, go_out,
     xb, h1, xtl, gtl, h1w, gw, h2w, h2t, wqf, wkf, wvf, wof, wgv, wuv, wdv,
     p1, p1a, p1s, p1r, p2, p2a, p2s, p2r, p3, p3a, p3s, p3r, p4, p4a, p4s, p4r,
     x1, n2, dhs, dhr, dho, gus, gur, guo, hda, dgu, dh2s, dh2t, dxt, dmt, dmix,
     qb, kb, vb, att, lse, cosb, sinb, mskb, dqkv, gop, gor, gof, fs, ft, lot, git, lob, gib, gif, segr, freq,
     send, recv, loc) = refs
    R, C, L, TL, D, DR, DC, HC, NT = (g[k] for k in ("R", "C", "L", "TL", "D", "DR", "DC", "HC", "NT"))
    LH, TH = L // NT, TL // NT
    Z = C // 2
    r = lax.axis_index("rows")
    c = lax.axis_index("cols")
    z = c // 2
    core = c % 2
    net = Net(send, recv)
    local = Local(loc)
    scale = HD ** (-0.5)
    my_th = at(c * TH, TH)

    def piece(val, j, t):
        return val[t * LH + j * TH:t * LH + (j + 1) * TH, :]

    bar = pltpu.get_barrier_semaphore()
    for k in range(1, R):
        pl.semaphore_signal(bar, inc=1, device_id={"rows": r ^ k}, device_id_type=MESH)
    for k in range(1, C):
        pl.semaphore_signal(bar, inc=1, device_id={"cols": c ^ k}, device_id_type=MESH)

    lsm = [local(seg_in, segr), local(freq_in, freq)]
    lx = local(tok, xb.at[:, :, at(c * DC, DC)])
    lg = local(cot.at[:, my_th, :], gtl.at[:, :, at(c * DC, DC)])
    lws = [local(wq, wqf.at[at(r * DR, DR), :]), local(wk, wkf.at[at(r * DR, DR), :]),
           local(wv, wvf.at[at(r * DR, DR), :]), local(wo, wof.at[:, at(r * DR, DR)])]
    lff = [local(wd, wdv), local(wg, wgv), local(wu, wuv)]

    pl.semaphore_wait(bar, R + C - 2)

    def half(n, h):
        return slice(h * (n // 2), (h + 1) * (n // 2))

    def w_in(w, full):
        n = DR // 2
        return Gather(net, R, r, lambda h: w.at[half(DR, h), :], lambda j, h: full.at[at(j * DR + h * n, n), :])

    def cols_start(blk):
        zs = [net(blk(c), blk(c), cols=c ^ (2 * m)) for m in range(1, Z)]
        return zs, net(blk(c), blk(c), cols=c ^ 1)

    def cols_forward(blk, zs):
        fw = []
        for m in range(1, Z):
            zs[m - 1].wait_recv()
            fw.append(net(blk(c ^ (2 * m)), blk(c ^ (2 * m)), cols=c ^ 1))
        return fw

    line = Z == 4
    mid = ((z + 1) // 2) % 2

    def line_start(blk):
        b = blk(c)
        z2 = net(b, b, cols=c ^ 4)
        z3 = net.only(mid == 1, b, b, cols=c ^ 6)
        return [net(b, b, cols=c ^ 2), z2, z3], net(b, b, cols=c ^ 1)

    def line_relay(blk, zs):
        zs[1].wait_recv()
        b = blk(c ^ 4)
        net.only(mid == 1, b, b, zs[2], cols=c ^ 2)

    def line_forward(blk, zs):
        fw = []
        for m in (2, 1, 3):
            zs[m - 1].wait_recv()
            fw.append(net(blk(c ^ (2 * m)), blk(c ^ (2 * m)), cols=c ^ 1))
        return fw

    def cols_finish(own, fw):
        own.wait_recv()
        for f in fw:
            f.wait_recv()

    def xblk(j):
        return xb.at[:, :, at(j * DC, DC)]

    cq = w_in(wq, wqf)
    xz = [net(tok, xblk(c), cols=c ^ (2 * m)) for m in range(1, Z)]
    xp = net(tok, xblk(c), cols=c ^ 1)
    ga = [net(cot.at[:, at((c ^ k) * TH, TH), :], gtl.at[:, :, at(c * DC, DC)], cols=c ^ k) for k in range(1, C)]
    ck = w_in(wk, wkf)

    for k in lsm:
        k.wait()
    sr = jnp.broadcast_to(segr[...].astype(F32), (L, L))
    sc = sr.T
    qi = lax.broadcasted_iota(jnp.int32, (L, L), 0)
    ki = lax.broadcasted_iota(jnp.int32, (L, L), 1)
    ok = (sr == sc) & (qi >= ki)
    okf = jnp.where(ok, 1.0, 0.0)
    mskb[...] = jnp.where(ok, 0.0, NEG)
    pos = jnp.sum(okf, 1, keepdims=True) - 1.0
    angle = pos * freq[...]
    lane = lax.broadcasted_iota(jnp.int32, (L, HD), 1)
    cosb[...] = jnp.cos(angle)
    sn = jnp.sin(angle)
    sinb[...] = jnp.where(lane < HD // 2, -sn, sn)

    def to_ws(src, dst, t=slice(None)):
        cps = [net(src.at[t, :, at((r ^ k) * DR, DR)], dst.at[r, t, my_th, :], rows=r ^ k) for k in range(1, R)]
        return cps, local(src.at[t, :, at(r * DR, DR)], dst.at[r, t, my_th, :])

    def landed(cl):
        for k in cl[0]:
            k.wait_recv()
        cl[1].wait()

    cq.forward()
    cv = w_in(wv, wvf)
    lx.wait()
    xf = cols_forward(xblk, xz)
    lg.wait()
    for k in ga:
        k.wait_recv()
    a_g = to_ws(gtl, gw)
    ck.forward()
    cols_finish(xp, xf)

    def stats(v):
        mean = jnp.sum(v, 1, keepdims=True) / D
        sq = jnp.sum(v * v, 1, keepdims=True) / D
        return mean, lax.rsqrt(sq - mean * mean + EPS)

    for t in range(NT):
        def norm_rows(i, _, t=t):
            rows = at(i * 32, 32)
            v = xb[t, rows, :].astype(F32)
            mean, rstd = stats(v)
            h1[t, rows, :] = ((v - mean) * rstd).astype(BF)
            return 0

        lax.fori_loop(0, LH // 32, norm_rows, 0)

    cv.forward()
    co = Gather(net, R, r, lambda h: wo.at[half(HC, h), :], lambda j, h: wof.at[half(HC, h), at(j * DR, DR)])

    def wsblk(buf, t=slice(None)):
        return lambda j: buf.at[:, t, at(j * TH, TH), :]

    heads = HC // HD

    def rope(v):
        return jnp.concatenate(
            [v[:, h * HD:(h + 1) * HD] * cosb[...]
             + pltpu.roll(v[:, h * HD:(h + 1) * HD], HD // 2, 1) * sinb[...] for h in range(heads)], 1)

    def unrope(v):
        return v * cosb[...] + pltpu.roll(v * sinb[...], HD // 2, 1)

    def arrived(g):
        for k in range(1, R):
            g.wait(k)

    landed(a_g)
    g_z, g_p = cols_start(wsblk(gw))
    lws[0].wait()
    arrived(cq)
    qb[...] = rope(nn(h1[...].reshape(L, D), wqf[...])).astype(BF)
    lws[1].wait()
    arrived(ck)
    kb[...] = rope(nn(h1[...].reshape(L, D), wkf[...])).astype(BF)
    lws[2].wait()
    arrived(cv)
    vb[...] = nn(h1[...].reshape(L, D), wvf[...]).astype(BF)

    for h in range(heads):
        hs = slice(h * HD, (h + 1) * HD)
        s = nt(qb[:, hs], kb[:, hs]) * scale
        s = jnp.where(mskb[...] < 0.0, NEG, s)
        top = jnp.max(s, 1, keepdims=True)
        e = jnp.exp(s - top)
        tot = jnp.sum(e, 1, keepdims=True)
        lse[:, hs] = jnp.broadcast_to(top + jnp.log(tot), (L, HD))
        att[:, hs] = nn((e / tot).astype(BF), vb[:, hs]).astype(BF)

    co.forward()
    lws[3].wait()
    arrived(co)
    W1 = min(512, D)
    for n in range(D // W1):
        ns = slice(n * W1, (n + 1) * W1)
        val = nn(att[...], wof[:, ns])
        for j in range(C):
            for t in range(NT):
                p1[t, j % 2, j // 2, :, ns] = piece(val, j, t).astype(BF)

    def pre(p, pa):
        return net(p.at[1 - core], pa, cols=c ^ 1)

    def zsend(p, pa, ps, pr):
        out = []
        for m in range(1, Z):
            ps[m] = (p[core, z ^ m].astype(F32) + pa[z ^ m].astype(F32)).astype(BF)
            out.append(net(ps.at[m], pr.at[m], cols=c ^ (2 * m)))
        return out

    class Line:
        def __init__(self, p, pa, ps, pr):
            self.ps, self.pr = ps, pr
            for m in (3, 1, 2):
                ps[m] = (p[core, z ^ m].astype(F32) + pa[z ^ m].astype(F32)).astype(BF)
                if m == 3:
                    self.i, self.j = net.slot(), net.slot()
                    far = net.make(ps.at[3], pr.at[3 * mid], self.i, self.j + mid * (self.i - self.j),
                                   {"cols": c ^ (2 + 4 * mid)})
                    far.start()
                    net.all[self.i] = Copy(far)
                if m == 1:
                    self.c1 = net(ps.at[1], pr.at[1], cols=c ^ 2)

            @pl.when(mid == 0)
            def _():
                pr[3] = jnp.zeros(pr.shape[1:], BF)

        def relay(self):
            ps, pr = self.ps, self.pr

            @pl.when(mid == 1)
            def _():
                net.make(ps.at[3], pr.at[0], self.i, self.j, {"cols": c ^ 2}).wait_recv()
                ps[2] = (ps[2].astype(F32) + pr[0].astype(F32)).astype(BF)

            self.c2 = net(ps.at[2], pr.at[2], cols=c ^ 4)

        def total(self, p, pa):
            ps, pr = self.ps, self.pr
            self.c1.wait_recv()
            self.c2.wait_recv()

            @pl.when(mid == 1)
            def _():
                net.make(ps.at[3], pr.at[3], self.i, self.i, {"cols": c ^ 6}).wait_recv()

            return (p[core, z].astype(F32) + pa[z].astype(F32) + pr[1].astype(F32) + pr[2].astype(F32)
                    + pr[3].astype(F32))

    def line_send(p, pa, ps, pr):
        return Line(p, pa, ps, pr) if line else zsend(p, pa, ps, pr)

    def zsum(p, pa, pr, cps):
        if isinstance(cps, Line):
            return cps.total(p, pa)
        tot = p[core, z].astype(F32) + pa[z].astype(F32)
        for m in range(1, Z):
            cps[m - 1].wait_recv()
            tot = tot + pr[m].astype(F32)
        return tot

    k1 = [pre(p1.at[t], p1a.at[t]) for t in range(NT)]
    g_f = cols_forward(wsblk(gw), g_z)
    z1 = []
    for t in range(NT):
        k1[t].wait_recv()
        z1.append(zsend(p1.at[t], p1a.at[t], p1s.at[t], p1r.at[t]))
    cols_finish(g_p, g_f)
    lout = [local(gw, gw_out)]

    lff[0].wait()
    order = list(range(1, R))
    FC = wgv.shape[1]
    DN = 2
    DW = FC // DN

    def dhid_chunk(n):
        for k in order:
            dhs[k, :, n * DW:(n + 1) * DW] = nt(gw[r ^ k].reshape(L, DR), wdv[n * DW:(n + 1) * DW, :]).astype(BF)

    def dhid_send(n):
        ns = slice(n * DW, (n + 1) * DW)
        return Reduce(net, R, r, lambda k, h: dhs.at[k, half(L, h), ns], lambda k, h: dhr.at[k, half(L, h), ns])

    dhid_chunk(0)
    dh = [dhid_send(0)]
    for n in range(1, DN):
        dhid_chunk(n)

    xv = xb[:, my_th, :].reshape(TL, D).astype(F32)
    xm, xr_ = stats(xv)
    xtl[...] = (xv - xm) * xr_

    def second_norm(t):
        rows = slice(t * TH, (t + 1) * TH)
        v = xb[t, my_th, :].astype(F32) + zsum(p1.at[t], p1a.at[t], p1r.at[t], z1[t])
        x1[rows, :] = v
        mean2, rstd2 = stats(v)
        n2v = (v - mean2) * rstd2
        n2[rows, :] = n2v
        h2t[t] = n2v.astype(BF)
        return to_ws(h2t, h2w, t)

    h2_c = []
    for t in range(NT):
        a_2 = second_norm(t)
        if t == 0:
            for n in range(1, DN):
                dh.append(dhid_send(n))
            for n in range(DN):
                dho[:, n * DW:(n + 1) * DW] = nt(gw[r].reshape(L, DR), wdv[n * DW:(n + 1) * DW, :])
        else:
            dh[0].relay()
        landed(a_2)
        h2_c.append(cols_start(wsblk(h2w, t)))
    for d in dh[min(NT, 2) - 1:]:
        d.relay()
    a_h = to_ws(h1.at[:, my_th, :], h1w)
    lff[1].wait()
    lff[2].wait()

    QN = g["QN"]
    QW = FC // QN
    gu = []
    parts = [(t, q) for t in range(NT) for q in range(QN)]

    def gu_chunk(t, q):
        qs = slice(q * QW, (q + 1) * QW)
        for k in order[::-1] + [0]:
            ga_ = nn(h2w[r ^ k, t], wgv[:, qs])
            up_ = nn(h2w[r ^ k, t], wuv[:, qs])
            if k:
                gus[k, t, q, 0] = ga_.astype(BF)
                gus[k, t, q, 1] = up_.astype(BF)
            else:
                guo[t, q, 0] = ga_
                guo[t, q, 1] = up_
        gu.append(Reduce(net, R, r, lambda k, h: gus.at[k, t, q, :, half(LH, h), :],
                         lambda k, h: gur.at[k, t, q, :, half(LH, h), :]))

    for t, q in parts:
        if q == 0:
            cols_finish(h2_c[t][1], cols_forward(wsblk(h2w, t), h2_c[t][0]))
        gu_chunk(t, q)
        if len(gu) > 1:
            gu[-2].relay()
    gu[-1].relay()
    lout.append(local(h2w, h2w_out))
    landed(a_h)
    h_z, h_p = cols_start(wsblk(h1w))

    for d in dh:
        d.wait()
    dgt = []
    AR = 16
    for n, (t, q) in enumerate(parts):
        gu[n].wait()
        qs = slice(q * QW, (q + 1) * QW)

        def act(i, _, n=n, t=t, q=q, qs=qs):
            part = at(i * AR, AR)
            rows = at(t * LH + i * AR, AR)
            gate, up = guo[t, q, 0, part, :], guo[t, q, 1, part, :]
            dhid = dho[rows, qs]
            for k in gu[n].ks:
                gate = gate + gur[k, t, q, 0, part, :].astype(F32)
                up = up + gur[k, t, q, 1, part, :].astype(F32)
                dhid = dhid + dhr[k, rows, qs].astype(F32)
            sig = 1.0 / (1.0 + jnp.exp(-gate))
            silu = gate * sig
            hda[r, rows, qs] = (silu * up).astype(BF)
            dgu[0, r, rows, qs] = (dhid * up * sig * (1.0 + gate * (1.0 - sig))).astype(BF)
            dgu[1, r, rows, qs] = (dhid * silu).astype(BF)
            return 0
        lax.fori_loop(0, LH // AR, act, 0)

        def tok_half(h, t=t):
            return slice(t * LH + h * (LH // 2), t * LH + (h + 1) * (LH // 2))
        dgt.append(Gather(net, R, r, lambda h, qs=qs, f=tok_half: dgu.at[:, r, f(h), qs],
                          lambda j, h, qs=qs, f=tok_half: dgu.at[:, j, f(h), qs]))

    k2 = {}

    def dh2_block(k):
        s = r ^ k
        tot = nt(dgu[0, s], wgv[...]) + nt(dgu[1, s], wuv[...])
        for j in range(C):
            for t in range(NT):
                p2[j % 2, k, j // 2, t * TH:(t + 1) * TH] = piece(tot, j, t).astype(BF)
        k2[k] = net(p2.at[1 - core, k], p2a.at[k], cols=c ^ 1)

    dh2_block(0)
    z2 = {}
    for d in dgt:
        d.forward()

    def hid_send(n):
        ns = slice(n * DW, (n + 1) * DW)
        return Gather(net, R, r, lambda h: hda.at[r, half(L, h), ns], lambda j, h: hda.at[j, half(L, h), ns])

    hdc = [hid_send(0)]

    def z2_send(k):
        k2[k].wait_recv()
        for m in range(1, Z):
            p2s[k, m] = (p2[core, k, z ^ m].astype(F32) + p2a[k, z ^ m].astype(F32)).astype(BF)
            z2[k, m] = net(p2s.at[k, m], p2r.at[k, m], cols=c ^ (2 * m))

    for n, k in enumerate(order):
        for d in dgt:
            d.wait(k)
        dh2_block(k)
        z2_send(n)
    z2_send(R - 1)
    lout += [local(dgu.at[0], dg_out), local(dgu.at[1], du_out)]
    hdc[0].forward()

    a_d = []
    for k in range(R):
        tot = p2[core, k, z].astype(F32) + p2a[k, z].astype(F32)
        for m in range(1, Z):
            z2[k, m].wait_recv()
            tot = tot + p2r[k, m].astype(F32)
        dh2s[k] = tot.astype(BF)
        if k:
            a_d.append(net(dh2s.at[k], dh2t.at[:, at(r * DR, DR)], rows=r ^ k))
        else:
            l_d = local(dh2s.at[0], dh2t.at[:, at(r * DR, DR)])
    hdc += [hid_send(n) for n in range(1, DN)]
    l_d.wait()
    for k in a_d:
        k.wait_recv()

    def norm_back(grad, normed, rstd):
        a = jnp.sum(grad, 1, keepdims=True) / D
        b = jnp.sum(grad * normed, 1, keepdims=True) / D
        return rstd * (grad - a - normed * b)

    _, rstd2b = stats(x1[...])
    dxv = gtl[...].reshape(TL, D).astype(F32) + norm_back(dh2t[...].astype(F32), n2[...], rstd2b)
    dxt[...] = dxv
    dmt[...] = dxv.astype(BF).reshape(NT, TH, D)
    l_m = local(dmt, dmix.at[:, my_th, :])

    def dblk(j):
        return dmix.at[:, at(j * TH, TH), :]
    l_m.wait()
    m_z, m_p = line_start(dblk) if line else cols_start(dblk)

    def ffn_block(k):
        s = r ^ k
        tot = nn(hda[s], wdv[...])
        for j in range(C):
            for t in range(NT):
                p3[j % 2, j // 2, k, t * TH:(t + 1) * TH] = piece(tot, j, t).astype(BF)

    ffn_block(0)
    h_f = cols_forward(wsblk(h1w), h_z)
    for d in hdc[1:]:
        d.forward()
    if line:
        line_relay(dblk, m_z)
    for k in order:
        for d in hdc:
            d.wait(k)
        ffn_block(k)
    k3 = pre(p3, p3a)
    cols_finish(h_p, h_f)
    lout += [local(hda, hd_out), local(h1w, h1w_out)]
    k3.wait_recv()
    m_f = line_forward(dblk, m_z) if line else cols_forward(dblk, m_z)
    z3 = line_send(p3, p3a, p3s, p3r)
    cols_finish(m_p, m_f)

    for k in order:
        gop[k] = tn(att[...], dmix[:, :, at((r ^ k) * DR, DR)].reshape(L, DR)).astype(BF)
    cgo = Reduce(net, R, r, lambda k, h: gop.at[k, half(HC, h), :], lambda k, h: gor.at[k, half(HC, h), :])
    da = nt(dmix[...].reshape(L, D), wof[...]).astype(BF)
    for h in range(heads):
        hs = slice(h * HD, (h + 1) * HD)
        s = nt(qb[:, hs], kb[:, hs]) * scale
        s = jnp.where(mskb[...] < 0.0, NEG, s)
        pr = jnp.exp(s - lse[:, h * HD:h * HD + 1])
        dp = nt(da[:, hs], vb[:, hs])
        inner = jnp.sum(pr * dp, 1, keepdims=True)
        ds = (pr * (dp - inner)).astype(BF)
        dqkv[0, r, :, hs] = unrope(nn(ds, kb[:, hs]) * scale).astype(BF)
        dqkv[1, r, :, hs] = unrope(tn(ds, qb[:, hs]) * scale).astype(BF)
        dqkv[2, r, :, hs] = tn(pr.astype(BF), da[:, hs]).astype(BF)
    cd = Gather(net, R, r, lambda h: dqkv.at[:, r, half(L, h), :], lambda j, h: dqkv.at[:, j, half(L, h), :])

    for n in range(D // W1):
        ns = slice(n * W1, (n + 1) * W1)
        val = (nt(dqkv[0, r], wqf[ns, :]) + nt(dqkv[1, r], wkf[ns, :]) + nt(dqkv[2, r], wvf[ns, :]))
        for j in range(C):
            for t in range(NT):
                p4[t, j % 2, j // 2, :, ns] = piece(val, j, t).astype(BF)
    k4 = [pre(p4.at[t], p4a.at[t]) for t in range(NT)]
    if line:
        z3.relay()
    z4 = []
    for t in range(NT):
        k4[t].wait_recv()
        z4.append(line_send(p4.at[t], p4a.at[t], p4s.at[t], p4r.at[t]))
    cgo.relay()
    if line:
        for k in z4:
            k.relay()
    gof[...] = tn(att[...], dmix[:, :, at(r * DR, DR)].reshape(L, DR))

    fs[...] = zsum(p3, p3a, p3r, z3).astype(BF)
    a_f = [net(fs.at[k], ft.at[:, at(r * DR, DR)], rows=r ^ k) for k in order]
    l_f = local(fs.at[0], ft.at[:, at(r * DR, DR)])
    cd.forward()

    def to_io(src, dst, t=slice(None)):
        cps = [net(src.at[t, :, at((c ^ k) * DC, DC)], dst.at[t, my_th, :], cols=c ^ k) for k in range(1, C)]
        return cps, local(src.at[t, :, at(c * DC, DC)], dst.at[t, my_th, :])

    l_f.wait()
    for k in a_f:
        k.wait_recv()
    lot[...] = (x1[...] + ft[...].astype(F32)).astype(BF).reshape(NT, TH, D)
    i_o = to_io(lot, lob)
    i_g = []
    for t in range(NT):
        rows = slice(t * TH, (t + 1) * TH)
        _, rstd1 = stats(xb[t, my_th, :].astype(F32))
        dh1 = zsum(p4.at[t], p4a.at[t], p4r.at[t], z4[t])
        git[t] = (dxt[rows, :] + norm_back(dh1, xtl[rows, :], rstd1)).astype(BF)
        i_g.append(to_io(git, gib, t))
    landed(i_o)
    lout.append(local(lob, o_out))
    for k in i_g:
        landed(k)
    gif[...] = gib[...].astype(F32)
    lout.append(local(gif, gi_out))
    arrived(cd)
    lout += [local(dqkv.at[0], dq_out), local(dqkv.at[1], dk_out), local(dqkv.at[2], dv_out)]
    cgo.wait()
    gsum = gof[...]
    for k in cgo.ks:
        gsum = gsum + gor[k].astype(F32)
    gof[...] = gsum
    lout.append(local(gof, go_out))
    net.drain()
    for k in lout:
        k.wait()


def body(R, C, tokens, segments, w_query, w_key, w_value, w_out, w_gate, w_up, w_down, cotangent):
    L, DC = tokens.shape
    DR, HC = w_query.shape
    D = DR * R
    FC = w_gate.shape[1]
    TL = L // C
    Z = C // 2
    NT = 2 if TL % 32 == 0 else 1
    LH, TH = L // NT, TL // NT
    QN = 4 // NT if FC % 1024 == 0 else 2
    QW = FC // QN
    g = dict(R=R, C=C, L=L, TL=TL, D=D, DR=DR, DC=DC, HC=HC, NT=NT, QN=QN)
    half = HD // 2
    fr = (BASE ** (-(np.arange(half, dtype=np.float32) * np.float32(2.0)) / np.float32(HD))).astype(np.float32)
    freq = jnp.asarray(np.concatenate([fr, fr])[None, :])
    S = jax.ShapeDtypeStruct
    V = pltpu.VMEM
    outs = [
        S((NT, LH, DC), BF), S((NT, LH, DC), F32), *[S((R, NT, LH, DR), BF)] * 3,
        S((R, L, FC), BF), S((R, L, FC), BF), S((R, L, FC), BF),
        S((R, L, HC), BF), S((R, L, HC), BF), S((R, L, HC), BF), S((HC, DR), F32),
    ]
    seq = lambda w: [V((NT, 2, Z, TH, w), BF)] + [V((NT, Z, TH, w), BF)] * 3
    seq4 = lambda: [V((2, Z, R, TL, DR), BF), V((Z, R, TL, DR), BF), V((Z, R, TL, DR), BF), V((Z, R, TL, DR), BF)]
    seq2 = lambda: [V((2, R, Z, TL, DR), BF), V((R, Z, TL, DR), BF), V((R, Z, TL, DR), BF), V((R, Z, TL, DR), BF)]
    scratch = [
        V((NT, LH, D), BF), V((NT, LH, D), BF), V((TL, D), F32), V((NT, TH, D), BF),
        *[V((R, NT, LH, DR), BF)] * 3, V((NT, TH, D), BF),
        V((D, HC), BF), V((D, HC), BF), V((D, HC), BF), V((HC, D), BF),
        V((DR, FC), BF), V((DR, FC), BF), V((FC, DR), BF),
        *seq(D), *seq2(), *seq4(), *seq(D),
        V((TL, D), F32), V((TL, D), F32),
        V((R, L, FC), BF), V((R, L, FC), BF), V((L, FC), F32),
        V((R, NT, QN, 2, LH, QW), BF), V((R, NT, QN, 2, LH, QW), BF), V((NT, QN, 2, LH, QW), F32),
        V((R, L, FC), BF), V((2, R, L, FC), BF),
        V((R, TL, DR), BF), V((TL, D), BF), V((TL, D), F32), V((NT, TH, D), BF), V((NT, LH, D), BF),
        V((L, HC), BF), V((L, HC), BF), V((L, HC), BF), V((L, HC), BF), V((L, HC), F32),
        V((L, HD), F32), V((L, HD), F32), V((L, L), F32),
        V((3, R, L, HC), BF), V((R, HC, DR), BF), V((R, HC, DR), BF), V((HC, DR), F32),
        V((R, TL, DR), BF), V((TL, D), BF), V((NT, TH, D), BF), V((NT, TH, D), BF),
        V((NT, LH, DC), BF), V((NT, LH, DC), BF), V((NT, LH, DC), F32),
        V((1, L), jnp.int32), V((1, HD), F32),
        pltpu.SemaphoreType.DMA((g_sems(R, C, NT * QN),)), pltpu.SemaphoreType.DMA((g_sems(R, C, NT * QN),)),
        pltpu.SemaphoreType.DMA((48,)),
    ]
    A = pl.BlockSpec(memory_space=pl.ANY)
    res = pl.pallas_call(
        functools.partial(step_kernel, g),
        out_shape=outs,
        in_specs=[A] * 11,
        out_specs=[A] * len(outs),
        scratch_shapes=scratch,
        compiler_params=pltpu.CompilerParams(
            collective_id=0, has_side_effects=True, vmem_limit_bytes=67043328),
        name="layer_step",
    )(tokens.reshape(NT, LH, DC), cotangent.reshape(NT, LH, DC), segments, freq, w_query, w_key, w_value, w_out, w_gate, w_up, w_down)
    layer_out, grad_in, h1w, gw, h2w, dg, du, hd, dq, dk, dv, go = res
    T = R * L
    h1w, gw, h2w = (t.reshape(T, DR) for t in (h1w, gw, h2w))
    gq, gk, gv = (tn(h1w, t.reshape(T, HC)) for t in (dq, dk, dv))
    ggate, gup, gdown = tn(h2w, dg.reshape(T, FC)), tn(h2w, du.reshape(T, FC)), tn(hd.reshape(T, FC), gw)
    return layer_out.reshape(L, DC), grad_in.reshape(L, DC), gq, gk, gv, go, ggate, gup, gdown


def g_sems(R, C, n):
    return 2 * (R - 1) * (8 + n) + 2 * R * (3 + n) + 8 * (R - 1) + 17 * C + (R + 4) * C // 2


def solution(mesh):
    R, C = mesh.shape["rows"], mesh.shape["cols"]
    rc, cr = P("rows", "cols"), P("cols", "rows")
    in_specs = (rc, P("rows", None), rc, rc, rc, cr, rc, rc, cr, rc)
    out_specs = (rc, rc, rc, rc, rc, cr, rc, rc, cr)
    return jax.shard_map(functools.partial(body, R, C), mesh=mesh, in_specs=in_specs,
                         out_specs=out_specs, check_vma=False)
```

```python
import functools
import jax
import jax.numpy as jnp
import numpy as np
from jax import lax
from jax.experimental import pallas as pl
from jax.experimental.pallas import tpu as pltpu
from jax.sharding import PartitionSpec as P

HD = 128
EPS = 1e-05
NEG = -1e30
BASE = 10000.0
F32 = jnp.float32
BF = jnp.bfloat16
MESH = pl.DeviceIdType.MESH


def nn(a, b):
    return jnp.dot(a, b, preferred_element_type=F32)


def nt(a, b):
    return lax.dot_general(a, b, (((1,), (1,)), ((), ())), preferred_element_type=F32)


def tn(a, b):
    return lax.dot_general(a, b, (((0,), (0,)), ((), ())), preferred_element_type=F32)


def at(start, size, step=None):
    return pl.ds(pl.multiple_of(start, step or size), size)


class Net:
    def __init__(self, send, recv):
        self.send, self.recv, self.all = send, recv, []

    def make(self, src, dst, i, j, peer):
        return pltpu.make_async_remote_copy(
            src_ref=src, dst_ref=dst, send_sem=self.send.at[i], recv_sem=self.recv.at[j],
            device_id=peer, device_id_type=MESH)

    def slot(self):
        assert len(self.all) < self.send.shape[0]
        self.all.append(None)
        return len(self.all) - 1

    def __call__(self, src, dst, **peer):
        i = self.slot()
        c = self.make(src, dst, i, i, peer)
        c.start()
        self.all[i] = Copy(c)
        return self.all[i]

    def only(self, pred, src, dst, land=None, **peer):
        i = self.slot()
        c = self.make(src, dst, i, i if land is None else land.i, peer)

        @pl.when(pred)
        def _():
            c.start()

        self.all[i] = Copy(c, pred, i)
        return self.all[i]

    def drain(self):
        for c in self.all:
            if c is None:
                continue
            if c.pred is None:
                c.c.wait_send()
            else:
                pl.when(c.pred)(c.c.wait_send)


class Copy:
    def __init__(self, c, pred=None, i=None):
        self.c, self.open, self.pred, self.i = c, True, pred, i

    def wait_recv(self):
        if self.open:
            self.c.wait_recv()
        self.open = False


class Gather:
    def __init__(self, net, R, r, own, blk):
        self.net, self.r, self.two, self.blk, self.c = net, r, R == 4, blk, {}
        todo = [(1, 0), (2, 1), (1, 1), (2, 0)] if self.two else [(k, h) for k in range(1, R) for h in range(2)]
        for k, h in todo:
            self.c[k, h] = net(own(h), blk(r, h), rows=r ^ k)

    def forward(self):
        if self.two:
            for k, h in ((1, 0), (2, 1)):
                self.c[k, h].wait_recv()
                b = self.blk(self.r ^ k, h)
                self.c[3, h] = self.net(b, b, rows=self.r ^ (3 - k))

    def wait(self, k):
        for h in range(2):
            self.c[k, h].wait_recv()


class Reduce:
    def __init__(self, net, R, r, snd, rcv):
        self.net, self.r, self.two, self.snd, self.rcv, self.c = net, r, R == 4, snd, rcv, {}
        self.ks = (1, 2) if self.two else tuple(range(1, R))
        if self.two:
            for k, h in ((1, 0), (2, 1)):
                self.c[3, h] = net(snd(3, h), rcv(3, h), rows=r ^ k)
            for k, h in ((1, 0), (2, 1)):
                self.c[k, h] = net(snd(k, h), rcv(k, h), rows=r ^ k)
        else:
            for k in self.ks:
                for h in range(2):
                    self.c[k, h] = net(snd(k, h), rcv(k, h), rows=r ^ k)

    def relay(self):
        if self.two:
            for k, h in ((2, 0), (1, 1)):
                self.c[3, h].wait_recv()
                a = self.snd(k, h)
                a[...] = (a[...].astype(F32) + self.rcv(3, h)[...].astype(F32)).astype(BF)
                self.c[k, h] = self.net(a, self.rcv(k, h), rows=self.r ^ k)

    def wait(self):
        for k in self.ks:
            for h in range(2):
                self.c[k, h].wait_recv()


class LCopy:
    def __init__(self, c):
        self.c, self.open = c, True

    def wait(self):
        if self.open:
            self.c.wait()
        self.open = False


class Local:
    def __init__(self, sem):
        self.sem, self.n, self.all = sem, 0, []

    def __call__(self, src, dst):
        c = pltpu.make_async_copy(src, dst, self.sem.at[self.n])
        self.n += 1
        c.start()
        self.all.append(LCopy(c))
        return self.all[-1]


def step_kernel(g, *refs):
    (tok, cot, seg_in, freq_in, wq, wk, wv, wo, wg, wu, wd,
     o_out, gi_out, gg_out, gu_out, gd_out, gq_out, gk_out, gv_out, go_out,
     xb, h1, xtl, gtl, h1w, gw, h2w, h2t, wqf, wkf, wvf, wof, wgv, wuv, wdv,
     p1, p1a, p1s, p1r, p2, p2a, p2s, p2r, p3, p3a, p3s, p3r, p4, p4a, p4s, p4r,
     x1, n2, dhs, dhr, dho, gus, gur, guo, hda, dgu, dh2s, dh2t, dxt, dmt, dmix,
     qb, kb, vb, att, lse, cosb, sinb, mskb, dqkv, gop, gor, gof, fs, ft, lot, git, lob, gib, wgg, wgu, wgd, wqa, segr, freq,
     send, recv, loc) = refs
    R, C, L, TL, D, DR, DC, HC, NT = (g[k] for k in ("R", "C", "L", "TL", "D", "DR", "DC", "HC", "NT"))
    LH, TH = L // NT, TL // NT
    Z = C // 2
    r = lax.axis_index("rows")
    c = lax.axis_index("cols")
    z = c // 2
    core = c % 2
    net = Net(send, recv)
    local = Local(loc)
    scale = HD ** (-0.5)
    my_th = at(c * TH, TH)

    def piece(val, j, t):
        return val[t * LH + j * TH:t * LH + (j + 1) * TH, :]

    bar = pltpu.get_barrier_semaphore()
    for k in range(1, R):
        pl.semaphore_signal(bar, inc=1, device_id={"rows": r ^ k}, device_id_type=MESH)
    for k in range(1, C):
        pl.semaphore_signal(bar, inc=1, device_id={"cols": c ^ k}, device_id_type=MESH)

    lsm = [local(seg_in, segr), local(freq_in, freq)]
    lx = local(tok, xb.at[:, :, at(c * DC, DC)])
    lg = local(cot.at[:, my_th, :], gtl.at[:, :, at(c * DC, DC)])
    lws = [local(wq, wqf.at[at(r * DR, DR), :]), local(wk, wkf.at[at(r * DR, DR), :]),
           local(wv, wvf.at[at(r * DR, DR), :]), local(wo, wof.at[:, at(r * DR, DR)])]
    lff = [local(wd, wdv), local(wg, wgv), local(wu, wuv)]

    pl.semaphore_wait(bar, R + C - 2)

    def half(n, h):
        return slice(h * (n // 2), (h + 1) * (n // 2))

    def w_in(w, full):
        n = DR // 2
        return Gather(net, R, r, lambda h: w.at[half(DR, h), :], lambda j, h: full.at[at(j * DR + h * n, n), :])

    def cols_start(blk):
        zs = [net(blk(c), blk(c), cols=c ^ (2 * m)) for m in range(1, Z)]
        return zs, net(blk(c), blk(c), cols=c ^ 1)

    def cols_forward(blk, zs):
        fw = []
        for m in range(1, Z):
            zs[m - 1].wait_recv()
            fw.append(net(blk(c ^ (2 * m)), blk(c ^ (2 * m)), cols=c ^ 1))
        return fw

    line = Z == 4
    mid = ((z + 1) // 2) % 2

    def line_start(blk):
        b = blk(c)
        z2 = net(b, b, cols=c ^ 4)
        z3 = net.only(mid == 1, b, b, cols=c ^ 6)
        return [net(b, b, cols=c ^ 2), z2, z3], net(b, b, cols=c ^ 1)

    def line_relay(blk, zs):
        zs[1].wait_recv()
        b = blk(c ^ 4)
        net.only(mid == 1, b, b, zs[2], cols=c ^ 2)

    def line_forward(blk, zs):
        fw = []
        for m in (2, 1, 3):
            zs[m - 1].wait_recv()
            fw.append(net(blk(c ^ (2 * m)), blk(c ^ (2 * m)), cols=c ^ 1))
        return fw

    def cols_finish(own, fw):
        own.wait_recv()
        for f in fw:
            f.wait_recv()

    def xblk(j):
        return xb.at[:, :, at(j * DC, DC)]

    cq = w_in(wq, wqf)
    xz = [net(tok, xblk(c), cols=c ^ (2 * m)) for m in range(1, Z)]
    xp = net(tok, xblk(c), cols=c ^ 1)
    ga = [net(cot.at[:, at((c ^ k) * TH, TH), :], gtl.at[:, :, at(c * DC, DC)], cols=c ^ k) for k in range(1, C)]
    ck = w_in(wk, wkf)

    for k in lsm:
        k.wait()
    sr = jnp.broadcast_to(segr[...].astype(F32), (L, L))
    sc = sr.T
    qi = lax.broadcasted_iota(jnp.int32, (L, L), 0)
    ki = lax.broadcasted_iota(jnp.int32, (L, L), 1)
    ok = (sr == sc) & (qi >= ki)
    okf = jnp.where(ok, 1.0, 0.0)
    mskb[...] = jnp.where(ok, 0.0, NEG)
    pos = jnp.sum(okf, 1, keepdims=True) - 1.0
    angle = pos * freq[...]
    lane = lax.broadcasted_iota(jnp.int32, (L, HD), 1)
    cosb[...] = jnp.cos(angle)
    sn = jnp.sin(angle)
    sinb[...] = jnp.where(lane < HD // 2, -sn, sn)

    def to_ws(src, dst, t=slice(None)):
        cps = [net(src.at[t, :, at((r ^ k) * DR, DR)], dst.at[r, t, my_th, :], rows=r ^ k) for k in range(1, R)]
        return cps, local(src.at[t, :, at(r * DR, DR)], dst.at[r, t, my_th, :])

    def landed(cl):
        for k in cl[0]:
            k.wait_recv()
        cl[1].wait()

    cq.forward()
    cv = w_in(wv, wvf)
    lx.wait()
    xf = cols_forward(xblk, xz)
    lg.wait()
    for k in ga:
        k.wait_recv()
    a_g = to_ws(gtl, gw)
    ck.forward()
    cols_finish(xp, xf)

    def stats(v):
        mean = jnp.sum(v, 1, keepdims=True) / D
        sq = jnp.sum(v * v, 1, keepdims=True) / D
        return mean, lax.rsqrt(sq - mean * mean + EPS)

    for t in range(NT):
        def norm_rows(i, _, t=t):
            rows = at(i * 32, 32)
            v = xb[t, rows, :].astype(F32)
            mean, rstd = stats(v)
            h1[t, rows, :] = ((v - mean) * rstd).astype(BF)
            return 0

        lax.fori_loop(0, LH // 32, norm_rows, 0)

    cv.forward()
    co = Gather(net, R, r, lambda h: wo.at[half(HC, h), :], lambda j, h: wof.at[half(HC, h), at(j * DR, DR)])

    def wsblk(buf, t=slice(None)):
        return lambda j: buf.at[:, t, at(j * TH, TH), :]

    heads = HC // HD

    def rope(v):
        return jnp.concatenate(
            [v[:, h * HD:(h + 1) * HD] * cosb[...]
             + pltpu.roll(v[:, h * HD:(h + 1) * HD], HD // 2, 1) * sinb[...] for h in range(heads)], 1)

    def unrope(v):
        return v * cosb[...] + pltpu.roll(v * sinb[...], HD // 2, 1)

    def arrived(g):
        for k in range(1, R):
            g.wait(k)

    landed(a_g)
    g_z, g_p = cols_start(wsblk(gw))
    lws[0].wait()
    arrived(cq)
    qb[...] = rope(nn(h1[...].reshape(L, D), wqf[...])).astype(BF)
    lws[1].wait()
    arrived(ck)
    kb[...] = rope(nn(h1[...].reshape(L, D), wkf[...])).astype(BF)
    lws[2].wait()
    arrived(cv)
    vb[...] = nn(h1[...].reshape(L, D), wvf[...]).astype(BF)

    for h in range(heads):
        hs = slice(h * HD, (h + 1) * HD)
        s = nt(qb[:, hs], kb[:, hs]) * scale
        s = jnp.where(mskb[...] < 0.0, NEG, s)
        top = jnp.max(s, 1, keepdims=True)
        e = jnp.exp(s - top)
        tot = jnp.sum(e, 1, keepdims=True)
        lse[:, hs] = jnp.broadcast_to(top + jnp.log(tot), (L, HD))
        att[:, hs] = nn((e / tot).astype(BF), vb[:, hs]).astype(BF)

    co.forward()
    lws[3].wait()
    arrived(co)
    W1 = min(512, D)
    for n in range(D // W1):
        ns = slice(n * W1, (n + 1) * W1)
        val = nn(att[...], wof[:, ns])
        for j in range(C):
            for t in range(NT):
                p1[t, j % 2, j // 2, :, ns] = piece(val, j, t).astype(BF)

    def pre(p, pa):
        return net(p.at[1 - core], pa, cols=c ^ 1)

    def zsend(p, pa, ps, pr):
        out = []
        for m in range(1, Z):
            ps[m] = (p[core, z ^ m].astype(F32) + pa[z ^ m].astype(F32)).astype(BF)
            out.append(net(ps.at[m], pr.at[m], cols=c ^ (2 * m)))
        return out

    class Line:
        def __init__(self, p, pa, ps, pr):
            self.ps, self.pr = ps, pr
            for m in (3, 1, 2):
                ps[m] = (p[core, z ^ m].astype(F32) + pa[z ^ m].astype(F32)).astype(BF)
                if m == 3:
                    self.i, self.j = net.slot(), net.slot()
                    far = net.make(ps.at[3], pr.at[3 * mid], self.i, self.j + mid * (self.i - self.j),
                                   {"cols": c ^ (2 + 4 * mid)})
                    far.start()
                    net.all[self.i] = Copy(far)
                if m == 1:
                    self.c1 = net(ps.at[1], pr.at[1], cols=c ^ 2)

            @pl.when(mid == 0)
            def _():
                pr[3] = jnp.zeros(pr.shape[1:], BF)

        def relay(self):
            ps, pr = self.ps, self.pr

            @pl.when(mid == 1)
            def _():
                net.make(ps.at[3], pr.at[0], self.i, self.j, {"cols": c ^ 2}).wait_recv()
                ps[2] = (ps[2].astype(F32) + pr[0].astype(F32)).astype(BF)

            self.c2 = net(ps.at[2], pr.at[2], cols=c ^ 4)

        def total(self, p, pa):
            ps, pr = self.ps, self.pr
            self.c1.wait_recv()
            self.c2.wait_recv()

            @pl.when(mid == 1)
            def _():
                net.make(ps.at[3], pr.at[3], self.i, self.i, {"cols": c ^ 6}).wait_recv()

            return (p[core, z].astype(F32) + pa[z].astype(F32) + pr[1].astype(F32) + pr[2].astype(F32)
                    + pr[3].astype(F32))

    def line_send(p, pa, ps, pr):
        return Line(p, pa, ps, pr) if line else zsend(p, pa, ps, pr)

    def zsum(p, pa, pr, cps):
        if isinstance(cps, Line):
            return cps.total(p, pa)
        tot = p[core, z].astype(F32) + pa[z].astype(F32)
        for m in range(1, Z):
            cps[m - 1].wait_recv()
            tot = tot + pr[m].astype(F32)
        return tot

    k1 = [pre(p1.at[t], p1a.at[t]) for t in range(NT)]
    g_f = cols_forward(wsblk(gw), g_z)
    z1 = []
    for t in range(NT):
        k1[t].wait_recv()
        z1.append(zsend(p1.at[t], p1a.at[t], p1s.at[t], p1r.at[t]))
    cols_finish(g_p, g_f)
    lout = []

    lff[0].wait()
    order = list(range(1, R))
    FC = wgv.shape[1]
    DN = 2
    DW = FC // DN

    def dhid_chunk(n):
        for k in order:
            dhs[k, :, n * DW:(n + 1) * DW] = nt(gw[r ^ k].reshape(L, DR), wdv[n * DW:(n + 1) * DW, :]).astype(BF)

    def dhid_send(n):
        ns = slice(n * DW, (n + 1) * DW)
        return Reduce(net, R, r, lambda k, h: dhs.at[k, half(L, h), ns], lambda k, h: dhr.at[k, half(L, h), ns])

    dhid_chunk(0)
    dh = [dhid_send(0)]
    for n in range(1, DN):
        dhid_chunk(n)

    xv = xb[:, my_th, :].reshape(TL, D).astype(F32)
    xm, xr_ = stats(xv)
    xtl[...] = (xv - xm) * xr_

    def second_norm(t):
        rows = slice(t * TH, (t + 1) * TH)
        v = xb[t, my_th, :].astype(F32) + zsum(p1.at[t], p1a.at[t], p1r.at[t], z1[t])
        x1[rows, :] = v
        mean2, rstd2 = stats(v)
        n2v = (v - mean2) * rstd2
        n2[rows, :] = n2v
        h2t[t] = n2v.astype(BF)
        return to_ws(h2t, h2w, t)

    h2_c = []
    for t in range(NT):
        a_2 = second_norm(t)
        if t == 0:
            for n in range(1, DN):
                dh.append(dhid_send(n))
            for n in range(DN):
                dho[:, n * DW:(n + 1) * DW] = nt(gw[r].reshape(L, DR), wdv[n * DW:(n + 1) * DW, :])
        else:
            dh[0].relay()
        landed(a_2)
        h2_c.append(cols_start(wsblk(h2w, t)))
    for d in dh[min(NT, 2) - 1:]:
        d.relay()
    a_h = to_ws(h1.at[:, my_th, :], h1w)
    lff[1].wait()
    lff[2].wait()

    QN = g["QN"]
    QW = FC // QN
    gu = []
    parts = [(t, q) for t in range(NT) for q in range(QN)]

    def gu_chunk(t, q):
        qs = slice(q * QW, (q + 1) * QW)
        for k in order[::-1] + [0]:
            ga_ = nn(h2w[r ^ k, t], wgv[:, qs])
            up_ = nn(h2w[r ^ k, t], wuv[:, qs])
            if k:
                gus[k, t, q, 0] = ga_.astype(BF)
                gus[k, t, q, 1] = up_.astype(BF)
            else:
                guo[t, q, 0] = ga_
                guo[t, q, 1] = up_
        gu.append(Reduce(net, R, r, lambda k, h: gus.at[k, t, q, :, half(LH, h), :],
                         lambda k, h: gur.at[k, t, q, :, half(LH, h), :]))

    for t, q in parts:
        if q == 0:
            cols_finish(h2_c[t][1], cols_forward(wsblk(h2w, t), h2_c[t][0]))
        gu_chunk(t, q)
        if len(gu) > 1:
            gu[-2].relay()
    gu[-1].relay()
    landed(a_h)
    h_z, h_p = cols_start(wsblk(h1w))

    for d in dh:
        d.wait()
    dgt = []
    AR = 16
    for n, (t, q) in enumerate(parts):
        gu[n].wait()
        qs = slice(q * QW, (q + 1) * QW)

        def act(i, _, n=n, t=t, q=q, qs=qs):
            part = at(i * AR, AR)
            rows = at(t * LH + i * AR, AR)
            gate, up = guo[t, q, 0, part, :], guo[t, q, 1, part, :]
            dhid = dho[rows, qs]
            for k in gu[n].ks:
                gate = gate + gur[k, t, q, 0, part, :].astype(F32)
                up = up + gur[k, t, q, 1, part, :].astype(F32)
                dhid = dhid + dhr[k, rows, qs].astype(F32)
            sig = 1.0 / (1.0 + jnp.exp(-gate))
            silu = gate * sig
            hda[r, rows, qs] = (silu * up).astype(BF)
            dgu[0, r, rows, qs] = (dhid * up * sig * (1.0 + gate * (1.0 - sig))).astype(BF)
            dgu[1, r, rows, qs] = (dhid * silu).astype(BF)
            return 0
        lax.fori_loop(0, LH // AR, act, 0)

        def tok_half(h, t=t):
            return slice(t * LH + h * (LH // 2), t * LH + (h + 1) * (LH // 2))
        dgt.append(Gather(net, R, r, lambda h, qs=qs, f=tok_half: dgu.at[:, r, f(h), qs],
                          lambda j, h, qs=qs, f=tok_half: dgu.at[:, j, f(h), qs]))

    k2 = {}

    def dh2_block(k):
        s = r ^ k
        tot = nt(dgu[0, s], wgv[...]) + nt(dgu[1, s], wuv[...])
        for j in range(C):
            for t in range(NT):
                p2[j % 2, k, j // 2, t * TH:(t + 1) * TH] = piece(tot, j, t).astype(BF)
        k2[k] = net(p2.at[1 - core, k], p2a.at[k], cols=c ^ 1)

    dh2_block(0)
    z2 = {}
    for d in dgt:
        d.forward()

    def hid_send(n):
        ns = slice(n * DW, (n + 1) * DW)
        return Gather(net, R, r, lambda h: hda.at[r, half(L, h), ns], lambda j, h: hda.at[j, half(L, h), ns])

    hdc = [hid_send(0)]

    def z2_send(k):
        k2[k].wait_recv()
        for m in range(1, Z):
            p2s[k, m] = (p2[core, k, z ^ m].astype(F32) + p2a[k, z ^ m].astype(F32)).astype(BF)
            z2[k, m] = net(p2s.at[k, m], p2r.at[k, m], cols=c ^ (2 * m))

    for n, k in enumerate(order):
        for d in dgt:
            d.wait(k)
        dh2_block(k)
        z2_send(n)
    z2_send(R - 1)
    T = R * L

    def wgrad(dst, lhs, rhs):
        w = 128
        for i in range(dst.shape[0] // w):
            dst[i * w:(i + 1) * w, :] = tn(lhs(slice(i * w, (i + 1) * w)), rhs).astype(BF)

    wgrad(wgg, lambda ns: h2w[:, :, :, ns].reshape(T, 128), dgu[0].reshape(T, FC))
    lout.append(local(wgg, gg_out))
    hdc[0].forward()

    a_d = []
    for k in range(R):
        tot = p2[core, k, z].astype(F32) + p2a[k, z].astype(F32)
        for m in range(1, Z):
            z2[k, m].wait_recv()
            tot = tot + p2r[k, m].astype(F32)
        dh2s[k] = tot.astype(BF)
        if k:
            a_d.append(net(dh2s.at[k], dh2t.at[:, at(r * DR, DR)], rows=r ^ k))
        else:
            l_d = local(dh2s.at[0], dh2t.at[:, at(r * DR, DR)])
    hdc += [hid_send(n) for n in range(1, DN)]
    l_d.wait()
    for k in a_d:
        k.wait_recv()

    def norm_back(grad, normed, rstd):
        a = jnp.sum(grad, 1, keepdims=True) / D
        b = jnp.sum(grad * normed, 1, keepdims=True) / D
        return rstd * (grad - a - normed * b)

    _, rstd2b = stats(x1[...])
    dxv = gtl[...].reshape(TL, D).astype(F32) + norm_back(dh2t[...].astype(F32), n2[...], rstd2b)
    dxt[...] = dxv
    dmt[...] = dxv.astype(BF).reshape(NT, TH, D)
    l_m = local(dmt, dmix.at[:, my_th, :])

    def dblk(j):
        return dmix.at[:, at(j * TH, TH), :]
    l_m.wait()
    m_z, m_p = line_start(dblk) if line else cols_start(dblk)

    def ffn_block(k):
        s = r ^ k
        tot = nn(hda[s], wdv[...])
        for j in range(C):
            for t in range(NT):
                p3[j % 2, j // 2, k, t * TH:(t + 1) * TH] = piece(tot, j, t).astype(BF)

    ffn_block(0)
    h_f = cols_forward(wsblk(h1w), h_z)
    wgrad(wgu, lambda ns: h2w[:, :, :, ns].reshape(T, 128), dgu[1].reshape(T, FC))
    lout.append(local(wgu, gu_out))
    for d in hdc[1:]:
        d.forward()
    if line:
        line_relay(dblk, m_z)
    for k in order:
        for d in hdc:
            d.wait(k)
        ffn_block(k)
    k3 = pre(p3, p3a)
    cols_finish(h_p, h_f)
    k3.wait_recv()
    m_f = line_forward(dblk, m_z) if line else cols_forward(dblk, m_z)
    z3 = line_send(p3, p3a, p3s, p3r)
    cols_finish(m_p, m_f)

    for k in order:
        gop[k] = tn(att[...], dmix[:, :, at((r ^ k) * DR, DR)].reshape(L, DR)).astype(BF)
    cgo = Reduce(net, R, r, lambda k, h: gop.at[k, half(HC, h), :], lambda k, h: gor.at[k, half(HC, h), :])
    da = nt(dmix[...].reshape(L, D), wof[...]).astype(BF)
    for h in range(heads):
        hs = slice(h * HD, (h + 1) * HD)
        s = nt(qb[:, hs], kb[:, hs]) * scale
        s = jnp.where(mskb[...] < 0.0, NEG, s)
        pr = jnp.exp(s - lse[:, h * HD:h * HD + 1])
        dp = nt(da[:, hs], vb[:, hs])
        inner = jnp.sum(pr * dp, 1, keepdims=True)
        ds = (pr * (dp - inner)).astype(BF)
        dqkv[0, r, :, hs] = unrope(nn(ds, kb[:, hs]) * scale).astype(BF)
        dqkv[1, r, :, hs] = unrope(tn(ds, qb[:, hs]) * scale).astype(BF)
        dqkv[2, r, :, hs] = tn(pr.astype(BF), da[:, hs]).astype(BF)
    cd = Gather(net, R, r, lambda h: dqkv.at[:, r, half(L, h), :], lambda j, h: dqkv.at[:, j, half(L, h), :])

    for n in range(D // W1):
        ns = slice(n * W1, (n + 1) * W1)
        val = (nt(dqkv[0, r], wqf[ns, :]) + nt(dqkv[1, r], wkf[ns, :]) + nt(dqkv[2, r], wvf[ns, :]))
        for j in range(C):
            for t in range(NT):
                p4[t, j % 2, j // 2, :, ns] = piece(val, j, t).astype(BF)
    k4 = [pre(p4.at[t], p4a.at[t]) for t in range(NT)]
    if line:
        z3.relay()
    z4 = []
    for t in range(NT):
        k4[t].wait_recv()
        z4.append(line_send(p4.at[t], p4a.at[t], p4s.at[t], p4r.at[t]))
    cgo.relay()
    if line:
        for k in z4:
            k.relay()
    gof[...] = tn(att[...], dmix[:, :, at(r * DR, DR)].reshape(L, DR))

    fs[...] = zsum(p3, p3a, p3r, z3).astype(BF)
    a_f = [net(fs.at[k], ft.at[:, at(r * DR, DR)], rows=r ^ k) for k in order]
    l_f = local(fs.at[0], ft.at[:, at(r * DR, DR)])
    cd.forward()

    def to_io(src, dst, t=slice(None)):
        cps = [net(src.at[t, :, at((c ^ k) * DC, DC)], dst.at[t, my_th, :], cols=c ^ k) for k in range(1, C)]
        return cps, local(src.at[t, :, at(c * DC, DC)], dst.at[t, my_th, :])

    def qkv_grad(k):
        for i in range(3):
            t = tn(h1w[r ^ k].reshape(L, DR), dqkv[i, r ^ k])
            wqa[i] = t if k == 0 else wqa[i] + t

    qkv_grad(0)
    wgrad(wgd, lambda ns: hda[:, :, ns].reshape(T, 128), gw[...].reshape(T, DR))
    lout.append(local(wgd, gd_out))
    l_f.wait()
    for k in a_f:
        k.wait_recv()
    lot[...] = (x1[...] + ft[...].astype(F32)).astype(BF).reshape(NT, TH, D)
    i_o = to_io(lot, lob)
    for k in order[:-1]:
        cd.wait(k)
        qkv_grad(k)
    i_g = []
    for t in range(NT):
        rows = slice(t * TH, (t + 1) * TH)
        _, rstd1 = stats(xb[t, my_th, :].astype(F32))
        dh1 = zsum(p4.at[t], p4a.at[t], p4r.at[t], z4[t])
        git[t] = (dxt[rows, :] + norm_back(dh1, xtl[rows, :], rstd1)).astype(BF)
        i_g.append(to_io(git, gib, t))
    cd.wait(R - 1)
    qkv_grad(R - 1)
    lout += [local(wqa.at[0], gq_out), local(wqa.at[1], gk_out), local(wqa.at[2], gv_out)]
    landed(i_o)
    lout.append(local(lob, o_out))
    for k in i_g:
        landed(k)
    lout.append(local(gib, gi_out))
    cgo.wait()
    gsum = gof[...]
    for k in cgo.ks:
        gsum = gsum + gor[k].astype(F32)
    gof[...] = gsum
    lout.append(local(gof, go_out))
    net.drain()
    for k in lout:
        k.wait()


def body(R, C, tokens, segments, w_query, w_key, w_value, w_out, w_gate, w_up, w_down, cotangent):
    L, DC = tokens.shape
    DR, HC = w_query.shape
    D = DR * R
    FC = w_gate.shape[1]
    TL = L // C
    Z = C // 2
    NT = 2 if TL % 32 == 0 else 1
    LH, TH = L // NT, TL // NT
    QN = 4 // NT if FC % 1024 == 0 else 2
    QW = FC // QN
    g = dict(R=R, C=C, L=L, TL=TL, D=D, DR=DR, DC=DC, HC=HC, NT=NT, QN=QN)
    half = HD // 2
    fr = (BASE ** (-(np.arange(half, dtype=np.float32) * np.float32(2.0)) / np.float32(HD))).astype(np.float32)
    freq = jnp.asarray(np.concatenate([fr, fr])[None, :])
    S = jax.ShapeDtypeStruct
    V = pltpu.VMEM
    outs = [
        S((NT, LH, DC), BF), S((NT, LH, DC), BF), S((DR, FC), BF), S((DR, FC), BF), S((FC, DR), BF),
        *[S((DR, HC), F32)] * 3, S((HC, DR), F32),
    ]
    seq = lambda w: [V((NT, 2, Z, TH, w), BF)] + [V((NT, Z, TH, w), BF)] * 3
    seq4 = lambda: [V((2, Z, R, TL, DR), BF), V((Z, R, TL, DR), BF), V((Z, R, TL, DR), BF), V((Z, R, TL, DR), BF)]
    seq2 = lambda: [V((2, R, Z, TL, DR), BF), V((R, Z, TL, DR), BF), V((R, Z, TL, DR), BF), V((R, Z, TL, DR), BF)]
    scratch = [
        V((NT, LH, D), BF), V((NT, LH, D), BF), V((TL, D), F32), V((NT, TH, D), BF),
        *[V((R, NT, LH, DR), BF)] * 3, V((NT, TH, D), BF),
        V((D, HC), BF), V((D, HC), BF), V((D, HC), BF), V((HC, D), BF),
        V((DR, FC), BF), V((DR, FC), BF), V((FC, DR), BF),
        *seq(D), *seq2(), *seq4(), *seq(D),
        V((TL, D), F32), V((TL, D), F32),
        V((R, L, FC), BF), V((R, L, FC), BF), V((L, FC), F32),
        V((R, NT, QN, 2, LH, QW), BF), V((R, NT, QN, 2, LH, QW), BF), V((NT, QN, 2, LH, QW), F32),
        V((R, L, FC), BF), V((2, R, L, FC), BF),
        V((R, TL, DR), BF), V((TL, D), BF), V((TL, D), F32), V((NT, TH, D), BF), V((NT, LH, D), BF),
        V((L, HC), BF), V((L, HC), BF), V((L, HC), BF), V((L, HC), BF), V((L, HC), F32),
        V((L, HD), F32), V((L, HD), F32), V((L, L), F32),
        V((3, R, L, HC), BF), V((R, HC, DR), BF), V((R, HC, DR), BF), V((HC, DR), F32),
        V((R, TL, DR), BF), V((TL, D), BF), V((NT, TH, D), BF), V((NT, TH, D), BF),
        V((NT, LH, DC), BF), V((NT, LH, DC), BF),
        V((DR, FC), BF), V((DR, FC), BF), V((FC, DR), BF), V((3, DR, HC), F32),
        V((1, L), jnp.int32), V((1, HD), F32),
        pltpu.SemaphoreType.DMA((g_sems(R, C, NT * QN),)), pltpu.SemaphoreType.DMA((g_sems(R, C, NT * QN),)),
        pltpu.SemaphoreType.DMA((48,)),
    ]
    A = pl.BlockSpec(memory_space=pl.ANY)
    res = pl.pallas_call(
        functools.partial(step_kernel, g),
        out_shape=outs,
        in_specs=[A] * 11,
        out_specs=[A] * len(outs),
        scratch_shapes=scratch,
        compiler_params=pltpu.CompilerParams(
            collective_id=0, has_side_effects=True, vmem_limit_bytes=67043328),
        name="layer_step",
    )(tokens.reshape(NT, LH, DC), cotangent.reshape(NT, LH, DC), segments, freq, w_query, w_key, w_value, w_out, w_gate, w_up, w_down)
    layer_out, grad_in, ggate, gup, gdown, gq, gk, gv, go = res
    return finish(layer_out.reshape(L, DC), grad_in.reshape(L, DC), gq, gk, gv, go, ggate, gup, gdown)


def finish(layer_out, *grads):
    ins = (layer_out,) + grads
    n = len(ins)
    types = [BF] + [F32] * len(grads)
    wide = [i for i in range(n) if ins[i].dtype != types[i]]

    def kern(*refs):
        src, dst, buf = refs[:n], refs[n:2 * n], refs[2 * n:3 * n]
        out = dict(zip(wide, refs[3 * n:3 * n + len(wide)]))
        si, so = refs[-2:]
        got = [pltpu.make_async_copy(src[i], buf[i], si.at[i]) for i in range(n)]
        put = [pltpu.make_async_copy(out.get(i, buf[i]), dst[i], so.at[i]) for i in range(n)]
        for i in reversed(range(n)):
            got[i].start()
        for i in reversed(range(n)):
            got[i].wait()
            if i in out:
                out[i][...] = buf[i][...].astype(F32)
            put[i].start()
        for i in range(n):
            put[i].wait()

    A = pl.BlockSpec(memory_space=pl.ANY)
    V = pltpu.VMEM
    return pl.pallas_call(
        kern,
        out_shape=[jax.ShapeDtypeStruct(a.shape, t) for a, t in zip(ins, types)],
        in_specs=[A] * n, out_specs=[A] * n,
        scratch_shapes=[V(a.shape, a.dtype) for a in ins] + [V(ins[i].shape, F32) for i in wide]
        + [pltpu.SemaphoreType.DMA((n,)), pltpu.SemaphoreType.DMA((n,))],
        compiler_params=pltpu.CompilerParams(vmem_limit_bytes=67043328),
        name="finish",
    )(*ins)

def g_sems(R, C, n):
    return 2 * (R - 1) * (8 + n) + 2 * R * (3 + n) + 8 * (R - 1) + 17 * C + (R + 4) * C // 2


def solution(mesh):
    R, C = mesh.shape["rows"], mesh.shape["cols"]
    rc, cr = P("rows", "cols"), P("cols", "rows")
    in_specs = (rc, P("rows", None), rc, rc, rc, cr, rc, rc, cr, rc)
    out_specs = (rc, rc, rc, rc, rc, cr, rc, rc, cr)
    return jax.shard_map(functools.partial(body, R, C), mesh=mesh, in_specs=in_specs,
                         out_specs=out_specs, check_vma=False)
```

```python
import functools
import jax
import jax.numpy as jnp
import numpy as np
from jax import lax
from jax.experimental import pallas as pl
from jax.experimental.pallas import tpu as pltpu
from jax.sharding import PartitionSpec as P

HD = 128
EPS = 1e-05
NEG = -1e30
BASE = 10000.0
F32 = jnp.float32
BF = jnp.bfloat16
MESH = pl.DeviceIdType.MESH


def nn(a, b):
    return jnp.dot(a, b, preferred_element_type=F32)


def nt(a, b):
    return lax.dot_general(a, b, (((1,), (1,)), ((), ())), preferred_element_type=F32)


def tn(a, b):
    return lax.dot_general(a, b, (((0,), (0,)), ((), ())), preferred_element_type=F32)


def at(start, size, step=None):
    return pl.ds(pl.multiple_of(start, step or size), size)


class Net:
    def __init__(self, send, recv):
        self.send, self.recv, self.all = send, recv, []

    def make(self, src, dst, i, j, peer):
        return pltpu.make_async_remote_copy(
            src_ref=src, dst_ref=dst, send_sem=self.send.at[i], recv_sem=self.recv.at[j],
            device_id=peer, device_id_type=MESH)

    def slot(self):
        assert len(self.all) < self.send.shape[0]
        self.all.append(None)
        return len(self.all) - 1

    def __call__(self, src, dst, **peer):
        i = self.slot()
        c = self.make(src, dst, i, i, peer)
        c.start()
        self.all[i] = Copy(c)
        return self.all[i]

    def only(self, pred, src, dst, land=None, **peer):
        i = self.slot()
        c = self.make(src, dst, i, i if land is None else land.i, peer)

        @pl.when(pred)
        def _():
            c.start()

        self.all[i] = Copy(c, pred, i)
        return self.all[i]

    def drain(self):
        for c in self.all:
            if c is None:
                continue
            if c.pred is None:
                c.c.wait_send()
            else:
                pl.when(c.pred)(c.c.wait_send)


class Copy:
    def __init__(self, c, pred=None, i=None):
        self.c, self.open, self.pred, self.i = c, True, pred, i

    def wait_recv(self):
        if self.open:
            self.c.wait_recv()
        self.open = False


class Gather:
    def __init__(self, net, R, r, own, blk):
        self.net, self.r, self.two, self.blk, self.c = net, r, R == 4, blk, {}
        todo = [(1, 0), (2, 1), (1, 1), (2, 0)] if self.two else [(k, h) for k in range(1, R) for h in range(2)]
        for k, h in todo:
            self.c[k, h] = net(own(h), blk(r, h), rows=r ^ k)

    def forward(self):
        if self.two:
            for k, h in ((1, 0), (2, 1)):
                self.c[k, h].wait_recv()
                b = self.blk(self.r ^ k, h)
                self.c[3, h] = self.net(b, b, rows=self.r ^ (3 - k))

    def wait(self, k):
        for h in range(2):
            self.c[k, h].wait_recv()


class Reduce:
    def __init__(self, net, R, r, snd, rcv):
        self.net, self.r, self.two, self.snd, self.rcv, self.c = net, r, R == 4, snd, rcv, {}
        self.ks = (1, 2) if self.two else tuple(range(1, R))
        if self.two:
            for k, h in ((1, 0), (2, 1)):
                self.c[3, h] = net(snd(3, h), rcv(3, h), rows=r ^ k)
            for k, h in ((1, 0), (2, 1)):
                self.c[k, h] = net(snd(k, h), rcv(k, h), rows=r ^ k)
        else:
            for k in self.ks:
                for h in range(2):
                    self.c[k, h] = net(snd(k, h), rcv(k, h), rows=r ^ k)

    def relay(self):
        if self.two:
            for k, h in ((2, 0), (1, 1)):
                self.c[3, h].wait_recv()
                a = self.snd(k, h)
                a[...] = (a[...].astype(F32) + self.rcv(3, h)[...].astype(F32)).astype(BF)
                self.c[k, h] = self.net(a, self.rcv(k, h), rows=self.r ^ k)

    def wait(self):
        for k in self.ks:
            for h in range(2):
                self.c[k, h].wait_recv()


class LCopy:
    def __init__(self, c):
        self.c, self.open = c, True

    def wait(self):
        if self.open:
            self.c.wait()
        self.open = False


class Local:
    def __init__(self, sem):
        self.sem, self.n, self.all = sem, 0, []

    def __call__(self, src, dst):
        c = pltpu.make_async_copy(src, dst, self.sem.at[self.n])
        self.n += 1
        c.start()
        self.all.append(LCopy(c))
        return self.all[-1]


def step_kernel(g, *refs):
    (tok, cot, seg_in, freq_in, wq, wk, wv, wo, wg, wu, wd,
     o_out, gi_out, gg_out, gu_out, gd_out, gq_out, gk_out, gv_out, go_out,
     xb, h1, xtl, gtl, h1w, gw, h2w, h2t, wqf, wkf, wvf, wof, wgv, wuv, wdv,
     p1, p1a, p1s, p1r, p2, p2a, p2s, p2r, p3, p3a, p3s, p3r, p4, p4a, p4s, p4r,
     x1, n2, dhs, dhr, dho, gus, gur, guo, hda, dgu, dh2s, dh2t, dxt, dmt, dmix,
     qb, kb, vb, att, lse, cosb, sinb, mskb, dqkv, gop, gor, gof, fs, ft, lot, git, lob, gib, wgg, wgu, wgd, wqa, segr, freq,
     send, recv, loc) = refs
    R, C, L, TL, D, DR, DC, HC, NT = (g[k] for k in ("R", "C", "L", "TL", "D", "DR", "DC", "HC", "NT"))
    LH, TH = L // NT, TL // NT
    Z = C // 2
    r = lax.axis_index("rows")
    c = lax.axis_index("cols")
    z = c // 2
    core = c % 2
    net = Net(send, recv)
    local = Local(loc)
    scale = HD ** (-0.5)
    my_th = at(c * TH, TH)

    def piece(val, j, t):
        return val[t * LH + j * TH:t * LH + (j + 1) * TH, :]

    bar = pltpu.get_barrier_semaphore()
    for k in range(1, R):
        pl.semaphore_signal(bar, inc=1, device_id={"rows": r ^ k}, device_id_type=MESH)
    for k in range(1, C):
        pl.semaphore_signal(bar, inc=1, device_id={"cols": c ^ k}, device_id_type=MESH)

    lsm = [local(seg_in, segr), local(freq_in, freq)]
    lx = local(tok, xb.at[:, :, at(c * DC, DC)])
    lg = local(cot.at[:, my_th, :], gtl.at[:, :, at(c * DC, DC)])
    lws = [local(wq, wqf.at[at(r * DR, DR), :]), local(wk, wkf.at[at(r * DR, DR), :]),
           local(wv, wvf.at[at(r * DR, DR), :]), local(wo, wof.at[:, at(r * DR, DR)])]
    lff = [local(wd, wdv), local(wg, wgv), local(wu, wuv)]

    pl.semaphore_wait(bar, R + C - 2)

    def half(n, h):
        return slice(h * (n // 2), (h + 1) * (n // 2))

    def w_in(w, full):
        n = DR // 2
        return Gather(net, R, r, lambda h: w.at[half(DR, h), :], lambda j, h: full.at[at(j * DR + h * n, n), :])

    def cols_start(blk):
        zs = [net(blk(c), blk(c), cols=c ^ (2 * m)) for m in range(1, Z)]
        return zs, net(blk(c), blk(c), cols=c ^ 1)

    def cols_forward(blk, zs):
        fw = []
        for m in range(1, Z):
            zs[m - 1].wait_recv()
            fw.append(net(blk(c ^ (2 * m)), blk(c ^ (2 * m)), cols=c ^ 1))
        return fw

    line = Z == 4
    mid = ((z + 1) // 2) % 2

    def line_start(blk):
        b = blk(c)
        z2 = net(b, b, cols=c ^ 4)
        z3 = net.only(mid == 1, b, b, cols=c ^ 6)
        return [net(b, b, cols=c ^ 2), z2, z3], net(b, b, cols=c ^ 1)

    def line_relay(blk, zs):
        zs[1].wait_recv()
        b = blk(c ^ 4)
        net.only(mid == 1, b, b, zs[2], cols=c ^ 2)

    def line_forward(blk, zs):
        fw = []
        for m in (2, 1, 3):
            zs[m - 1].wait_recv()
            fw.append(net(blk(c ^ (2 * m)), blk(c ^ (2 * m)), cols=c ^ 1))
        return fw

    def cols_finish(own, fw):
        own.wait_recv()
        for f in fw:
            f.wait_recv()

    def xblk(j):
        return xb.at[:, :, at(j * DC, DC)]

    cq = w_in(wq, wqf)
    ga = [net(cot.at[:, at((c ^ k) * TH, TH), :], gtl.at[:, :, at(c * DC, DC)], cols=c ^ k) for k in range(1, C)]
    xz = [net(tok, xblk(c), cols=c ^ (2 * m)) for m in range(1, Z)]
    xp = net(tok, xblk(c), cols=c ^ 1)

    for k in lsm:
        k.wait()
    sr = jnp.broadcast_to(segr[...].astype(F32), (L, L))
    sc = sr.T
    qi = lax.broadcasted_iota(jnp.int32, (L, L), 0)
    ki = lax.broadcasted_iota(jnp.int32, (L, L), 1)
    ok = (sr == sc) & (qi >= ki)
    okf = jnp.where(ok, 1.0, 0.0)
    mskb[...] = jnp.where(ok, 0.0, NEG)
    pos = jnp.sum(okf, 1, keepdims=True) - 1.0
    angle = pos * freq[...]
    lane = lax.broadcasted_iota(jnp.int32, (L, HD), 1)
    cosb[...] = jnp.cos(angle)
    sn = jnp.sin(angle)
    sinb[...] = jnp.where(lane < HD // 2, -sn, sn)

    def to_ws(src, dst, t=slice(None)):
        cps = [net(src.at[t, :, at((r ^ k) * DR, DR)], dst.at[r, t, my_th, :], rows=r ^ k) for k in range(1, R)]
        return cps, local(src.at[t, :, at(r * DR, DR)], dst.at[r, t, my_th, :])

    def landed(cl):
        for k in cl[0]:
            k.wait_recv()
        cl[1].wait()

    def wsblk(buf, t=slice(None)):
        return lambda j: buf.at[:, t, at(j * TH, TH), :]

    lg.wait()
    for k in ga:
        k.wait_recv()
    a_g = to_ws(gtl, gw)
    ck = w_in(wk, wkf)
    cq.forward()
    landed(a_g)
    g_z, g_p = cols_start(wsblk(gw))
    cv = w_in(wv, wvf)
    lx.wait()
    xf = cols_forward(xblk, xz)
    ck.forward()
    cols_finish(xp, xf)

    def stats(v):
        mean = jnp.sum(v, 1, keepdims=True) / D
        sq = jnp.sum(v * v, 1, keepdims=True) / D
        return mean, lax.rsqrt(sq - mean * mean + EPS)

    for t in range(NT):
        def norm_rows(i, _, t=t):
            rows = at(i * 32, 32)
            v = xb[t, rows, :].astype(F32)
            mean, rstd = stats(v)
            h1[t, rows, :] = ((v - mean) * rstd).astype(BF)
            return 0

        lax.fori_loop(0, LH // 32, norm_rows, 0)

    cv.forward()
    co = Gather(net, R, r, lambda h: wo.at[half(HC, h), :], lambda j, h: wof.at[half(HC, h), at(j * DR, DR)])

    heads = HC // HD

    def rope(v):
        return jnp.concatenate(
            [v[:, h * HD:(h + 1) * HD] * cosb[...]
             + pltpu.roll(v[:, h * HD:(h + 1) * HD], HD // 2, 1) * sinb[...] for h in range(heads)], 1)

    def unrope(v):
        return v * cosb[...] + pltpu.roll(v * sinb[...], HD // 2, 1)

    def arrived(g):
        for k in range(1, R):
            g.wait(k)

    lws[0].wait()
    arrived(cq)
    qb[...] = rope(nn(h1[...].reshape(L, D), wqf[...])).astype(BF)
    lws[1].wait()
    arrived(ck)
    kb[...] = rope(nn(h1[...].reshape(L, D), wkf[...])).astype(BF)
    lws[2].wait()
    arrived(cv)
    vb[...] = nn(h1[...].reshape(L, D), wvf[...]).astype(BF)
    g_f = cols_forward(wsblk(gw), g_z)

    for h in range(heads):
        hs = slice(h * HD, (h + 1) * HD)
        s = nt(qb[:, hs], kb[:, hs]) * scale
        s = jnp.where(mskb[...] < 0.0, NEG, s)
        top = jnp.max(s, 1, keepdims=True)
        e = jnp.exp(s - top)
        tot = jnp.sum(e, 1, keepdims=True)
        lse[:, hs] = jnp.broadcast_to(top + jnp.log(tot), (L, HD))
        att[:, hs] = nn((e / tot).astype(BF), vb[:, hs]).astype(BF)

    def pre(p, pa):
        return net(p.at[1 - core], pa, cols=c ^ 1)

    def zsend(p, pa, ps, pr):
        out = []
        for m in range(1, Z):
            ps[m] = (p[core, z ^ m].astype(F32) + pa[z ^ m].astype(F32)).astype(BF)
            out.append(net(ps.at[m], pr.at[m], cols=c ^ (2 * m)))
        return out

    class Line:
        def __init__(self, p, pa, ps, pr):
            self.ps, self.pr = ps, pr
            for m in (3, 1, 2):
                ps[m] = (p[core, z ^ m].astype(F32) + pa[z ^ m].astype(F32)).astype(BF)
                if m == 3:
                    self.i, self.j = net.slot(), net.slot()
                    far = net.make(ps.at[3], pr.at[3 * mid], self.i, self.j + mid * (self.i - self.j),
                                   {"cols": c ^ (2 + 4 * mid)})
                    far.start()
                    net.all[self.i] = Copy(far)
                if m == 1:
                    self.c1 = net(ps.at[1], pr.at[1], cols=c ^ 2)

            @pl.when(mid == 0)
            def _():
                pr[3] = jnp.zeros(pr.shape[1:], BF)

        def relay(self):
            ps, pr = self.ps, self.pr

            @pl.when(mid == 1)
            def _():
                net.make(ps.at[3], pr.at[0], self.i, self.j, {"cols": c ^ 2}).wait_recv()
                ps[2] = (ps[2].astype(F32) + pr[0].astype(F32)).astype(BF)

            self.c2 = net(ps.at[2], pr.at[2], cols=c ^ 4)

        def total(self, p, pa):
            ps, pr = self.ps, self.pr
            self.c1.wait_recv()
            self.c2.wait_recv()

            @pl.when(mid == 1)
            def _():
                net.make(ps.at[3], pr.at[3], self.i, self.i, {"cols": c ^ 6}).wait_recv()

            return (p[core, z].astype(F32) + pa[z].astype(F32) + pr[1].astype(F32) + pr[2].astype(F32)
                    + pr[3].astype(F32))

    def line_send(p, pa, ps, pr):
        return Line(p, pa, ps, pr) if line else zsend(p, pa, ps, pr)

    def zsum(p, pa, pr, cps):
        if isinstance(cps, Line):
            return cps.total(p, pa)
        tot = p[core, z].astype(F32) + pa[z].astype(F32)
        for m in range(1, Z):
            for cp in cps[m - 1] if isinstance(cps[m - 1], list) else [cps[m - 1]]:
                cp.wait_recv()
            tot = tot + pr[m].astype(F32)
        return tot

    def x1_slice(k):
        ns = at((r ^ k) * DR, DR)
        val = nn(att[...], wof[:, ns])
        for j in range(C):
            for t in range(NT):
                p1[t, j % 2, j // 2, :, ns] = piece(val, j, t).astype(BF)
        return net(p1.at[:, 1 - core, :, :, ns], p1a.at[:, :, :, ns], cols=c ^ 1)

    z1 = [[[] for _ in range(1, Z)] for _ in range(NT)]

    def z1_send(k, pre_sum, last=False):
        ns = at((r ^ k) * DR, DR)
        pre_sum.wait_recv()
        for t in range(NT):
            for m in range(1, Z):
                p1s[t, m, :, ns] = (p1[t, core, z ^ m, :, ns].astype(F32) + p1a[t, z ^ m, :, ns].astype(F32)).astype(BF)
                if last:
                    z1[t][m - 1].append(net(p1s.at[t, m, :, ns], p1r.at[t, m, :, ns], cols=c ^ (2 * m)))
        if not last:
            for m in range(1, Z):
                cp = net(p1s.at[:, m, :, ns], p1r.at[:, m, :, ns], cols=c ^ (2 * m))
                for t in range(NT):
                    z1[t][m - 1].append(cp)

    order = list(range(1, R))
    FC = wgv.shape[1]
    DN = 2
    DW = FC // DN

    def dhid_chunk(n):
        for k in order:
            dhs[k, :, n * DW:(n + 1) * DW] = nt(gw[r ^ k].reshape(L, DR), wdv[n * DW:(n + 1) * DW, :]).astype(BF)

    def dhid_send(n):
        ns = slice(n * DW, (n + 1) * DW)
        return Reduce(net, R, r, lambda k, h: dhs.at[k, half(L, h), ns], lambda k, h: dhr.at[k, half(L, h), ns])

    lws[3].wait()
    k1 = [x1_slice(0)]
    co.forward()
    cols_finish(g_p, g_f)
    lout = []
    z1_send(0, k1[0])
    lff[0].wait()
    dhid_chunk(0)
    dh = [dhid_send(0)]
    for k in order[:-1]:
        co.wait(k)
        k1.append(x1_slice(k))
    for k in order[:-1]:
        z1_send(k, k1[k])
    co.wait(R - 1)
    k1.append(x1_slice(R - 1))
    z1_send(R - 1, k1[R - 1], True)
    for n in range(1, DN):
        dhid_chunk(n)

    xv = xb[:, my_th, :].reshape(TL, D).astype(F32)
    xm, xr_ = stats(xv)
    xtl[...] = (xv - xm) * xr_

    def second_norm(t):
        rows = slice(t * TH, (t + 1) * TH)
        v = xb[t, my_th, :].astype(F32) + zsum(p1.at[t], p1a.at[t], p1r.at[t], z1[t])
        x1[rows, :] = v
        mean2, rstd2 = stats(v)
        n2v = (v - mean2) * rstd2
        n2[rows, :] = n2v
        h2t[t] = n2v.astype(BF)
        return to_ws(h2t, h2w, t)

    lff[1].wait()
    lff[2].wait()

    QN = g["QN"]
    QW = FC // QN
    gu = []
    parts = [(t, q) for t in range(NT) for q in range(QN)]

    def gu_chunk(t, q):
        qs = slice(q * QW, (q + 1) * QW)
        for k in order[::-1] + [0]:
            ga_ = nn(h2w[r ^ k, t], wgv[:, qs])
            up_ = nn(h2w[r ^ k, t], wuv[:, qs])
            if k:
                gus[k, t, q, 0] = ga_.astype(BF)
                gus[k, t, q, 1] = up_.astype(BF)
            else:
                guo[t, q, 0] = ga_
                guo[t, q, 1] = up_
        gu.append(Reduce(net, R, r, lambda k, h: gus.at[k, t, q, :, half(LH, h), :],
                         lambda k, h: gur.at[k, t, q, :, half(LH, h), :]))

    def ahead():
        cols_finish(h2_c[0][1], (line_forward if line else cols_forward)(wsblk(h2w, 0), h2_c[0][0]))
        gu_chunk(*parts[0])

    h2_c = []
    for t in range(NT):
        a_2 = second_norm(t)
        if t == 0:
            dh[0].relay()
            for n in range(1, DN):
                dh.append(dhid_send(n))
            for n in range(DN):
                dho[:, n * DW:(n + 1) * DW] = nt(gw[r].reshape(L, DR), wdv[n * DW:(n + 1) * DW, :])
        if t:
            ahead()
        landed(a_2)
        h2_c.append((line_start if line else cols_start)(wsblk(h2w, t)))
        if line:
            line_relay(wsblk(h2w, t), h2_c[t][0])
    for d in dh[1:]:
        d.relay()
    a_h = to_ws(h1.at[:, my_th, :], h1w)
    for t, q in parts[len(gu):]:
        if q == 0:
            cols_finish(h2_c[t][1], (line_forward if line else cols_forward)(wsblk(h2w, t), h2_c[t][0]))
        gu_chunk(t, q)
        if len(gu) > 1:
            gu[-2].relay()
    gu[-1].relay()
    landed(a_h)
    h_z, h_p = cols_start(wsblk(h1w))

    for d in dh:
        d.wait()
    dgt = []
    AR = 16
    for n, (t, q) in enumerate(parts):
        gu[n].wait()
        qs = slice(q * QW, (q + 1) * QW)

        def act(i, _, n=n, t=t, q=q, qs=qs):
            part = at(i * AR, AR)
            rows = at(t * LH + i * AR, AR)
            gate, up = guo[t, q, 0, part, :], guo[t, q, 1, part, :]
            dhid = dho[rows, qs]
            for k in gu[n].ks:
                gate = gate + gur[k, t, q, 0, part, :].astype(F32)
                up = up + gur[k, t, q, 1, part, :].astype(F32)
                dhid = dhid + dhr[k, rows, qs].astype(F32)
            sig = 1.0 / (1.0 + jnp.exp(-gate))
            silu = gate * sig
            hda[r, rows, qs] = (silu * up).astype(BF)
            dgu[0, r, rows, qs] = (dhid * up * sig * (1.0 + gate * (1.0 - sig))).astype(BF)
            dgu[1, r, rows, qs] = (dhid * silu).astype(BF)
            return 0
        lax.fori_loop(0, LH // AR, act, 0)

        def tok_half(h, t=t):
            return slice(t * LH + h * (LH // 2), t * LH + (h + 1) * (LH // 2))
        dgt.append(Gather(net, R, r, lambda h, qs=qs, f=tok_half: dgu.at[:, r, f(h), qs],
                          lambda j, h, qs=qs, f=tok_half: dgu.at[:, j, f(h), qs]))

    k2 = {}

    def dh2_block(k):
        s = r ^ k
        tot = nt(dgu[0, s], wgv[...]) + nt(dgu[1, s], wuv[...])
        for j in range(C):
            for t in range(NT):
                p2[j % 2, k, j // 2, t * TH:(t + 1) * TH] = piece(tot, j, t).astype(BF)
        k2[k] = net(p2.at[1 - core, k], p2a.at[k], cols=c ^ 1)

    dh2_block(0)
    z2 = {}
    for d in dgt:
        d.forward()

    def hid_send(n):
        ns = slice(n * DW, (n + 1) * DW)
        return Gather(net, R, r, lambda h: hda.at[r, half(L, h), ns], lambda j, h: hda.at[j, half(L, h), ns])

    hdc = [hid_send(0)]

    def z2_send(k):
        k2[k].wait_recv()
        for m in range(1, Z):
            p2s[k, m] = (p2[core, k, z ^ m].astype(F32) + p2a[k, z ^ m].astype(F32)).astype(BF)
            z2[k, m] = net(p2s.at[k, m], p2r.at[k, m], cols=c ^ (2 * m))

    for n, k in enumerate(order):
        for d in dgt:
            d.wait(k)
        dh2_block(k)
        z2_send(n)
    z2_send(R - 1)
    T = R * L

    def wgrad(dst, lhs, rhs):
        w = 128
        for i in range(dst.shape[0] // w):
            dst[i * w:(i + 1) * w, :] = tn(lhs(slice(i * w, (i + 1) * w)), rhs).astype(BF)

    wgrad(wgg, lambda ns: h2w[:, :, :, ns].reshape(T, 128), dgu[0].reshape(T, FC))
    lout.append(local(wgg, gg_out))
    hdc[0].forward()

    a_d = []
    for k in range(R):
        tot = p2[core, k, z].astype(F32) + p2a[k, z].astype(F32)
        for m in range(1, Z):
            z2[k, m].wait_recv()
            tot = tot + p2r[k, m].astype(F32)
        dh2s[k] = tot.astype(BF)
        if k:
            a_d.append(net(dh2s.at[k], dh2t.at[:, at(r * DR, DR)], rows=r ^ k))
        else:
            l_d = local(dh2s.at[0], dh2t.at[:, at(r * DR, DR)])
    hdc += [hid_send(n) for n in range(1, DN)]
    l_d.wait()
    for k in a_d:
        k.wait_recv()

    def norm_back(grad, normed, rstd):
        a = jnp.sum(grad, 1, keepdims=True) / D
        b = jnp.sum(grad * normed, 1, keepdims=True) / D
        return rstd * (grad - a - normed * b)

    _, rstd2b = stats(x1[...])
    dxv = gtl[...].reshape(TL, D).astype(F32) + norm_back(dh2t[...].astype(F32), n2[...], rstd2b)
    dxt[...] = dxv
    dmt[...] = dxv.astype(BF).reshape(NT, TH, D)
    l_m = local(dmt, dmix.at[:, my_th, :])

    def dblk(j):
        return dmix.at[:, at(j * TH, TH), :]
    l_m.wait()
    m_z, m_p = line_start(dblk) if line else cols_start(dblk)

    def ffn_block(k):
        s = r ^ k
        tot = nn(hda[s], wdv[...])
        for j in range(C):
            for t in range(NT):
                p3[j % 2, j // 2, k, t * TH:(t + 1) * TH] = piece(tot, j, t).astype(BF)

    ffn_block(0)
    h_f = cols_forward(wsblk(h1w), h_z)
    wgrad(wgu, lambda ns: h2w[:, :, :, ns].reshape(T, 128), dgu[1].reshape(T, FC))
    lout.append(local(wgu, gu_out))
    for d in hdc[1:]:
        d.forward()
    if line:
        line_relay(dblk, m_z)
    for k in order:
        for d in hdc:
            d.wait(k)
        ffn_block(k)
    k3 = pre(p3, p3a)
    cols_finish(h_p, h_f)
    k3.wait_recv()
    m_f = line_forward(dblk, m_z) if line else cols_forward(dblk, m_z)
    z3 = line_send(p3, p3a, p3s, p3r)
    cols_finish(m_p, m_f)

    for k in order:
        gop[k] = tn(att[...], dmix[:, :, at((r ^ k) * DR, DR)].reshape(L, DR)).astype(BF)
    cgo = Reduce(net, R, r, lambda k, h: gop.at[k, half(HC, h), :], lambda k, h: gor.at[k, half(HC, h), :])
    da = nt(dmix[...].reshape(L, D), wof[...]).astype(BF)
    for h in range(heads):
        hs = slice(h * HD, (h + 1) * HD)
        s = nt(qb[:, hs], kb[:, hs]) * scale
        s = jnp.where(mskb[...] < 0.0, NEG, s)
        pr = jnp.exp(s - lse[:, h * HD:h * HD + 1])
        dp = nt(da[:, hs], vb[:, hs])
        inner = jnp.sum(pr * dp, 1, keepdims=True)
        ds = (pr * (dp - inner)).astype(BF)
        dqkv[0, r, :, hs] = unrope(nn(ds, kb[:, hs]) * scale).astype(BF)
        dqkv[1, r, :, hs] = unrope(tn(ds, qb[:, hs]) * scale).astype(BF)
        dqkv[2, r, :, hs] = tn(pr.astype(BF), da[:, hs]).astype(BF)
    cd = Gather(net, R, r, lambda h: dqkv.at[:, r, half(L, h), :], lambda j, h: dqkv.at[:, j, half(L, h), :])

    W1 = min(512, D)
    for n in range(D // W1):
        ns = slice(n * W1, (n + 1) * W1)
        val = (nt(dqkv[0, r], wqf[ns, :]) + nt(dqkv[1, r], wkf[ns, :]) + nt(dqkv[2, r], wvf[ns, :]))
        for j in range(C):
            for t in range(NT):
                p4[t, j % 2, j // 2, :, ns] = piece(val, j, t).astype(BF)
    k4 = [pre(p4.at[t], p4a.at[t]) for t in range(NT)]
    if line:
        z3.relay()
    z4 = []
    for t in range(NT):
        k4[t].wait_recv()
        z4.append(line_send(p4.at[t], p4a.at[t], p4s.at[t], p4r.at[t]))
    cgo.relay()
    if line:
        for k in z4:
            k.relay()
    gof[...] = tn(att[...], dmix[:, :, at(r * DR, DR)].reshape(L, DR))

    fs[...] = zsum(p3, p3a, p3r, z3).astype(BF)
    a_f = [net(fs.at[k], ft.at[:, at(r * DR, DR)], rows=r ^ k) for k in order]
    l_f = local(fs.at[0], ft.at[:, at(r * DR, DR)])
    cd.forward()

    def to_io(src, dst, t=slice(None)):
        cps = [net(src.at[t, :, at((c ^ k) * DC, DC)], dst.at[t, my_th, :], cols=c ^ k) for k in range(1, C)]
        return cps, local(src.at[t, :, at(c * DC, DC)], dst.at[t, my_th, :])

    def qkv_grad(k):
        for i in range(3):
            t = tn(h1w[r ^ k].reshape(L, DR), dqkv[i, r ^ k])
            wqa[i] = t if k == 0 else wqa[i] + t

    qkv_grad(0)
    wgrad(wgd, lambda ns: hda[:, :, ns].reshape(T, 128), gw[...].reshape(T, DR))
    lout.append(local(wgd, gd_out))
    l_f.wait()
    for k in a_f:
        k.wait_recv()
    lot[...] = (x1[...] + ft[...].astype(F32)).astype(BF).reshape(NT, TH, D)
    i_o = to_io(lot, lob)
    for k in order[:-1]:
        cd.wait(k)
        qkv_grad(k)
    i_g = []
    for t in range(NT):
        rows = slice(t * TH, (t + 1) * TH)
        _, rstd1 = stats(xb[t, my_th, :].astype(F32))
        dh1 = zsum(p4.at[t], p4a.at[t], p4r.at[t], z4[t])
        git[t] = (dxt[rows, :] + norm_back(dh1, xtl[rows, :], rstd1)).astype(BF)
        i_g.append(to_io(git, gib, t))
    cd.wait(R - 1)
    qkv_grad(R - 1)
    lout += [local(wqa.at[0], gq_out), local(wqa.at[1], gk_out), local(wqa.at[2], gv_out)]
    landed(i_o)
    lout.append(local(lob, o_out))
    for k in i_g:
        landed(k)
    lout.append(local(gib, gi_out))
    cgo.wait()
    gsum = gof[...]
    for k in cgo.ks:
        gsum = gsum + gor[k].astype(F32)
    gof[...] = gsum
    lout.append(local(gof, go_out))
    net.drain()
    for k in lout:
        k.wait()


def body(R, C, tokens, segments, w_query, w_key, w_value, w_out, w_gate, w_up, w_down, cotangent):
    L, DC = tokens.shape
    DR, HC = w_query.shape
    D = DR * R
    FC = w_gate.shape[1]
    TL = L // C
    Z = C // 2
    NT = 2 if TL % 32 == 0 else 1
    LH, TH = L // NT, TL // NT
    QN = 4 // NT if FC % 1024 == 0 else 2
    QW = FC // QN
    g = dict(R=R, C=C, L=L, TL=TL, D=D, DR=DR, DC=DC, HC=HC, NT=NT, QN=QN)
    half = HD // 2
    fr = (BASE ** (-(np.arange(half, dtype=np.float32) * np.float32(2.0)) / np.float32(HD))).astype(np.float32)
    freq = jnp.asarray(np.concatenate([fr, fr])[None, :])
    S = jax.ShapeDtypeStruct
    V = pltpu.VMEM
    outs = [
        S((NT, LH, DC), BF), S((NT, LH, DC), BF), S((DR, FC), BF), S((DR, FC), BF), S((FC, DR), BF),
        *[S((DR, HC), F32)] * 3, S((HC, DR), F32),
    ]
    seq = lambda w: [V((NT, 2, Z, TH, w), BF)] + [V((NT, Z, TH, w), BF)] * 3
    seq4 = lambda: [V((2, Z, R, TL, DR), BF), V((Z, R, TL, DR), BF), V((Z, R, TL, DR), BF), V((Z, R, TL, DR), BF)]
    seq2 = lambda: [V((2, R, Z, TL, DR), BF), V((R, Z, TL, DR), BF), V((R, Z, TL, DR), BF), V((R, Z, TL, DR), BF)]
    scratch = [
        V((NT, LH, D), BF), V((NT, LH, D), BF), V((TL, D), F32), V((NT, TH, D), BF),
        *[V((R, NT, LH, DR), BF)] * 3, V((NT, TH, D), BF),
        V((D, HC), BF), V((D, HC), BF), V((D, HC), BF), V((HC, D), BF),
        V((DR, FC), BF), V((DR, FC), BF), V((FC, DR), BF),
        *seq(D), *seq2(), *seq4(), *seq(D),
        V((TL, D), F32), V((TL, D), F32),
        V((R, L, FC), BF), V((R, L, FC), BF), V((L, FC), F32),
        V((R, NT, QN, 2, LH, QW), BF), V((R, NT, QN, 2, LH, QW), BF), V((NT, QN, 2, LH, QW), F32),
        V((R, L, FC), BF), V((2, R, L, FC), BF),
        V((R, TL, DR), BF), V((TL, D), BF), V((TL, D), F32), V((NT, TH, D), BF), V((NT, LH, D), BF),
        V((L, HC), BF), V((L, HC), BF), V((L, HC), BF), V((L, HC), BF), V((L, HC), F32),
        V((L, HD), F32), V((L, HD), F32), V((L, L), F32),
        V((3, R, L, HC), BF), V((R, HC, DR), BF), V((R, HC, DR), BF), V((HC, DR), F32),
        V((R, TL, DR), BF), V((TL, D), BF), V((NT, TH, D), BF), V((NT, TH, D), BF),
        V((NT, LH, DC), BF), V((NT, LH, DC), BF),
        V((DR, FC), BF), V((DR, FC), BF), V((FC, DR), BF), V((3, DR, HC), F32),
        V((1, L), jnp.int32), V((1, HD), F32),
        pltpu.SemaphoreType.DMA((g_sems(R, C, NT * QN),)), pltpu.SemaphoreType.DMA((g_sems(R, C, NT * QN),)),
        pltpu.SemaphoreType.DMA((48,)),
    ]
    A = pl.BlockSpec(memory_space=pl.ANY)
    res = pl.pallas_call(
        functools.partial(step_kernel, g),
        out_shape=outs,
        in_specs=[A] * 11,
        out_specs=[A] * len(outs),
        scratch_shapes=scratch,
        compiler_params=pltpu.CompilerParams(
            collective_id=0, has_side_effects=True, vmem_limit_bytes=67043328),
        name="layer_step",
    )(tokens.reshape(NT, LH, DC), cotangent.reshape(NT, LH, DC), segments, freq, w_query, w_key, w_value, w_out, w_gate, w_up, w_down)
    layer_out, grad_in, ggate, gup, gdown, gq, gk, gv, go = res
    return finish(layer_out.reshape(L, DC), grad_in.reshape(L, DC), gq, gk, gv, go, ggate, gup, gdown)


def finish(layer_out, *grads):
    ins = (layer_out,) + grads
    n = len(ins)
    types = [BF] + [F32] * len(grads)
    wide = [i for i in range(n) if ins[i].dtype != types[i]]

    def kern(*refs):
        src, dst, buf = refs[:n], refs[n:2 * n], refs[2 * n:3 * n]
        out = dict(zip(wide, refs[3 * n:3 * n + len(wide)]))
        si, so = refs[-2:]
        got = [pltpu.make_async_copy(src[i], buf[i], si.at[i]) for i in range(n)]
        put = [pltpu.make_async_copy(out.get(i, buf[i]), dst[i], so.at[i]) for i in range(n)]
        for i in reversed(range(n)):
            got[i].start()
        for i in reversed(range(n)):
            got[i].wait()
            if i in out:
                out[i][...] = buf[i][...].astype(F32)
            put[i].start()
        for i in range(n):
            put[i].wait()

    A = pl.BlockSpec(memory_space=pl.ANY)
    V = pltpu.VMEM
    return pl.pallas_call(
        kern,
        out_shape=[jax.ShapeDtypeStruct(a.shape, t) for a, t in zip(ins, types)],
        in_specs=[A] * n, out_specs=[A] * n,
        scratch_shapes=[V(a.shape, a.dtype) for a in ins] + [V(ins[i].shape, F32) for i in wide]
        + [pltpu.SemaphoreType.DMA((n,)), pltpu.SemaphoreType.DMA((n,))],
        compiler_params=pltpu.CompilerParams(vmem_limit_bytes=67043328),
        name="finish",
    )(*ins)

def g_sems(R, C, n):
    return 2 * (R - 1) * (8 + n) + 2 * R * (3 + n) + 8 * (R - 1) + 17 * C + (2 * R + 6) * C // 2


def solution(mesh):
    R, C = mesh.shape["rows"], mesh.shape["cols"]
    rc, cr = P("rows", "cols"), P("cols", "rows")
    in_specs = (rc, P("rows", None), rc, rc, rc, cr, rc, rc, cr, rc)
    out_specs = (rc, rc, rc, rc, rc, cr, rc, rc, cr)
    return jax.shard_map(functools.partial(body, R, C), mesh=mesh, in_specs=in_specs,
                         out_specs=out_specs, check_vma=False)
```
